32 devices in a mesh: dp: 4 (over x, core), fsdp: 8 (over z, y).
Axes of the slice: x: 2, y: 2, z: 4, core: 2. Of those that a mesh axis runs over, the one named last changes fastest.
Arguments:
- block_in: bfloat16 [32, 1024, 1024], P(('dp', 'fsdp')), may hold values from -6 to 6
- images: bfloat16 [128, 588, 1024], P(('dp', 'fsdp')), may hold values from -6 to 6
- segment_ids: int32 [32, 1024], P(('dp', 'fsdp')), may hold values from 0 to 3, never falling along the last dimension, each value on 1 to 512 neighbouring positions
- page_map: int32 [32, 4], P(('dp', 'fsdp')), may hold values from 0 to 3, each once within a row
- ln1_gain: float32 [1024], P(('dp', 'fsdp')), may hold values from 0.25 to 1.75
- ln1_shift: float32 [1024], P(('dp', 'fsdp')), may hold values from -1.5 to 1.5
- ln2_gain: float32 [1024], P(('dp', 'fsdp')), may hold values from 0.25 to 1.75
- ln2_shift: float32 [1024], P(('dp', 'fsdp')), may hold values from -1.5 to 1.5
- ln3_gain: float32 [1024], P(('dp', 'fsdp')), may hold values from 0.25 to 1.75
- ln3_shift: float32 [1024], P(('dp', 'fsdp')), may hold values from -1.5 to 1.5
- self_query: float32 [1024, 1024], P(None, ('dp', 'fsdp')), may hold values from -0.1875 to 0.1875
- self_key: float32 [1024, 1024], P(None, ('dp', 'fsdp')), may hold values from -0.1875 to 0.1875
- self_value: float32 [1024, 1024], P(None, ('dp', 'fsdp')), may hold values from -0.1875 to 0.1875
- self_out: float32 [1024, 1024], P(None, ('dp', 'fsdp')), may hold values from -0.5 to 0.5
- cross_query: float32 [1024, 1024], P(None, ('dp', 'fsdp')), may hold values from -0.1875 to 0.1875
- cross_key: float32 [1024, 1024], P(None, ('dp', 'fsdp')), may hold values from -0.1875 to 0.1875
- cross_value: float32 [1024, 1024], P(None, ('dp', 'fsdp')), may hold values from -0.1875 to 0.1875
- cross_out: float32 [1024, 1024], P(None, ('dp', 'fsdp')), may hold values from -0.75 to 0.75
- mlp_in: float32 [1024, 4096], P(None, ('dp', 'fsdp')), may hold values from -0.1875 to 0.1875
- mlp_out: float32 [4096, 1024], P(None, ('dp', 'fsdp')), may hold values from -0.125 to 0.125
- cotangent: bfloat16 [32, 1024, 1024], P(('dp', 'fsdp')), may hold values from -6 to 6
Outputs:
- block_out: bfloat16 [32, 1024, 1024], P(('dp', 'fsdp'))
- grad_in: float32 [32, 1024, 1024], P(('dp', 'fsdp'))
- grad_images: float32 [128, 588, 1024], P(('dp', 'fsdp'))
- grad_ln1_gain: float32 [1024], P(('dp', 'fsdp'))
- grad_ln1_shift: float32 [1024], P(('dp', 'fsdp'))
- grad_ln2_gain: float32 [1024], P(('dp', 'fsdp'))
- grad_ln2_shift: float32 [1024], P(('dp', 'fsdp'))
- grad_ln3_gain: float32 [1024], P(('dp', 'fsdp'))
- grad_ln3_shift: float32 [1024], P(('dp', 'fsdp'))
- grad_self_query: float32 [1024, 1024], P(None, ('dp', 'fsdp'))
- grad_self_key: float32 [1024, 1024], P(None, ('dp', 'fsdp'))
- grad_self_value: float32 [1024, 1024], P(None, ('dp', 'fsdp'))
- grad_self_out: float32 [1024, 1024], P(None, ('dp', 'fsdp'))
- grad_cross_query: float32 [1024, 1024], P(None, ('dp', 'fsdp'))
- grad_cross_key: float32 [1024, 1024], P(None, ('dp', 'fsdp'))
- grad_cross_value: float32 [1024, 1024], P(None, ('dp', 'fsdp'))
- grad_cross_out: float32 [1024, 1024], P(None, ('dp', 'fsdp'))
- grad_mlp_in: float32 [1024, 4096], P(None, ('dp', 'fsdp'))
- grad_mlp_out: float32 [4096, 1024], P(None, ('dp', 'fsdp'))
The draws below stay inside these ranges and needn't reach their ends.
Inputs may be any that keep to these rules, and one draw needn't show every extreme that they name: `segment_ids`: within each row segment ids never fall; each of the 4 segments holds 1 to 512 positions, and some segment of each row holds exactly 512. Each row lists every number 0 to 3 once; segment t of decoder row r reads image r * 4 + page_map[r, t].
All inputs are finite; a program needn't handle non-finite values.
Results may differ from the reference program's by a relative error of at most 0.02.
The reference program's roundings to bfloat16 on the way count: a program that leaves them out, or rounds other values in their place, can miss the bound.
Values may be sent and summed in bfloat16 or wider, within the bound.
A program may use at most 768 MiB of HBM per device.

```python
import math
import jax
import jax.numpy as jnp
import numpy as np
from jax import lax

D = 1024
HEADS = 16
FF = 4096
HEAD_DIM = 64
IMG_TOK = 588
PAGES = 4
ROW_LEN = 1024
ROWS = 32
IMAGES = 128


def spiked(values, stream_key, source, target, parts, factor):
    def block_of(dim):
        return (jnp.arange(values.shape[dim]) // (values.shape[dim] // parts)).reshape((-1,) + (1,) * (values.ndim - 1 - dim))

    first = jax.random.permutation(stream_key, parts)[block_of(target)]
    second = (block_of(target) + parts // 2) % parts
    return jnp.where((block_of(source) == first) | (block_of(source) == second), factor * values, values)


def steps_of(key, dims, cuts, smallest, high):
    def one(position, blocks):
        heights = jax.random.uniform(jax.random.fold_in(jax.random.fold_in(key, 6), position), (blocks,), jnp.float32, smallest / len(cuts), high / len(cuts))
        return jnp.repeat(jnp.exp(heights), dims[position] // blocks).reshape((-1,) + (1,) * (len(dims) - position - 1))

    factor_of = one(*cuts[0])
    for cut in cuts[1:]:
        factor_of = factor_of * one(*cut)
    return factor_of


def profile(count, total, bound, skew):
    portions = [(1 << 20) // math.isqrt(standing ** skew) + 1 for standing in range(2, count + 1)]
    surplus, counts = total - bound - (count - 1), [1] * (count - 1)
    while surplus > 0:
        free = [i for i in range(count - 1) if counts[i] < bound]
        pool, budget = sum([portions[i] for i in free]), surplus
        for i in free:
            addition = min(bound - counts[i], max(1, budget * portions[i] // pool), surplus)
            counts[i] = counts[i] + addition
            surplus = surplus - addition
    return np.array([bound] + counts)


def uneven_parts(own_key, amount, total, most, skew):
    if amount == 2:
        one = jax.random.randint(own_key, (), max(1, total - most), min(most, total - 1) + 1)
        return jnp.stack([one, total - one])
    lengths = jnp.asarray(profile(amount, total, most, skew), jnp.int32)
    twos = (amount - 1) // 2
    giver, taker = lengths[1:1 + 2 * twos:2], lengths[2:2 + 2 * twos:2]
    room = jnp.minimum(giver - 1, most - taker)
    shifted = jax.random.randint(jax.random.fold_in(own_key, 1), (twos,), 0, 1 << 20) % (room + 1)
    lengths = lengths.at[1:1 + 2 * twos:2].set(giver - shifted).at[2:2 + 2 * twos:2].set(taker + shifted)
    return lengths[jax.random.permutation(jax.random.fold_in(own_key, 2), amount)]


def scatter_about(rng, shape, width, bound, split=(), held_as=jnp.bfloat16):
    drawn = width * jax.random.normal(rng, shape, jnp.float32)
    if split:
        drawn = drawn * steps_of(rng, shape, split, -0.22, 0.18)
    return jnp.clip(drawn, -bound, bound).astype(held_as)


def gaussian_with(own_key, shape, deviation, limit, shards, heavy, held_as=jnp.bfloat16):
    values = deviation * jax.random.normal(own_key, shape, jnp.float32)
    if shards:
        values = values * steps_of(own_key, shape, shards, -0.22, 0.18)
    return jnp.clip(spiked(values, jax.random.fold_in(own_key, 3), *heavy), -limit, limit).astype(held_as)


def setup_inputs(seed: int = 0) -> dict:
    arg_keys = jax.random.split(jax.random.key(seed), 22)
    block_in = scatter_about(arg_keys[0], (ROWS, ROW_LEN, D), 1.0, 6.0, ((0, 32),))
    images = scatter_about(arg_keys[1], (IMAGES, IMG_TOK, D), 1.0, 6.0, ((0, 32),))
    segment_ids = jax.vmap(lambda own: jnp.searchsorted(jnp.cumsum(uneven_parts(own, PAGES, ROW_LEN, ROW_LEN // 2, 1)), jnp.arange(ROW_LEN), side="right"))(jax.random.split(arg_keys[2], ROWS)).reshape((ROWS, ROW_LEN)).astype(jnp.int32)
    page_map = jax.vmap(lambda own: jax.random.permutation(own, PAGES))(jax.random.split(arg_keys[3], ROWS)).reshape((ROWS, PAGES)).astype(jnp.int32)
    ln1_gain = jnp.clip(1.0 + 0.15 * jax.random.normal(arg_keys[4], (D,), jnp.float32), 0.25, 1.75)
    ln1_shift = scatter_about(arg_keys[5], (D,), 0.3, 1.5, ((0, 32),), jnp.float32)
    ln2_gain = jnp.clip(1.0 + 0.15 * jax.random.normal(arg_keys[6], (D,), jnp.float32), 0.25, 1.75)
    ln2_shift = scatter_about(arg_keys[7], (D,), 0.3, 1.5, ((0, 32),), jnp.float32)
    ln3_gain = jnp.clip(1.0 + 0.15 * jax.random.normal(arg_keys[8], (D,), jnp.float32), 0.25, 1.75)
    ln3_shift = scatter_about(arg_keys[9], (D,), 0.3, 1.5, ((0, 32),), jnp.float32)
    self_query = scatter_about(arg_keys[10], (D, D), D ** -0.5, 0.1875, ((1, 32),), jnp.float32)
    self_key = scatter_about(arg_keys[11], (D, D), D ** -0.5, 0.1875, ((1, 32),), jnp.float32)
    self_value = scatter_about(arg_keys[12], (D, D), D ** -0.5, 0.1875, ((1, 32),), jnp.float32)
    self_out = scatter_about(arg_keys[13], (D, D), (D // 8) ** -0.5, 0.5, ((1, 32),), jnp.float32)
    cross_query = scatter_about(arg_keys[14], (D, D), D ** -0.5, 0.1875, ((1, 32),), jnp.float32)
    cross_key = scatter_about(arg_keys[15], (D, D), D ** -0.5, 0.1875, ((1, 32),), jnp.float32)
    cross_value = scatter_about(arg_keys[16], (D, D), D ** -0.5, 0.1875, ((1, 32),), jnp.float32)
    cross_out = scatter_about(arg_keys[17], (D, D), (D // 16) ** -0.5, 0.75, ((1, 32),), jnp.float32)
    mlp_in = scatter_about(arg_keys[18], (D, FF), D ** -0.5, 0.1875, ((1, 32),), jnp.float32)
    mlp_out = scatter_about(arg_keys[19], (FF, D), (FF // 2) ** -0.5, 0.125, ((1, 32),), jnp.float32)
    cotangent = gaussian_with(arg_keys[20], (ROWS, ROW_LEN, D), 1.0, 6.0, ((0, 32),), (0, 2, 32, 2.75))
    return dict(block_in=block_in, images=images, segment_ids=segment_ids, page_map=page_map, ln1_gain=ln1_gain, ln1_shift=ln1_shift, ln2_gain=ln2_gain, ln2_shift=ln2_shift, ln3_gain=ln3_gain, ln3_shift=ln3_shift, self_query=self_query, self_key=self_key, self_value=self_value, self_out=self_out, cross_query=cross_query, cross_key=cross_key, cross_value=cross_value, cross_out=cross_out, mlp_in=mlp_in, mlp_out=mlp_out, cotangent=cotangent)


@jax.custom_vjp
def low(v):
    return lax.optimization_barrier(v.astype(jnp.bfloat16)).astype(jnp.float32)

@jax.custom_vjp
def low_back(v):
    return v

def low_keep(v):
    return (low(v), None)

def low_pass(kept, grad):
    return (grad,)

def back_keep(v):
    return (v, None)

def back_low(kept, grad):
    return (low(grad),)
low.defvjp(low_keep, low_pass)
low_back.defvjp(back_keep, back_low)
EPSILON = 1e-05
NEGATIVE = -1e+30

def exact_dot(left_side, right_side):
    return jnp.dot(left_side, right_side, precision=lax.Precision.HIGHEST, preferred_element_type=jnp.float32)

def layer_norm(values, norm_gain, norm_shift):
    average = lax.optimization_barrier(jnp.mean(values, axis=-1, keepdims=True))
    centered = values - average
    variance = lax.optimization_barrier(jnp.mean(centered * centered, axis=-1, keepdims=True))
    return centered * lax.rsqrt(variance + EPSILON) * norm_gain + norm_shift

def attend(queries, keys_all, values_all, allowed):
    length = queries.shape[0]
    query_heads = queries.reshape(length, HEADS, HEAD_DIM)
    key_heads = keys_all.reshape(keys_all.shape[0], HEADS, HEAD_DIM)
    value_heads = values_all.reshape(values_all.shape[0], HEADS, HEAD_DIM)
    scores = jnp.einsum('qhd,khd->hqk', query_heads, key_heads, precision=lax.Precision.HIGHEST) * HEAD_DIM ** (-0.5)
    scores = low_back(jnp.where(allowed[None], scores, NEGATIVE))
    attention = jax.nn.softmax(scores, axis=-1)
    mixed_heads = jnp.einsum('hqk,khd->qhd', low(attention), value_heads, precision=lax.Precision.HIGHEST)
    return low_back(low(mixed_heads.reshape(length, D)))

def row_forward(row_in, row_images, row_segments, row_pages, params):
    gain_one, shift_one, gain_two, shift_two, gain_three, shift_three, self_q_weight, self_k_weight, self_v_weight, self_o_weight, cross_q_weight, cross_k_weight, cross_v_weight, cross_o_weight, input_weight, output_weight = params
    places = jnp.arange(ROW_LEN, dtype=jnp.int32)
    self_mask = (row_segments[:, None] == row_segments[None, :]) & (places[None, :] <= places[:, None])
    normed_one = low(layer_norm(row_in, gain_one, shift_one))
    self_queries = low_back(low(exact_dot(normed_one, self_q_weight)))
    self_keys = low_back(low(exact_dot(normed_one, self_k_weight)))
    self_values = low_back(low(exact_dot(normed_one, self_v_weight)))
    self_mixed = attend(self_queries, self_keys, self_values, self_mask)
    after_self = row_in + low_back(exact_dot(self_mixed, self_o_weight))
    normed_two = low(layer_norm(after_self, gain_two, shift_two))
    cross_queries = low_back(low(exact_dot(normed_two, cross_q_weight)))
    flat_images = row_images.reshape(PAGES * IMG_TOK, D)
    cross_keys = low_back(low(exact_dot(flat_images, cross_k_weight)))
    cross_values = low_back(low(exact_dot(flat_images, cross_v_weight)))
    page_index = jnp.arange(PAGES, dtype=jnp.int32)
    query_image = lax.optimization_barrier(jnp.sum(jnp.where(row_segments[:, None] == page_index[None, :], row_pages[None, :], 0), axis=1)).astype(jnp.int32)
    key_image = (jnp.arange(PAGES * IMG_TOK, dtype=jnp.int32) // IMG_TOK).astype(jnp.int32)
    cross_mask = query_image[:, None] == key_image[None, :]
    cross_mixed = attend(cross_queries, cross_keys, cross_values, cross_mask)
    after_cross = after_self + low_back(exact_dot(cross_mixed, cross_o_weight))
    normed_three = low(layer_norm(after_cross, gain_three, shift_three))
    pre_act = low_back(exact_dot(normed_three, input_weight))
    hidden = low(jax.nn.gelu(pre_act, approximate=False))
    return after_cross + low_back(exact_dot(hidden, output_weight))

def reference(block_in, images, segment_ids, page_map, ln1_gain, ln1_shift, ln2_gain, ln2_shift, ln3_gain, ln3_shift, self_query, self_key, self_value, self_out, cross_query, cross_key, cross_value, cross_out, mlp_in, mlp_out, cotangent):
    masters = (ln1_gain, ln1_shift, ln2_gain, ln2_shift, ln3_gain, ln3_shift, self_query, self_key, self_value, self_out, cross_query, cross_key, cross_value, cross_out, mlp_in, mlp_out)
    inputs = block_in.astype(jnp.float32)
    image_rows = images.astype(jnp.float32).reshape(block_in.shape[0], PAGES, IMG_TOK, D)

    def forward(inputs_now, images_now, masters_now):
        params = tuple((low(master) for master in masters_now))

        def one_row(packed):
            return row_forward(packed[0], packed[1], packed[2], packed[3], params)
        return lax.map(jax.checkpoint(one_row), (inputs_now, images_now, segment_ids, page_map))
    block_out, pullback = jax.vjp(forward, inputs, image_rows, masters)
    grad_in, grad_images, grad_masters = pullback(cotangent.astype(jnp.float32))
    return (block_out.astype(jnp.bfloat16), grad_in, grad_images.reshape(images.shape), grad_masters[0], grad_masters[1], grad_masters[2], grad_masters[3], grad_masters[4], grad_masters[5], grad_masters[6], grad_masters[7], grad_masters[8], grad_masters[9], grad_masters[10], grad_masters[11], grad_masters[12], grad_masters[13], grad_masters[14], grad_masters[15])
```

```python
import functools
import jax
import jax.numpy as jnp
from jax import lax
from jax.experimental import pallas as pl
from jax.experimental.pallas import tpu as pltpu
from jax.sharding import PartitionSpec as P

LANES = 128
HALF = 64
QB = 128


def dot_nt(a, b):
    return lax.dot_general(a, b, (((1,), (1,)), ((), ())), preferred_element_type=jnp.float32)


def dot_nn(a, b):
    return lax.dot_general(a, b, (((1,), (0,)), ((), ())), preferred_element_type=jnp.float32)


def head_stack(block, scale=None):
    lane = lax.broadcasted_iota(jnp.int32, block.shape, 1)
    wide = block.astype(jnp.float32)
    if scale is not None:
        wide = wide * scale
    first = jnp.where(lane < HALF, wide, 0.0).astype(jnp.bfloat16)
    second = jnp.where(lane < HALF, 0.0, wide).astype(jnp.bfloat16)
    return jnp.concatenate([first, second], axis=0)


def twice(row):
    return jnp.concatenate([row, row], axis=1)


def diagonal(pair):
    return jnp.concatenate([pair[:HALF, :QB], pair[HALF:, QB:]], axis=0)


def query_places(block):
    return block * QB + lax.broadcasted_iota(jnp.int32, (1, QB), 1)


def cross_forward_kernel(pairs, starts, pages, q_ref, k_ref, v_ref, o_ref, l_ref, vt_ref):
    page_count = k_ref.shape[0]
    for page in range(page_count):
        image = pages[page]
        low, high = starts[page], starts[page + 1]
        for pair in range(pairs):
            lanes = slice(pair * LANES, (pair + 1) * LANES)
            vt_ref[pair] = flip(v_ref[image, :, lanes])

        def body(block, carry):
            rows = pl.ds(pl.multiple_of(block * QB, QB), QB)
            place = query_places(block)
            member = (place >= low) & (place < high)
            for pair in range(pairs):
                lanes = slice(pair * LANES, (pair + 1) * LANES)
                stacked = head_stack(q_ref[rows, lanes], 0.125)
                scores = dot_nt(k_ref[image, :, lanes], stacked)
                peak = jnp.max(scores, axis=0, keepdims=True)
                raised = jnp.exp(scores - peak)
                total = jnp.sum(raised, axis=0, keepdims=True)
                attention = (raised * (1.0 / total)).astype(jnp.bfloat16)
                mixed = diagonal(dot_nn(vt_ref[pair], attention)).astype(jnp.bfloat16)
                lse = peak + jnp.log(total)
                o_ref[lanes, rows] = jnp.where(member, mixed, o_ref[lanes, rows])
                l_ref[0, 2 * pair : 2 * pair + 1, rows] = jnp.where(
                    member, lse[:, :QB], l_ref[0, 2 * pair : 2 * pair + 1, rows]
                )
                l_ref[0, 2 * pair + 1 : 2 * pair + 2, rows] = jnp.where(
                    member, lse[:, QB:], l_ref[0, 2 * pair + 1 : 2 * pair + 2, rows]
                )
            return carry

        lax.fori_loop(low // QB, (high - 1) // QB + 1, body, 0)


def flip(block):
    return jnp.transpose(block)


def cross_backward_kernel(
    pairs, starts, pages, q_ref, k_ref, v_ref, g_ref, l_ref, dq_ref, dk_ref, dv_ref,
    kt_ref, dka_ref, dva_ref,
):
    page_count = k_ref.shape[0]
    for page in range(page_count):
        image = pages[page]
        low, high = starts[page], starts[page + 1]
        for pair in range(pairs):
            lanes = slice(pair * LANES, (pair + 1) * LANES)
            kt_ref[pair] = flip(k_ref[image, :, lanes])
            dka_ref[pair] = jnp.zeros(dka_ref.shape[1:], jnp.float32)
            dva_ref[pair] = jnp.zeros(dva_ref.shape[1:], jnp.float32)

        def body(block, carry):
            rows = pl.ds(pl.multiple_of(block * QB, QB), QB)
            place = query_places(block)
            member = (place >= low) & (place < high)
            for pair in range(pairs):
                lanes = slice(pair * LANES, (pair + 1) * LANES)
                stacked = head_stack(q_ref[rows, lanes], 0.125)
                pulled = head_stack(g_ref[rows, lanes])
                lse = jnp.concatenate(
                    [
                        jnp.where(member, l_ref[0, 2 * pair : 2 * pair + 1, rows], 1e30),
                        jnp.where(member, l_ref[0, 2 * pair + 1 : 2 * pair + 2, rows], 1e30),
                    ],
                    axis=1,
                )
                scores = dot_nt(k_ref[image, :, lanes], stacked)
                attention = jnp.exp(scores - lse)
                pushed = dot_nt(v_ref[image, :, lanes], pulled)
                dva_ref[pair] += dot_nn(attention.astype(jnp.bfloat16), pulled)
                inner = jnp.sum(attention * pushed, axis=0, keepdims=True)
                grad = (attention * (pushed - inner)).astype(jnp.bfloat16)
                dka_ref[pair] += dot_nn(grad, stacked)
                turned = diagonal(dot_nn(kt_ref[pair], grad) * 0.125).astype(jnp.bfloat16)
                dq_ref[lanes, rows] = jnp.where(member, turned, dq_ref[lanes, rows])
            return carry

        lax.fori_loop(low // QB, (high - 1) // QB + 1, body, 0)
        for pair in range(pairs):
            lanes = slice(pair * LANES, (pair + 1) * LANES)
            dk_ref[image, :, lanes] = dka_ref[pair].astype(jnp.bfloat16)
            dv_ref[image, :, lanes] = dva_ref[pair].astype(jnp.bfloat16)


def self_window(starts, block):
    start = starts[0]
    for page in range(1, starts.shape[0] - 1):
        start = jnp.where(starts[page] <= block * QB, starts[page], start)
    first = start // QB
    return first, block + 1 - first


def self_allowed(starts, place, first, chunks):
    begin = jnp.zeros(place.shape, jnp.int32)
    for page in range(1, starts.shape[0] - 1):
        begin = jnp.where(place >= starts[page], starts[page], begin)
    begin, end = twice(begin), twice(place)
    key = first * QB + lax.broadcasted_iota(jnp.int32, (chunks * QB, 2 * QB), 0)
    return (key >= begin) & (key <= end)


def self_forward_kernel(pairs, most, starts, q_ref, k_ref, v_ref, o_ref, l_ref, vt_ref):
    for pair in range(pairs):
        lanes = slice(pair * LANES, (pair + 1) * LANES)
        vt_ref[pair] = flip(v_ref[:, lanes])

    def body(block, carry):
        rows = pl.ds(pl.multiple_of(block * QB, QB), QB)
        first, count = self_window(starts, block)
        for chunks in range(1, most + 1):

            @pl.when(count == chunks)
            def _():
                keys = pl.ds(pl.multiple_of(first * QB, QB), chunks * QB)
                allowed = self_allowed(starts, query_places(block), first, chunks)
                for pair in range(pairs):
                    lanes = slice(pair * LANES, (pair + 1) * LANES)
                    stacked = head_stack(q_ref[rows, lanes], 0.125)
                    scores = jnp.where(allowed, dot_nt(k_ref[keys, lanes], stacked), -1e30)
                    peak = jnp.max(scores, axis=0, keepdims=True)
                    raised = jnp.exp(scores - peak)
                    total = jnp.sum(raised, axis=0, keepdims=True)
                    attention = (raised * (1.0 / total)).astype(jnp.bfloat16)
                    mixed = diagonal(dot_nn(vt_ref[pair, :, keys], attention))
                    lse = peak + jnp.log(total)
                    o_ref[lanes, rows] = mixed.astype(jnp.bfloat16)
                    l_ref[0, 2 * pair : 2 * pair + 1, rows] = lse[:, :QB]
                    l_ref[0, 2 * pair + 1 : 2 * pair + 2, rows] = lse[:, QB:]

        return carry

    lax.fori_loop(0, q_ref.shape[0] // QB, body, 0)


def self_backward_kernel(
    pairs, most, starts, q_ref, k_ref, v_ref, g_ref, l_ref, dq_ref, dk_ref, dv_ref,
    kt_ref, dka_ref, dva_ref,
):
    for pair in range(pairs):
        lanes = slice(pair * LANES, (pair + 1) * LANES)
        kt_ref[pair] = flip(k_ref[:, lanes])
    dka_ref[...] = jnp.zeros(dka_ref.shape, jnp.float32)
    dva_ref[...] = jnp.zeros(dva_ref.shape, jnp.float32)

    def body(block, carry):
        rows = pl.ds(pl.multiple_of(block * QB, QB), QB)
        first, count = self_window(starts, block)
        for chunks in range(1, most + 1):

            @pl.when(count == chunks)
            def _():
                keys = pl.ds(pl.multiple_of(first * QB, QB), chunks * QB)
                allowed = self_allowed(starts, query_places(block), first, chunks)
                for pair in range(pairs):
                    lanes = slice(pair * LANES, (pair + 1) * LANES)
                    stacked = head_stack(q_ref[rows, lanes], 0.125)
                    pulled = head_stack(g_ref[rows, lanes])
                    lse = jnp.concatenate(
                        [l_ref[0, 2 * pair : 2 * pair + 1, rows], l_ref[0, 2 * pair + 1 : 2 * pair + 2, rows]],
                        axis=1,
                    )
                    scores = jnp.where(allowed, dot_nt(k_ref[keys, lanes], stacked), -1e30)
                    attention = jnp.exp(scores - lse)
                    pushed = dot_nt(v_ref[keys, lanes], pulled)
                    dva_ref[pair, keys, :] += dot_nn(attention.astype(jnp.bfloat16), pulled)
                    inner = jnp.sum(attention * pushed, axis=0, keepdims=True)
                    grad = (attention * (pushed - inner)).astype(jnp.bfloat16)
                    dka_ref[pair, keys, :] += dot_nn(grad, stacked)
                    turned = diagonal(dot_nn(kt_ref[pair, :, keys], grad) * 0.125)
                    dq_ref[lanes, rows] = turned.astype(jnp.bfloat16)

        return carry

    lax.fori_loop(0, q_ref.shape[0] // QB, body, 0)
    for pair in range(pairs):
        lanes = slice(pair * LANES, (pair + 1) * LANES)
        dk_ref[:, lanes] = dka_ref[pair].astype(jnp.bfloat16)
        dv_ref[:, lanes] = dva_ref[pair].astype(jnp.bfloat16)


def cost(flops, bytes_accessed, exps):
    return pl.CostEstimate(flops=flops, bytes_accessed=bytes_accessed, transcendentals=exps)


def specs(pairs, prefetch):
    wide = pairs * LANES

    def at(index):
        return lambda step, *scalars: index(step)

    return {
        "rows": lambda length: pl.BlockSpec((length, wide), at(lambda i: (0, i))),
        "turned": lambda length: pl.BlockSpec((wide, length), at(lambda i: (i, 0))),
        "images": lambda count, tokens: pl.BlockSpec((count, tokens, wide), at(lambda i: (0, 0, i))),
        "stats": lambda length: pl.BlockSpec((1, 2 * pairs, length), at(lambda i: (i, 0, 0))),
    }


def cross_forward(starts, pages, queries, keys_all, values_all, pairs=2):
    length, width = queries.shape
    count, tokens, _ = keys_all.shape
    steps = width // (pairs * LANES)
    s = specs(pairs, 2)
    return pl.pallas_call(
        functools.partial(cross_forward_kernel, pairs),
        out_shape=(
            jax.ShapeDtypeStruct((width, length), jnp.bfloat16),
            jax.ShapeDtypeStruct((steps, 2 * pairs, length), jnp.float32),
        ),
        grid_spec=pltpu.PrefetchScalarGridSpec(
            num_scalar_prefetch=2,
            grid=(steps,),
            in_specs=[s["rows"](length), s["images"](count, tokens), s["images"](count, tokens)],
            out_specs=[s["turned"](length), s["stats"](length)],
            scratch_shapes=[pltpu.VMEM((pairs, LANES, tokens), jnp.bfloat16)],
        ),
        cost_estimate=cost(11 * 128 * tokens * width * 4 * 4, 20 * 2**20, 2**24),
        name="cross_forward",
    )(starts, pages, queries, keys_all, values_all)


def cross_backward(starts, pages, queries, keys_all, values_all, grads, stats, pairs=2):
    length, width = queries.shape
    count, tokens, _ = keys_all.shape
    steps = width // (pairs * LANES)
    s = specs(pairs, 2)
    image_spec = s["images"](count, tokens)
    return pl.pallas_call(
        functools.partial(cross_backward_kernel, pairs),
        out_shape=(
            jax.ShapeDtypeStruct((width, length), jnp.bfloat16),
            jax.ShapeDtypeStruct(keys_all.shape, jnp.bfloat16),
            jax.ShapeDtypeStruct(values_all.shape, jnp.bfloat16),
        ),
        grid_spec=pltpu.PrefetchScalarGridSpec(
            num_scalar_prefetch=2,
            grid=(steps,),
            in_specs=[s["rows"](length), image_spec, image_spec, s["rows"](length), s["stats"](length)],
            out_specs=[s["turned"](length), image_spec, image_spec],
            scratch_shapes=[
                pltpu.VMEM((pairs, LANES, tokens), jnp.bfloat16),
                pltpu.VMEM((pairs, tokens, LANES), jnp.float32),
                pltpu.VMEM((pairs, tokens, LANES), jnp.float32),
            ],
        ),
        cost_estimate=cost(11 * 128 * tokens * width * 10 * 4, 30 * 2**20, 2**24),
        name="cross_backward",
    )(starts, pages, queries, keys_all, values_all, grads, stats)


def self_forward(starts, queries, keys_all, values_all, most, pairs=2):
    length, width = queries.shape
    steps = width // (pairs * LANES)
    s = specs(pairs, 1)
    rows = s["rows"](length)
    return pl.pallas_call(
        functools.partial(self_forward_kernel, pairs, most),
        out_shape=(
            jax.ShapeDtypeStruct((width, length), jnp.bfloat16),
            jax.ShapeDtypeStruct((steps, 2 * pairs, length), jnp.float32),
        ),
        grid_spec=pltpu.PrefetchScalarGridSpec(
            num_scalar_prefetch=1,
            grid=(steps,),
            in_specs=[rows, rows, rows],
            out_specs=[s["turned"](length), s["stats"](length)],
            scratch_shapes=[pltpu.VMEM((pairs, LANES, length), jnp.bfloat16)],
        ),
        cost_estimate=cost(20 * 128 * 128 * width * 4 * 4, 10 * 2**20, 2**23),
        name="self_forward",
    )(starts, queries, keys_all, values_all)


def self_backward(starts, queries, keys_all, values_all, grads, stats, most, pairs=2):
    length, width = queries.shape
    steps = width // (pairs * LANES)
    s = specs(pairs, 1)
    rows = s["rows"](length)
    return pl.pallas_call(
        functools.partial(self_backward_kernel, pairs, most),
        out_shape=(
            jax.ShapeDtypeStruct((width, length), jnp.bfloat16),
            jax.ShapeDtypeStruct((length, width), jnp.bfloat16),
            jax.ShapeDtypeStruct((length, width), jnp.bfloat16),
        ),
        grid_spec=pltpu.PrefetchScalarGridSpec(
            num_scalar_prefetch=1,
            grid=(steps,),
            in_specs=[rows, rows, rows, rows, s["stats"](length)],
            out_specs=[s["turned"](length), rows, rows],
            scratch_shapes=[
                pltpu.VMEM((pairs, LANES, length), jnp.bfloat16),
                pltpu.VMEM((pairs, length, LANES), jnp.float32),
                pltpu.VMEM((pairs, length, LANES), jnp.float32),
            ],
        ),
        cost_estimate=cost(20 * 128 * 128 * width * 10 * 4, 16 * 2**20, 2**23),
        name="self_backward",
    )(starts, queries, keys_all, values_all, grads, stats)


EPSILON = 1e-05
ROOT_HALF = 0.7071067811865476
ROOT_TAU = 0.3989422804014327
AXES = ("dp", "fsdp")
LONGEST = 512


def contract(a, b, left, right, out=jnp.float32):
    return lax.dot_general(
        a, b, ((left, right), ((), ())), preferred_element_type=jnp.float32
    ).astype(out)


def normalise(values):
    average = jnp.mean(values, axis=-1, keepdims=True)
    centered = values - average
    variance = jnp.mean(centered * centered, axis=-1, keepdims=True)
    scale = lax.rsqrt(variance + EPSILON)
    return centered * scale, scale


def norm_back(values, gain, grads):
    hat, scale = normalise(values)
    pulled = grads * gain
    first = jnp.mean(pulled, axis=-1, keepdims=True)
    second = jnp.mean(pulled * hat, axis=-1, keepdims=True)
    back = scale * (pulled - first - hat * second)
    return back, jnp.sum(grads * hat, axis=0), jnp.sum(grads, axis=0)


def swap(value, axis, size, bit):
    return lax.ppermute(value, axis, [(i, i ^ bit) for i in range(size)])


def butterfly_sum(value, sizes):
    for axis, size in sizes:
        bit = 1
        while bit < size:
            value = value + swap(value, axis, size, bit)
            bit *= 2
    return value


def pick(value, index, axis):
    return lax.dynamic_index_in_dim(value, index, axis, keepdims=False)


def reduce_rows(grads, sizes):
    dp_size, inner = sizes
    place = lax.axis_index("dp")
    low, high = place % 2, place // 2
    count = len(grads)
    rows, columns = grads[0].shape
    own = rows // (dp_size * inner)
    sends = [g.reshape(dp_size // 2, 2, inner * own, columns) for g in grads]
    keeps = [pick(g, low, 1) for g in sends]
    sends = [pick(g, 1 - low, 1) for g in sends]
    got = [swap(s, "dp", dp_size, 1) for s in sends]

    def half(index):
        return [
            (pick(k, index, 0).astype(jnp.float32) + pick(r, index, 0).astype(jnp.float32))
            for k, r in zip(keeps, got)
        ]

    out = [s.astype(jnp.bfloat16) for s in half(1 - high)]
    mine = half(high)
    came = [swap(s, "dp", dp_size, 2) for s in out]
    both = [(m + c.astype(jnp.float32)).astype(jnp.bfloat16) for m, c in zip(mine, came)]
    packed = jnp.stack([b.reshape(inner, own, columns) for b in both], axis=1)
    packed = packed.reshape(inner * count * own, columns)
    summed = lax.psum_scatter(packed, "fsdp", scatter_dimension=0, tiled=True)
    summed = summed.reshape(count, own, columns).astype(jnp.float32)
    return [summed[i] for i in range(count)]


def layer(
    sizes, block_in, images, segment_ids, page_map, ln1_gain, ln1_shift, ln2_gain, ln2_shift,
    ln3_gain, ln3_shift, self_query, self_key, self_value, self_out, cross_query, cross_key,
    cross_value, cross_out, mlp_in, mlp_out, cotangent,
):
    dp_size, inner = sizes
    axes = (("dp", dp_size), ("fsdp", inner))
    _, length, width = block_in.shape
    low = jnp.bfloat16

    def turned(master):
        return master.astype(low).T

    def gather(*masters):
        stacked = jnp.stack([turned(m) for m in masters])
        return lax.all_gather(stacked, AXES, axis=1, tiled=True)

    norms = jnp.stack([ln1_gain, ln1_shift, ln2_gain, ln2_shift, ln3_gain, ln3_shift])
    norms = norms.astype(low).astype(jnp.float32)
    mine = norms.shape[1]
    offset = (lax.axis_index("dp") * inner + lax.axis_index("fsdp")) * mine
    spread = lax.dynamic_update_slice(jnp.zeros((6, width), jnp.float32), norms, (0, offset))
    norms = butterfly_sum(spread, axes)
    w_sqkv = gather(self_query, self_key, self_value)
    w_rest = gather(self_out, cross_query, cross_key, cross_value, cross_out)
    w_in = lax.all_gather(turned(mlp_in), AXES, axis=0, tiled=True)
    w_out = lax.all_gather(turned(mlp_out), AXES, axis=0, tiled=True)
    w_so, w_cq, w_ck, w_cv, w_co = [w_rest[i] for i in range(5)]

    starts = jnp.sum(
        segment_ids[0][None, :] < jnp.arange(page_map.shape[1] + 1, dtype=jnp.int32)[:, None],
        axis=1,
    ).astype(jnp.int32)
    pages = page_map[0]
    most = LONGEST // QB + 1

    rows = block_in[0].astype(jnp.float32)
    a1 = (normalise(rows)[0] * norms[0] + norms[1]).astype(low)
    sq, sk, sv = [contract(a1, w_sqkv[i], (1,), (1,), low) for i in range(3)]
    so, s_stats = self_forward(starts, sq, sk, sv, most)
    x1 = rows + contract(so, w_so, (0,), (1,))
    a2 = (normalise(x1)[0] * norms[2] + norms[3]).astype(low)
    cq = contract(a2, w_cq, (1,), (1,), low)
    ck = contract(images, w_ck, (2,), (1,), low)
    cv = contract(images, w_cv, (2,), (1,), low)
    co, c_stats = cross_forward(starts, pages, cq, ck, cv)
    x2 = x1 + contract(co, w_co, (0,), (1,))
    a3 = (normalise(x2)[0] * norms[4] + norms[5]).astype(low)
    u = contract(a3, w_in, (1,), (1,))
    phi = 0.5 * (1.0 + lax.erf(u * ROOT_HALF))
    hidden = (u * phi).astype(low)
    slope = (phi + u * (ROOT_TAU * jnp.exp(-0.5 * u * u))).astype(low)
    block_out = (x2 + contract(hidden, w_out, (1,), (1,))).astype(low)

    eb = cotangent[0]
    e = eb.astype(jnp.float32)
    du = (contract(eb, w_out, (1,), (0,)) * slope.astype(jnp.float32)).astype(low)
    g_out = contract(eb, hidden, (0,), (0,), low)
    g_in = contract(du, a3, (0,), (0,), low)
    d3 = contract(du, w_in, (1,), (0,))
    (g_mlp_out,) = reduce_rows([g_out], sizes)
    (g_mlp_in,) = reduce_rows([g_in], sizes)
    back, gg3, gs3 = norm_back(x2, norms[4], d3)
    e2 = e + back
    e2b = e2.astype(low)
    g_co = contract(e2b, co, (0,), (1,), low)
    d_co = contract(e2b, w_co, (1,), (0,), low)
    dcq, dck, dcv = cross_backward(starts, pages, cq, ck, cv, d_co, c_stats)
    g_cq = contract(dcq, a2, (1,), (0,), low)
    g_ck = contract(dck, images, (0, 1), (0, 1), low)
    g_cv = contract(dcv, images, (0, 1), (0, 1), low)
    g_cross = reduce_rows([g_cq, g_ck, g_cv, g_co], sizes)
    grad_images = contract(dck, w_ck, (2,), (0,)) + contract(dcv, w_cv, (2,), (0,))
    d2 = contract(dcq, w_cq, (0,), (0,))
    back, gg2, gs2 = norm_back(x1, norms[2], d2)
    e1 = e2 + back
    e1b = e1.astype(low)
    g_so = contract(e1b, so, (0,), (1,), low)
    d_so = contract(e1b, w_so, (1,), (0,), low)
    dsq, dsk, dsv = self_backward(starts, sq, sk, sv, d_so, s_stats, most)
    g_sq = contract(dsq, a1, (1,), (0,), low)
    g_sk = contract(dsk, a1, (0,), (0,), low)
    g_sv = contract(dsv, a1, (0,), (0,), low)
    g_self = reduce_rows([g_sq, g_sk, g_sv, g_so], sizes)
    d1 = (
        contract(dsq, w_sqkv[0], (0,), (0,))
        + contract(dsk, w_sqkv[1], (1,), (0,))
        + contract(dsv, w_sqkv[2], (1,), (0,))
    )
    back, gg1, gs1 = norm_back(rows, norms[0], d1)
    grad_in = e1 + back
    norm_grads = butterfly_sum(jnp.stack([gg1, gs1, gg2, gs2, gg3, gs3]), axes)
    norm_grads = lax.dynamic_slice(norm_grads, (0, offset), (6, mine))
    weight_grads = [g.T for g in g_self + g_cross + [g_mlp_in, g_mlp_out]]
    return (
        block_out[None], grad_in[None], grad_images, *[norm_grads[i] for i in range(6)],
        *weight_grads,
    )


def solution(mesh):
    sizes = (mesh.shape["dp"], mesh.shape["fsdp"])
    rows3 = P(AXES, None, None)
    rows2 = P(AXES, None)
    vector = P(AXES)
    columns = P(None, AXES)
    return jax.shard_map(
        functools.partial(layer, sizes),
        mesh=mesh,
        in_specs=(rows3, rows3, rows2, rows2) + (vector,) * 6 + (columns,) * 10 + (rows3,),
        out_specs=(rows3,) * 3 + (vector,) * 6 + (columns,) * 10,
        check_vma=False,
    )
```

```python
import functools
import jax
import jax.numpy as jnp
from jax import lax
from jax.experimental import pallas as pl
from jax.experimental.pallas import tpu as pltpu
from jax.sharding import PartitionSpec as P

LANES = 128
HALF = 64
QB = 128


def dot_nt(a, b):
    return lax.dot_general(a, b, (((1,), (1,)), ((), ())), preferred_element_type=jnp.float32)


def dot_nn(a, b):
    return lax.dot_general(a, b, (((1,), (0,)), ((), ())), preferred_element_type=jnp.float32)


def head_stack(block, scale=None):
    lane = lax.broadcasted_iota(jnp.int32, block.shape, 1)
    wide = block.astype(jnp.float32)
    if scale is not None:
        wide = wide * scale
    first = jnp.where(lane < HALF, wide, 0.0).astype(jnp.bfloat16)
    second = jnp.where(lane < HALF, 0.0, wide).astype(jnp.bfloat16)
    return jnp.concatenate([first, second], axis=0)


def twice(row):
    return jnp.concatenate([row, row], axis=1)


def diagonal(pair):
    return jnp.concatenate([pair[:HALF, :QB], pair[HALF:, QB:]], axis=0)


def query_places(block):
    return block * QB + lax.broadcasted_iota(jnp.int32, (1, QB), 1)


def cross_forward_kernel(pairs, starts, pages, q_ref, k_ref, v_ref, o_ref, l_ref, vt_ref):
    page_count = k_ref.shape[0]
    for page in range(page_count):
        image = pages[page]
        low, high = starts[page], starts[page + 1]
        for pair in range(pairs):
            lanes = slice(pair * LANES, (pair + 1) * LANES)
            vt_ref[pair] = flip(v_ref[image, :, lanes])

        def body(block, carry):
            rows = pl.ds(pl.multiple_of(block * QB, QB), QB)
            place = query_places(block)
            member = (place >= low) & (place < high)
            for pair in range(pairs):
                lanes = slice(pair * LANES, (pair + 1) * LANES)
                stacked = head_stack(q_ref[rows, lanes], 0.125)
                scores = dot_nt(k_ref[image, :, lanes], stacked)
                peak = jnp.max(scores, axis=0, keepdims=True)
                raised = jnp.exp(scores - peak)
                total = jnp.sum(raised, axis=0, keepdims=True)
                attention = (raised * (1.0 / total)).astype(jnp.bfloat16)
                mixed = diagonal(dot_nn(vt_ref[pair], attention)).astype(jnp.bfloat16)
                lse = peak + jnp.log(total)
                o_ref[lanes, rows] = jnp.where(member, mixed, o_ref[lanes, rows])
                l_ref[0, 2 * pair : 2 * pair + 1, rows] = jnp.where(
                    member, lse[:, :QB], l_ref[0, 2 * pair : 2 * pair + 1, rows]
                )
                l_ref[0, 2 * pair + 1 : 2 * pair + 2, rows] = jnp.where(
                    member, lse[:, QB:], l_ref[0, 2 * pair + 1 : 2 * pair + 2, rows]
                )
            return carry

        lax.fori_loop(low // QB, (high - 1) // QB + 1, body, 0)


def flip(block):
    return jnp.transpose(block)


def cross_backward_kernel(
    pairs, starts, pages, q_ref, k_ref, v_ref, g_ref, l_ref, dq_ref, dk_ref, dv_ref,
    kt_ref, dka_ref, dva_ref,
):
    page_count = k_ref.shape[0]
    for page in range(page_count):
        image = pages[page]
        low, high = starts[page], starts[page + 1]
        for pair in range(pairs):
            lanes = slice(pair * LANES, (pair + 1) * LANES)
            kt_ref[pair] = flip(k_ref[image, :, lanes])
            dka_ref[pair] = jnp.zeros(dka_ref.shape[1:], jnp.float32)
            dva_ref[pair] = jnp.zeros(dva_ref.shape[1:], jnp.float32)

        def body(block, carry):
            rows = pl.ds(pl.multiple_of(block * QB, QB), QB)
            place = query_places(block)
            member = (place >= low) & (place < high)
            for pair in range(pairs):
                lanes = slice(pair * LANES, (pair + 1) * LANES)
                stacked = head_stack(q_ref[rows, lanes], 0.125)
                pulled = head_stack(g_ref[rows, lanes])
                lse = jnp.concatenate(
                    [
                        jnp.where(member, l_ref[0, 2 * pair : 2 * pair + 1, rows], 1e30),
                        jnp.where(member, l_ref[0, 2 * pair + 1 : 2 * pair + 2, rows], 1e30),
                    ],
                    axis=1,
                )
                scores = dot_nt(k_ref[image, :, lanes], stacked)
                attention = jnp.exp(scores - lse)
                pushed = dot_nt(v_ref[image, :, lanes], pulled)
                dva_ref[pair] += dot_nn(attention.astype(jnp.bfloat16), pulled)
                inner = jnp.sum(attention * pushed, axis=0, keepdims=True)
                grad = (attention * (pushed - inner)).astype(jnp.bfloat16)
                dka_ref[pair] += dot_nn(grad, stacked)
                turned = diagonal(dot_nn(kt_ref[pair], grad) * 0.125).astype(jnp.bfloat16)
                dq_ref[lanes, rows] = jnp.where(member, turned, dq_ref[lanes, rows])
            return carry

        lax.fori_loop(low // QB, (high - 1) // QB + 1, body, 0)
        for pair in range(pairs):
            lanes = slice(pair * LANES, (pair + 1) * LANES)
            dk_ref[image, :, lanes] = dka_ref[pair].astype(jnp.bfloat16)
            dv_ref[image, :, lanes] = dva_ref[pair].astype(jnp.bfloat16)


def self_window(starts, block):
    start = starts[0]
    for page in range(1, starts.shape[0] - 1):
        start = jnp.where(starts[page] <= block * QB, starts[page], start)
    first = start // QB
    return first, block + 1 - first


def self_allowed(starts, place, first, chunks):
    begin = jnp.zeros(place.shape, jnp.int32)
    for page in range(1, starts.shape[0] - 1):
        begin = jnp.where(place >= starts[page], starts[page], begin)
    begin, end = twice(begin), twice(place)
    key = first * QB + lax.broadcasted_iota(jnp.int32, (chunks * QB, 2 * QB), 0)
    return (key >= begin) & (key <= end)


def self_forward_kernel(pairs, most, starts, q_ref, k_ref, v_ref, o_ref, l_ref, vt_ref):
    for pair in range(pairs):
        lanes = slice(pair * LANES, (pair + 1) * LANES)
        vt_ref[pair] = flip(v_ref[:, lanes])

    def body(block, carry):
        rows = pl.ds(pl.multiple_of(block * QB, QB), QB)
        first, count = self_window(starts, block)
        for chunks in range(1, most + 1):

            @pl.when(count == chunks)
            def _():
                keys = pl.ds(pl.multiple_of(first * QB, QB), chunks * QB)
                allowed = self_allowed(starts, query_places(block), first, chunks)
                for pair in range(pairs):
                    lanes = slice(pair * LANES, (pair + 1) * LANES)
                    stacked = head_stack(q_ref[rows, lanes], 0.125)
                    scores = jnp.where(allowed, dot_nt(k_ref[keys, lanes], stacked), -1e30)
                    peak = jnp.max(scores, axis=0, keepdims=True)
                    raised = jnp.exp(scores - peak)
                    total = jnp.sum(raised, axis=0, keepdims=True)
                    attention = (raised * (1.0 / total)).astype(jnp.bfloat16)
                    mixed = diagonal(dot_nn(vt_ref[pair, :, keys], attention))
                    lse = peak + jnp.log(total)
                    o_ref[lanes, rows] = mixed.astype(jnp.bfloat16)
                    l_ref[0, 2 * pair : 2 * pair + 1, rows] = lse[:, :QB]
                    l_ref[0, 2 * pair + 1 : 2 * pair + 2, rows] = lse[:, QB:]

        return carry

    lax.fori_loop(0, q_ref.shape[0] // QB, body, 0)


def self_backward_kernel(
    pairs, most, starts, q_ref, k_ref, v_ref, g_ref, l_ref, dq_ref, dk_ref, dv_ref,
    kt_ref, dka_ref, dva_ref,
):
    for pair in range(pairs):
        lanes = slice(pair * LANES, (pair + 1) * LANES)
        kt_ref[pair] = flip(k_ref[:, lanes])
    dka_ref[...] = jnp.zeros(dka_ref.shape, jnp.float32)
    dva_ref[...] = jnp.zeros(dva_ref.shape, jnp.float32)

    def body(block, carry):
        rows = pl.ds(pl.multiple_of(block * QB, QB), QB)
        first, count = self_window(starts, block)
        for chunks in range(1, most + 1):

            @pl.when(count == chunks)
            def _():
                keys = pl.ds(pl.multiple_of(first * QB, QB), chunks * QB)
                allowed = self_allowed(starts, query_places(block), first, chunks)
                for pair in range(pairs):
                    lanes = slice(pair * LANES, (pair + 1) * LANES)
                    stacked = head_stack(q_ref[rows, lanes], 0.125)
                    pulled = head_stack(g_ref[rows, lanes])
                    lse = jnp.concatenate(
                        [l_ref[0, 2 * pair : 2 * pair + 1, rows], l_ref[0, 2 * pair + 1 : 2 * pair + 2, rows]],
                        axis=1,
                    )
                    scores = jnp.where(allowed, dot_nt(k_ref[keys, lanes], stacked), -1e30)
                    attention = jnp.exp(scores - lse)
                    pushed = dot_nt(v_ref[keys, lanes], pulled)
                    dva_ref[pair, keys, :] += dot_nn(attention.astype(jnp.bfloat16), pulled)
                    inner = jnp.sum(attention * pushed, axis=0, keepdims=True)
                    grad = (attention * (pushed - inner)).astype(jnp.bfloat16)
                    dka_ref[pair, keys, :] += dot_nn(grad, stacked)
                    turned = diagonal(dot_nn(kt_ref[pair, :, keys], grad) * 0.125)
                    dq_ref[lanes, rows] = turned.astype(jnp.bfloat16)

        return carry

    lax.fori_loop(0, q_ref.shape[0] // QB, body, 0)
    for pair in range(pairs):
        lanes = slice(pair * LANES, (pair + 1) * LANES)
        dk_ref[:, lanes] = dka_ref[pair].astype(jnp.bfloat16)
        dv_ref[:, lanes] = dva_ref[pair].astype(jnp.bfloat16)


def cost(flops, bytes_accessed, exps):
    return pl.CostEstimate(flops=flops, bytes_accessed=bytes_accessed, transcendentals=exps)


def specs(pairs, prefetch):
    wide = pairs * LANES

    def at(index):
        return lambda step, *scalars: index(step)

    return {
        "rows": lambda length: pl.BlockSpec((length, wide), at(lambda i: (0, i))),
        "turned": lambda length: pl.BlockSpec((wide, length), at(lambda i: (i, 0))),
        "images": lambda count, tokens: pl.BlockSpec((count, tokens, wide), at(lambda i: (0, 0, i))),
        "stats": lambda length: pl.BlockSpec((1, 2 * pairs, length), at(lambda i: (i, 0, 0))),
    }


def cross_forward(starts, pages, queries, keys_all, values_all, pairs=2):
    length, width = queries.shape
    count, tokens, _ = keys_all.shape
    steps = width // (pairs * LANES)
    s = specs(pairs, 2)
    return pl.pallas_call(
        functools.partial(cross_forward_kernel, pairs),
        out_shape=(
            jax.ShapeDtypeStruct((width, length), jnp.bfloat16),
            jax.ShapeDtypeStruct((steps, 2 * pairs, length), jnp.float32),
        ),
        grid_spec=pltpu.PrefetchScalarGridSpec(
            num_scalar_prefetch=2,
            grid=(steps,),
            in_specs=[s["rows"](length), s["images"](count, tokens), s["images"](count, tokens)],
            out_specs=[s["turned"](length), s["stats"](length)],
            scratch_shapes=[pltpu.VMEM((pairs, LANES, tokens), jnp.bfloat16)],
        ),
        cost_estimate=cost(11 * 128 * tokens * width * 4 * 4, 20 * 2**20, 2**24),
        name="cross_forward",
    )(starts, pages, queries, keys_all, values_all)


def cross_backward(starts, pages, queries, keys_all, values_all, grads, stats, pairs=2):
    length, width = queries.shape
    count, tokens, _ = keys_all.shape
    steps = width // (pairs * LANES)
    s = specs(pairs, 2)
    image_spec = s["images"](count, tokens)
    return pl.pallas_call(
        functools.partial(cross_backward_kernel, pairs),
        out_shape=(
            jax.ShapeDtypeStruct((width, length), jnp.bfloat16),
            jax.ShapeDtypeStruct(keys_all.shape, jnp.bfloat16),
            jax.ShapeDtypeStruct(values_all.shape, jnp.bfloat16),
        ),
        grid_spec=pltpu.PrefetchScalarGridSpec(
            num_scalar_prefetch=2,
            grid=(steps,),
            in_specs=[s["rows"](length), image_spec, image_spec, s["rows"](length), s["stats"](length)],
            out_specs=[s["turned"](length), image_spec, image_spec],
            scratch_shapes=[
                pltpu.VMEM((pairs, LANES, tokens), jnp.bfloat16),
                pltpu.VMEM((pairs, tokens, LANES), jnp.float32),
                pltpu.VMEM((pairs, tokens, LANES), jnp.float32),
            ],
        ),
        cost_estimate=cost(11 * 128 * tokens * width * 10 * 4, 30 * 2**20, 2**24),
        name="cross_backward",
    )(starts, pages, queries, keys_all, values_all, grads, stats)


def self_forward(starts, queries, keys_all, values_all, most, pairs=2):
    length, width = queries.shape
    steps = width // (pairs * LANES)
    s = specs(pairs, 1)
    rows = s["rows"](length)
    return pl.pallas_call(
        functools.partial(self_forward_kernel, pairs, most),
        out_shape=(
            jax.ShapeDtypeStruct((width, length), jnp.bfloat16),
            jax.ShapeDtypeStruct((steps, 2 * pairs, length), jnp.float32),
        ),
        grid_spec=pltpu.PrefetchScalarGridSpec(
            num_scalar_prefetch=1,
            grid=(steps,),
            in_specs=[rows, rows, rows],
            out_specs=[s["turned"](length), s["stats"](length)],
            scratch_shapes=[pltpu.VMEM((pairs, LANES, length), jnp.bfloat16)],
        ),
        cost_estimate=cost(20 * 128 * 128 * width * 4 * 4, 10 * 2**20, 2**23),
        name="self_forward",
    )(starts, queries, keys_all, values_all)


def self_backward(starts, queries, keys_all, values_all, grads, stats, most, pairs=2):
    length, width = queries.shape
    steps = width // (pairs * LANES)
    s = specs(pairs, 1)
    rows = s["rows"](length)
    return pl.pallas_call(
        functools.partial(self_backward_kernel, pairs, most),
        out_shape=(
            jax.ShapeDtypeStruct((width, length), jnp.bfloat16),
            jax.ShapeDtypeStruct((length, width), jnp.bfloat16),
            jax.ShapeDtypeStruct((length, width), jnp.bfloat16),
        ),
        grid_spec=pltpu.PrefetchScalarGridSpec(
            num_scalar_prefetch=1,
            grid=(steps,),
            in_specs=[rows, rows, rows, rows, s["stats"](length)],
            out_specs=[s["turned"](length), rows, rows],
            scratch_shapes=[
                pltpu.VMEM((pairs, LANES, length), jnp.bfloat16),
                pltpu.VMEM((pairs, length, LANES), jnp.float32),
                pltpu.VMEM((pairs, length, LANES), jnp.float32),
            ],
        ),
        cost_estimate=cost(20 * 128 * 128 * width * 10 * 4, 16 * 2**20, 2**23),
        name="self_backward",
    )(starts, queries, keys_all, values_all, grads, stats)


EPSILON = 1e-05
ROOT_HALF = 0.7071067811865476
ROOT_TAU = 0.3989422804014327
AXES = ("dp", "fsdp")
LONGEST = 512


def contract(a, b, left, right, out=jnp.float32):
    return lax.dot_general(
        a, b, ((left, right), ((), ())), preferred_element_type=jnp.float32
    ).astype(out)


def normalise(values):
    average = jnp.mean(values, axis=-1, keepdims=True)
    centered = values - average
    variance = jnp.mean(centered * centered, axis=-1, keepdims=True)
    scale = lax.rsqrt(variance + EPSILON)
    return centered * scale, scale


def norm_back(values, gain, grads):
    hat, scale = normalise(values)
    pulled = grads * gain
    first = jnp.mean(pulled, axis=-1, keepdims=True)
    second = jnp.mean(pulled * hat, axis=-1, keepdims=True)
    back = scale * (pulled - first - hat * second)
    return back, jnp.sum(grads * hat, axis=0), jnp.sum(grads, axis=0)


def swap(value, axis, size, bit):
    return lax.ppermute(value, axis, [(i, i ^ bit) for i in range(size)])


def butterfly_sum(value, sizes):
    for axis, size in sizes:
        bit = 1
        while bit < size:
            value = value + swap(value, axis, size, bit)
            bit *= 2
    return value


def pick(value, index, axis):
    return lax.dynamic_index_in_dim(value, index, axis, keepdims=False)


def fence(*values):
    return lax.optimization_barrier(values)


class Partial:
    def __init__(self, value, sizes):
        dp_size, inner = sizes
        keys, places = [], {}
        for axis, size in (("dp", dp_size), ("fsdp", inner)):
            bit = size // 2
            while bit:
                keys.append((axis, bit))
                places[(axis, bit)] = (lax.axis_index(axis) // bit) % 2
                bit //= 2
        own = value.shape[0] // (dp_size * inner)
        self.sizes = {"dp": dp_size, "fsdp": inner}
        self.keys, self.places = keys, places
        self.value = value.reshape((2,) * len(keys) + (own, value.shape[1]))

    def send(self, key):
        axis = self.keys.index(key)
        self.keys.remove(key)
        out = pick(self.value, 1 - self.places[key], axis).astype(jnp.bfloat16)
        self.value = pick(self.value, self.places[key], axis).astype(jnp.float32)
        return swap(out, key[0], self.sizes[key[0]], key[1])

    def take(self, received):
        self.value = self.value + received.astype(jnp.float32)

    def rest(self):
        return self.value.astype(jnp.bfloat16)


CORE = ("dp", 1)
ACROSS = ("dp", 2)


def scatter(parts, sizes):
    inner = sizes[1]
    rests = []
    for part in parts:
        rest = part.rest()
        own, columns = rest.shape[-2:]
        rests.append(rest.reshape(inner, own, columns))
    packed = rests[0] if len(rests) == 1 else jnp.concatenate(rests, axis=1)
    summed = lax.psum_scatter(
        packed.reshape(-1, columns), "fsdp", scatter_dimension=0, tiled=True
    ).astype(jnp.float32)
    return [summed[i * own : (i + 1) * own] for i in range(len(parts))]


def layer(
    sizes, block_in, images, segment_ids, page_map, ln1_gain, ln1_shift, ln2_gain, ln2_shift,
    ln3_gain, ln3_shift, self_query, self_key, self_value, self_out, cross_query, cross_key,
    cross_value, cross_out, mlp_in, mlp_out, cotangent,
):
    dp_size, inner = sizes
    axes = (("dp", dp_size), ("fsdp", inner))
    _, length, width = block_in.shape
    low = jnp.bfloat16

    def turned(master):
        return master.astype(low).T

    def gather(*masters):
        stacked = jnp.stack([turned(m) for m in masters])
        return lax.all_gather(stacked, AXES, axis=1, tiled=True)

    norms = jnp.stack([ln1_gain, ln1_shift, ln2_gain, ln2_shift, ln3_gain, ln3_shift])
    norms = norms.astype(low).astype(jnp.float32)
    mine = norms.shape[1]
    offset = (lax.axis_index("dp") * inner + lax.axis_index("fsdp")) * mine
    spread = lax.dynamic_update_slice(jnp.zeros((6, width), jnp.float32), norms, (0, offset))
    norms = butterfly_sum(spread, axes)
    w_sqkv = gather(self_query, self_key, self_value)
    w_rest = gather(self_out, cross_query, cross_key, cross_value, cross_out)
    w_in = lax.all_gather(turned(mlp_in), AXES, axis=0, tiled=True)
    w_out = lax.all_gather(turned(mlp_out), AXES, axis=0, tiled=True)
    w_so, w_cq, w_ck, w_cv, w_co = [w_rest[i] for i in range(5)]

    starts = jnp.sum(
        segment_ids[0][None, :] < jnp.arange(page_map.shape[1] + 1, dtype=jnp.int32)[:, None],
        axis=1,
    ).astype(jnp.int32)
    pages = page_map[0]
    most = LONGEST // QB + 1

    rows = block_in[0].astype(jnp.float32)
    a1 = (normalise(rows)[0] * norms[0] + norms[1]).astype(low)
    sq, sk, sv = [contract(a1, w_sqkv[i], (1,), (1,), low) for i in range(3)]
    so, s_stats = self_forward(starts, sq, sk, sv, most)
    x1 = rows + contract(so, w_so, (0,), (1,))
    a2 = (normalise(x1)[0] * norms[2] + norms[3]).astype(low)
    cq = contract(a2, w_cq, (1,), (1,), low)
    ck = contract(images, w_ck, (2,), (1,), low)
    cv = contract(images, w_cv, (2,), (1,), low)
    co, c_stats = cross_forward(starts, pages, cq, ck, cv)
    x2 = x1 + contract(co, w_co, (0,), (1,))
    a3 = (normalise(x2)[0] * norms[4] + norms[5]).astype(low)
    u = contract(a3, w_in, (1,), (1,))
    phi = 0.5 * (1.0 + lax.erf(u * ROOT_HALF))
    hidden = (u * phi).astype(low)
    slope = (phi + u * (ROOT_TAU * jnp.exp(-0.5 * u * u))).astype(low)

    eb = cotangent[0]
    e = eb.astype(jnp.float32)
    g_out = contract(eb, hidden, (0,), (0,), low)
    p_out = Partial(g_out, sizes)
    flying = p_out.send(CORE)
    eb, hidden, g_out = fence(eb, hidden, g_out)
    du = (contract(eb, w_out, (1,), (0,)) * slope.astype(jnp.float32)).astype(low)
    du, flying = fence(du, flying)
    p_out.take(flying)
    flying = p_out.send(ACROSS)
    g_in = contract(du, a3, (0,), (0,), low)
    du, g_in = fence(du, g_in)
    p_in = Partial(g_in, sizes)
    flying_in = p_in.send(CORE)
    d3 = contract(du, w_in, (1,), (0,))
    back, gg3, gs3 = norm_back(x2, norms[4], d3)
    e2 = e + back
    e2b = e2.astype(low)
    e2, e2b, flying, flying_in = fence(e2, e2b, flying, flying_in)
    p_out.take(flying)
    (g_mlp_out,) = scatter([p_out], sizes)
    p_in.take(flying_in)
    flying_in = p_in.send(ACROSS)
    d_co = contract(e2b, w_co, (1,), (0,), low)
    dcq, dck, dcv = cross_backward(starts, pages, cq, ck, cv, d_co, c_stats)
    dcq, dck, dcv, flying_in = fence(dcq, dck, dcv, flying_in)
    p_in.take(flying_in)
    (g_mlp_in,) = scatter([p_in], sizes)
    g_co = contract(e2b, co, (0,), (1,), low)
    g_cq = contract(dcq, a2, (1,), (0,), low)
    g_ck = contract(dck, images, (0, 1), (0, 1), low)
    g_cv = contract(dcv, images, (0, 1), (0, 1), low)
    dcq, g_cq, g_ck, g_cv, g_co = fence(dcq, g_cq, g_ck, g_cv, g_co)
    p_cross = [Partial(g, sizes) for g in (g_cq, g_ck, g_cv, g_co)]
    flying = [p.send(CORE) for p in p_cross]
    d2 = contract(dcq, w_cq, (0,), (0,))
    back, gg2, gs2 = norm_back(x1, norms[2], d2)
    e1 = e2 + back
    e1b = e1.astype(low)
    e1, e1b, *flying = fence(e1, e1b, *flying)
    for p, f in zip(p_cross, flying):
        p.take(f)
    flying = [p.send(ACROSS) for p in p_cross]
    g_so = contract(e1b, so, (0,), (1,), low)
    p_so = Partial(g_so, sizes)
    flying_so = p_so.send(CORE)
    d_so = contract(e1b, w_so, (1,), (0,), low)
    dsq, dsk, dsv = self_backward(starts, sq, sk, sv, d_so, s_stats, most)
    dsq, dsk, dsv, flying_so, *flying = fence(dsq, dsk, dsv, flying_so, *flying)
    for p, f in zip(p_cross, flying):
        p.take(f)
    g_cross = scatter(p_cross, sizes)
    orders = []
    keys = [ACROSS] + [("fsdp", 1 << i) for i in range(inner.bit_length() - 1)]
    for shift in range(3):
        orders.append(keys[shift:] + keys[:shift])
    p_so.take(flying_so)
    flying_so = p_so.send(keys[0])
    g_sq = contract(dsq, a1, (1,), (0,), low)
    g_sk = contract(dsk, a1, (0,), (0,), low)
    g_sv = contract(dsv, a1, (0,), (0,), low)
    dsq, dsk, dsv, g_sq, g_sk, g_sv, flying_so = fence(dsq, dsk, dsv, g_sq, g_sk, g_sv, flying_so)
    p_so.take(flying_so)
    p_self = [Partial(g, sizes) for g in (g_sq, g_sk, g_sv)]
    flying = [p.send(CORE) for p in p_self]
    flying_so = p_so.send(keys[1])
    d1 = (
        contract(dsq, w_sqkv[0], (0,), (0,))
        + contract(dsk, w_sqkv[1], (1,), (0,))
        + contract(dsv, w_sqkv[2], (1,), (0,))
    )

    def norm_one(d1):
        back, gg1, gs1 = norm_back(rows, norms[0], d1)
        return e1 + back, gg1, gs1

    def image_grads(dck, dcv):
        both = jnp.concatenate([dck, dcv], axis=2).transpose(1, 0, 2)
        tokens, count, _ = both.shape
        flat = contract(
            both.reshape(tokens * count, 2 * width), w_rest[2:4].reshape(2 * width, width), (1,), (0,)
        )
        return flat.reshape(tokens, count, width).transpose(1, 0, 2)

    def finish(hidden):
        return (x2 + contract(hidden, w_out, (1,), (1,))).astype(low)

    fillers = [(norm_one, (d1,)), (finish, (hidden,)), (image_grads, (dck, dcv))]
    results = []
    waits = (d1,)
    parts = p_self + [p_so]
    flights = flying + [flying_so]
    for stage in range(len(keys)):
        if stage < 3:
            job, needs = fillers[stage]
            fenced = fence(*(flights + list(waits) + list(needs)))
            needs = fenced[-len(needs) :]
        else:
            fenced = fence(*(flights + list(waits)))
        for p, f in zip(parts, fenced):
            p.take(f)
        parts = [p for p in parts if len(p.keys)]
        flights = [p.send(o[stage]) for p, o in zip(p_self, orders)]
        if len(p_so.keys):
            flights.append(p_so.send(p_so.keys[-1] if len(p_so.keys) == 1 else keys[stage + 2]))
        if stage < 3:
            done = job(*needs)
            waits = jax.tree.leaves(done)[:1]
            results.append(done)
    for p, f in zip(parts, flights):
        p.take(f)
    grad_in, gg1, gs1 = results[0]
    block_out, grad_images = results[1], results[2]
    g_self = [p.value for p in p_self + [p_so]]
    norm_grads = butterfly_sum(jnp.stack([gg1, gs1, gg2, gs2, gg3, gs3]), axes)
    norm_grads = lax.dynamic_slice(norm_grads, (0, offset), (6, mine))
    weight_grads = [g.T for g in g_self + g_cross + [g_mlp_in, g_mlp_out]]
    return (
        block_out[None], grad_in[None], grad_images, *[norm_grads[i] for i in range(6)],
        *weight_grads,
    )


def solution(mesh):
    sizes = (mesh.shape["dp"], mesh.shape["fsdp"])
    rows3 = P(AXES, None, None)
    rows2 = P(AXES, None)
    vector = P(AXES)
    columns = P(None, AXES)
    return jax.shard_map(
        functools.partial(layer, sizes),
        mesh=mesh,
        in_specs=(rows3, rows3, rows2, rows2) + (vector,) * 6 + (columns,) * 10 + (rows3,),
        out_specs=(rows3,) * 3 + (vector,) * 6 + (columns,) * 10,
        check_vma=False,
    )
```

```python
import functools
import jax
import jax.numpy as jnp
from jax import lax
from jax.experimental import pallas as pl
from jax.experimental.layout import Layout, with_layout_constraint
from jax.experimental.pallas import tpu as pltpu
from jax.sharding import PartitionSpec as P

LANES = 128
HALF = 64
QB = 128


def dot_nt(a, b):
    return lax.dot_general(a, b, (((1,), (1,)), ((), ())), preferred_element_type=jnp.float32)


def dot_nn(a, b):
    return lax.dot_general(a, b, (((1,), (0,)), ((), ())), preferred_element_type=jnp.float32)


def head_stack(block, scale=None):
    lane = lax.broadcasted_iota(jnp.int32, block.shape, 1)
    wide = block.astype(jnp.float32)
    if scale is not None:
        wide = wide * scale
    first = jnp.where(lane < HALF, wide, 0.0).astype(jnp.bfloat16)
    second = jnp.where(lane < HALF, 0.0, wide).astype(jnp.bfloat16)
    return jnp.concatenate([first, second], axis=0)


def twice(row):
    return jnp.concatenate([row, row], axis=1)


def diagonal(pair):
    return jnp.concatenate([pair[:HALF, :QB], pair[HALF:, QB:]], axis=0)


def attend(scores, values_turned):
    peaks = [jnp.max(s, axis=0, keepdims=True) for s in scores]
    raised = [jnp.exp(s - peak) for s, peak in zip(scores, peaks)]
    totals = [jnp.sum(r, axis=0, keepdims=True) for r in raised]
    low = [(r * (1.0 / total)).astype(jnp.bfloat16) for r, total in zip(raised, totals)]
    mixed = [diagonal(dot_nn(vt, p)).astype(jnp.bfloat16) for vt, p in zip(values_turned, low)]
    stats = []
    for peak, total in zip(peaks, totals):
        lse = peak + jnp.log(total)
        stats += [lse[:, :QB], lse[:, QB:]]
    return mixed, jnp.concatenate(stats, axis=0)


def pull_back(scores, values_in, pulled, stats, keys_turned):
    attention = [
        jnp.exp(s - jnp.concatenate([stats[2 * i : 2 * i + 1], stats[2 * i + 1 : 2 * i + 2]], axis=1))
        for i, s in enumerate(scores)
    ]
    low = [a.astype(jnp.bfloat16) for a in attention]
    pushed = [dot_nt(v, g) for v, g in zip(values_in, pulled)]
    inner = [jnp.sum(a * p, axis=0, keepdims=True) for a, p in zip(attention, pushed)]
    grads = [
        (a * (p - i)).astype(jnp.bfloat16) for a, p, i in zip(attention, pushed, inner)
    ]
    turned = [
        diagonal(dot_nn(kt, g) * 0.125).astype(jnp.bfloat16) for kt, g in zip(keys_turned, grads)
    ]
    return low, grads, turned


def query_places(block):
    return block * QB + lax.broadcasted_iota(jnp.int32, (1, QB), 1)


def cross_forward_kernel(pairs, starts, pages, q_ref, k_ref, v_ref, o_ref, l_ref, vt_ref):
    page_count = k_ref.shape[0]
    for page in range(page_count):
        image = pages[page]
        low, high = starts[page], starts[page + 1]
        for pair in range(pairs):
            lanes = slice(pair * LANES, (pair + 1) * LANES)
            vt_ref[pair] = flip(v_ref[image, :, lanes])

        def body(block, carry):
            rows = pl.ds(pl.multiple_of(block * QB, QB), QB)
            place = query_places(block)
            member = (place >= low) & (place < high)
            spans = [slice(pair * LANES, (pair + 1) * LANES) for pair in range(pairs)]
            scores = [
                dot_nt(k_ref[image, :, lanes], head_stack(q_ref[rows, lanes], 0.125))
                for lanes in spans
            ]
            mixed, stats = attend(scores, [vt_ref[pair] for pair in range(pairs)])
            for lanes, block_out in zip(spans, mixed):
                o_ref[lanes, rows] = jnp.where(member, block_out, o_ref[lanes, rows])
            l_ref[0, :, rows] = jnp.where(member, stats, l_ref[0, :, rows])
            return carry

        lax.fori_loop(low // QB, (high - 1) // QB + 1, body, 0)


def flip(block):
    return jnp.transpose(block)


def cross_backward_kernel(
    pairs, starts, pages, q_ref, k_ref, v_ref, g_ref, l_ref, dq_ref, dk_ref, dv_ref,
    kt_ref, dka_ref, dva_ref,
):
    page_count = k_ref.shape[0]
    for page in range(page_count):
        image = pages[page]
        low, high = starts[page], starts[page + 1]
        for pair in range(pairs):
            lanes = slice(pair * LANES, (pair + 1) * LANES)
            kt_ref[pair] = flip(k_ref[image, :, lanes])
            dka_ref[pair] = jnp.zeros(dka_ref.shape[1:], jnp.float32)
            dva_ref[pair] = jnp.zeros(dva_ref.shape[1:], jnp.float32)

        def body(block, carry):
            rows = pl.ds(pl.multiple_of(block * QB, QB), QB)
            place = query_places(block)
            member = (place >= low) & (place < high)
            spans = [slice(pair * LANES, (pair + 1) * LANES) for pair in range(pairs)]
            stacked = [head_stack(q_ref[rows, lanes], 0.125) for lanes in spans]
            pulled = [head_stack(g_ref[rows, lanes]) for lanes in spans]
            stats = jnp.where(member, l_ref[0, :, rows], 1e30)
            keys_in = [k_ref[image, :, lanes] for lanes in spans]
            values_in = [v_ref[image, :, lanes] for lanes in spans]
            soft, grads, turned = pull_back(
                [dot_nt(k, q) for k, q in zip(keys_in, stacked)], values_in, pulled, stats,
                [kt_ref[pair] for pair in range(pairs)],
            )
            for pair, lanes in enumerate(spans):
                dq_ref[lanes, rows] = jnp.where(member, turned[pair], dq_ref[lanes, rows])
            for pair in range(pairs):
                dva_ref[pair] += dot_nn(soft[pair], pulled[pair])
            for pair in range(pairs):
                dka_ref[pair] += dot_nn(grads[pair], stacked[pair])
            return carry

        lax.fori_loop(low // QB, (high - 1) // QB + 1, body, 0)
        for pair in range(pairs):
            lanes = slice(pair * LANES, (pair + 1) * LANES)
            dk_ref[image, :, lanes] = dka_ref[pair].astype(jnp.bfloat16)
            dv_ref[image, :, lanes] = dva_ref[pair].astype(jnp.bfloat16)


def self_window(starts, block):
    start = starts[0]
    for page in range(1, starts.shape[0] - 1):
        start = jnp.where(starts[page] <= block * QB, starts[page], start)
    first = start // QB
    return first, block + 1 - first


def self_allowed(starts, place, first, chunks):
    begin = jnp.zeros(place.shape, jnp.int32)
    for page in range(1, starts.shape[0] - 1):
        begin = jnp.where(place >= starts[page], starts[page], begin)
    begin, end = twice(begin), twice(place)
    key = first * QB + lax.broadcasted_iota(jnp.int32, (chunks * QB, 2 * QB), 0)
    return (key >= begin) & (key <= end)


def self_forward_kernel(pairs, most, starts, q_ref, k_ref, v_ref, o_ref, l_ref, vt_ref):
    for pair in range(pairs):
        lanes = slice(pair * LANES, (pair + 1) * LANES)
        vt_ref[pair] = flip(v_ref[:, lanes])

    def body(block, carry):
        rows = pl.ds(pl.multiple_of(block * QB, QB), QB)
        first, count = self_window(starts, block)
        for chunks in range(1, most + 1):

            @pl.when(count == chunks)
            def _():
                keys = pl.ds(pl.multiple_of(first * QB, QB), chunks * QB)
                allowed = self_allowed(starts, query_places(block), first, chunks)
                spans = [slice(pair * LANES, (pair + 1) * LANES) for pair in range(pairs)]
                scores = [
                    jnp.where(
                        allowed, dot_nt(k_ref[keys, lanes], head_stack(q_ref[rows, lanes], 0.125)), -1e30
                    )
                    for lanes in spans
                ]
                mixed, stats = attend(scores, [vt_ref[pair, :, keys] for pair in range(pairs)])
                for lanes, block_out in zip(spans, mixed):
                    o_ref[lanes, rows] = block_out
                l_ref[0, :, rows] = stats

        return carry

    lax.fori_loop(0, q_ref.shape[0] // QB, body, 0)


def self_backward_kernel(
    pairs, most, starts, q_ref, k_ref, v_ref, g_ref, l_ref, dq_ref, dk_ref, dv_ref,
    kt_ref, dka_ref, dva_ref,
):
    for pair in range(pairs):
        lanes = slice(pair * LANES, (pair + 1) * LANES)
        kt_ref[pair] = flip(k_ref[:, lanes])
    dka_ref[...] = jnp.zeros(dka_ref.shape, jnp.float32)
    dva_ref[...] = jnp.zeros(dva_ref.shape, jnp.float32)

    def body(block, carry):
        rows = pl.ds(pl.multiple_of(block * QB, QB), QB)
        first, count = self_window(starts, block)
        for chunks in range(1, most + 1):

            @pl.when(count == chunks)
            def _():
                keys = pl.ds(pl.multiple_of(first * QB, QB), chunks * QB)
                allowed = self_allowed(starts, query_places(block), first, chunks)
                spans = [slice(pair * LANES, (pair + 1) * LANES) for pair in range(pairs)]
                stacked = [head_stack(q_ref[rows, lanes], 0.125) for lanes in spans]
                pulled = [head_stack(g_ref[rows, lanes]) for lanes in spans]
                scores = [
                    jnp.where(allowed, dot_nt(k_ref[keys, lanes], q), -1e30)
                    for lanes, q in zip(spans, stacked)
                ]
                soft, grads, turned = pull_back(
                    scores, [v_ref[keys, lanes] for lanes in spans], pulled, l_ref[0, :, rows],
                    [kt_ref[pair, :, keys] for pair in range(pairs)],
                )
                for pair, lanes in enumerate(spans):
                    dq_ref[lanes, rows] = turned[pair]
                for pair in range(pairs):
                    dva_ref[pair, keys, :] += dot_nn(soft[pair], pulled[pair])
                for pair in range(pairs):
                    dka_ref[pair, keys, :] += dot_nn(grads[pair], stacked[pair])

        return carry

    lax.fori_loop(0, q_ref.shape[0] // QB, body, 0)
    for pair in range(pairs):
        lanes = slice(pair * LANES, (pair + 1) * LANES)
        dk_ref[:, lanes] = dka_ref[pair].astype(jnp.bfloat16)
        dv_ref[:, lanes] = dva_ref[pair].astype(jnp.bfloat16)


def cost(flops, bytes_accessed, exps):
    return pl.CostEstimate(flops=flops, bytes_accessed=bytes_accessed, transcendentals=exps)


def specs(pairs, prefetch):
    wide = pairs * LANES

    def at(index):
        return lambda step, *scalars: index(step)

    return {
        "rows": lambda length: pl.BlockSpec((length, wide), at(lambda i: (0, i))),
        "turned": lambda length: pl.BlockSpec((wide, length), at(lambda i: (i, 0))),
        "images": lambda count, tokens: pl.BlockSpec((count, tokens, wide), at(lambda i: (0, 0, i))),
        "stats": lambda length: pl.BlockSpec((1, 2 * pairs, length), at(lambda i: (i, 0, 0))),
    }


def cross_forward(starts, pages, queries, keys_all, values_all, pairs=4):
    length, width = queries.shape
    count, tokens, _ = keys_all.shape
    steps = width // (pairs * LANES)
    s = specs(pairs, 2)
    return pl.pallas_call(
        functools.partial(cross_forward_kernel, pairs),
        out_shape=(
            jax.ShapeDtypeStruct((width, length), jnp.bfloat16),
            jax.ShapeDtypeStruct((steps, 2 * pairs, length), jnp.float32),
        ),
        grid_spec=pltpu.PrefetchScalarGridSpec(
            num_scalar_prefetch=2,
            grid=(steps,),
            in_specs=[s["rows"](length), s["images"](count, tokens), s["images"](count, tokens)],
            out_specs=[s["turned"](length), s["stats"](length)],
            scratch_shapes=[pltpu.VMEM((pairs, LANES, tokens), jnp.bfloat16)],
        ),
        cost_estimate=cost(11 * 128 * tokens * width * 4 * 4, 20 * 2**20, 2**24),
        name="cross_forward",
    )(starts, pages, queries, keys_all, values_all)


def cross_backward(starts, pages, queries, keys_all, values_all, grads, stats, pairs=4):
    length, width = queries.shape
    count, tokens, _ = keys_all.shape
    steps = width // (pairs * LANES)
    s = specs(pairs, 2)
    image_spec = s["images"](count, tokens)
    return pl.pallas_call(
        functools.partial(cross_backward_kernel, pairs),
        out_shape=(
            jax.ShapeDtypeStruct((width, length), jnp.bfloat16),
            jax.ShapeDtypeStruct(keys_all.shape, jnp.bfloat16),
            jax.ShapeDtypeStruct(values_all.shape, jnp.bfloat16),
        ),
        grid_spec=pltpu.PrefetchScalarGridSpec(
            num_scalar_prefetch=2,
            grid=(steps,),
            in_specs=[s["rows"](length), image_spec, image_spec, s["rows"](length), s["stats"](length)],
            out_specs=[s["turned"](length), image_spec, image_spec],
            scratch_shapes=[
                pltpu.VMEM((pairs, LANES, tokens), jnp.bfloat16),
                pltpu.VMEM((pairs, tokens, LANES), jnp.float32),
                pltpu.VMEM((pairs, tokens, LANES), jnp.float32),
            ],
        ),
        cost_estimate=cost(11 * 128 * tokens * width * 10 * 4, 30 * 2**20, 2**24),
        name="cross_backward",
    )(starts, pages, queries, keys_all, values_all, grads, stats)


def self_forward(starts, queries, keys_all, values_all, most, pairs=4):
    length, width = queries.shape
    steps = width // (pairs * LANES)
    s = specs(pairs, 1)
    rows = s["rows"](length)
    return pl.pallas_call(
        functools.partial(self_forward_kernel, pairs, most),
        out_shape=(
            jax.ShapeDtypeStruct((width, length), jnp.bfloat16),
            jax.ShapeDtypeStruct((steps, 2 * pairs, length), jnp.float32),
        ),
        grid_spec=pltpu.PrefetchScalarGridSpec(
            num_scalar_prefetch=1,
            grid=(steps,),
            in_specs=[rows, rows, rows],
            out_specs=[s["turned"](length), s["stats"](length)],
            scratch_shapes=[pltpu.VMEM((pairs, LANES, length), jnp.bfloat16)],
        ),
        cost_estimate=cost(20 * 128 * 128 * width * 4 * 4, 10 * 2**20, 2**23),
        name="self_forward",
    )(starts, queries, keys_all, values_all)


def self_backward(starts, queries, keys_all, values_all, grads, stats, most, pairs=4):
    length, width = queries.shape
    steps = width // (pairs * LANES)
    s = specs(pairs, 1)
    rows = s["rows"](length)
    return pl.pallas_call(
        functools.partial(self_backward_kernel, pairs, most),
        out_shape=(
            jax.ShapeDtypeStruct((width, length), jnp.bfloat16),
            jax.ShapeDtypeStruct((length, width), jnp.bfloat16),
            jax.ShapeDtypeStruct((length, width), jnp.bfloat16),
        ),
        grid_spec=pltpu.PrefetchScalarGridSpec(
            num_scalar_prefetch=1,
            grid=(steps,),
            in_specs=[rows, rows, rows, rows, s["stats"](length)],
            out_specs=[s["turned"](length), rows, rows],
            scratch_shapes=[
                pltpu.VMEM((pairs, LANES, length), jnp.bfloat16),
                pltpu.VMEM((pairs, length, LANES), jnp.float32),
                pltpu.VMEM((pairs, length, LANES), jnp.float32),
            ],
        ),
        cost_estimate=cost(20 * 128 * 128 * width * 10 * 4, 16 * 2**20, 2**23),
        name="self_backward",
    )(starts, queries, keys_all, values_all, grads, stats)


EPSILON = 1e-05
ROOT_HALF = 0.7071067811865476
ROOT_TAU = 0.3989422804014327
AXES = ("dp", "fsdp")
LONGEST = 512


def contract(a, b, left, right, out=jnp.float32):
    return lax.dot_general(
        a, b, ((left, right), ((), ())), preferred_element_type=jnp.float32
    ).astype(out)


def row_major(values):
    return with_layout_constraint(values, Layout(major_to_minor=(0, 1)))


def normalise(values):
    average = jnp.mean(values, axis=-1, keepdims=True)
    centered = values - average
    variance = jnp.mean(centered * centered, axis=-1, keepdims=True)
    scale = lax.rsqrt(variance + EPSILON)
    return centered * scale, scale


def norm_back(values, gain, grads):
    hat, scale = normalise(values)
    pulled = grads * gain
    first = jnp.mean(pulled, axis=-1, keepdims=True)
    second = jnp.mean(pulled * hat, axis=-1, keepdims=True)
    back = scale * (pulled - first - hat * second)
    return back, jnp.sum(grads * hat, axis=0), jnp.sum(grads, axis=0)


def swap(value, axis, size, bit):
    return lax.ppermute(value, axis, [(i, i ^ bit) for i in range(size)])


def butterfly_sum(value, sizes):
    for axis, size in sizes:
        bit = 1
        while bit < size:
            value = value + swap(value, axis, size, bit)
            bit *= 2
    return value


def pick(value, index, axis):
    return lax.dynamic_index_in_dim(value, index, axis, keepdims=False)


def fence(*values):
    return lax.optimization_barrier(values)


class Partial:
    def __init__(self, value, sizes, blocks=1):
        dp_size, inner = sizes
        keys, places = ["block"], {}
        for axis, size in (("dp", dp_size), ("fsdp", inner)):
            bit = size // 2
            while bit:
                keys.append((axis, bit))
                places[(axis, bit)] = (lax.axis_index(axis) // bit) % 2
                bit //= 2
        own = value.shape[0] // (blocks * dp_size * inner)
        self.sizes = {"dp": dp_size, "fsdp": inner}
        self.keys, self.places = keys, places
        bits = (2,) * (len(keys) - 1)
        self.terms = [value.reshape((blocks,) + bits + (own, value.shape[1]))]

    def total(self, terms):
        wide = [term.astype(jnp.float32) for term in terms]
        return functools.reduce(jnp.add, wide)

    def send(self, key):
        axis = self.keys.index(key)
        self.keys.remove(key)
        out = self.total([pick(term, 1 - self.places[key], axis) for term in self.terms])
        self.terms = [pick(term, self.places[key], axis) for term in self.terms]
        return swap(out.astype(jnp.bfloat16), key[0], self.sizes[key[0]], key[1])

    def take(self, received):
        self.terms.append(received)

    def rest(self):
        return self.total(self.terms).astype(jnp.bfloat16)


CORE = ("dp", 1)
ACROSS = ("dp", 2)


def scatter(parts, sizes):
    inner = sizes[1]
    rests = []
    for part in parts:
        rest = part.rest()
        blocks, (own, columns) = rest.shape[0], rest.shape[-2:]
        rest = rest.reshape(blocks, inner, own, columns).transpose(1, 0, 2, 3)
        rests.append(rest.reshape(inner, blocks * own, columns))
    packed = rests[0] if len(rests) == 1 else jnp.concatenate(rests, axis=1)
    summed = lax.psum_scatter(
        packed.reshape(-1, columns), "fsdp", scatter_dimension=0, tiled=True
    ).astype(jnp.float32)
    own = summed.shape[0] // len(parts)
    return [summed[i * own : (i + 1) * own] for i in range(len(parts))]


def layer(
    sizes, block_in, images, segment_ids, page_map, ln1_gain, ln1_shift, ln2_gain, ln2_shift,
    ln3_gain, ln3_shift, self_query, self_key, self_value, self_out, cross_query, cross_key,
    cross_value, cross_out, mlp_in, mlp_out, cotangent,
):
    dp_size, inner = sizes
    axes = (("dp", dp_size), ("fsdp", inner))
    _, length, width = block_in.shape
    low = jnp.bfloat16

    def turned(master):
        return master.astype(low).T

    def gather(*masters):
        stacked = jnp.stack([turned(m) for m in masters])
        return lax.all_gather(stacked, AXES, axis=1, tiled=True)

    norms = jnp.stack([ln1_gain, ln1_shift, ln2_gain, ln2_shift, ln3_gain, ln3_shift])
    norms = norms.astype(low).astype(jnp.float32)
    mine = norms.shape[1]
    offset = (lax.axis_index("dp") * inner + lax.axis_index("fsdp")) * mine
    spread = lax.dynamic_update_slice(jnp.zeros((6, width), jnp.float32), norms, (0, offset))
    norms = butterfly_sum(spread, axes)
    near = gather(
        self_query, self_key, self_value, self_out, cross_query, cross_key, cross_value, cross_out
    )
    w_sqkv, w_kv = near[:3], near[5:7]
    w_so, w_cq, w_ck, w_cv, w_co = [near[i] for i in range(3, 8)]
    own, devices = mlp_out.shape[1], dp_size * inner
    blocks = mlp_out.shape[0] // width
    step = width // devices
    in_rows = turned(mlp_in).reshape(blocks, step, width)
    out_rows = turned(mlp_out).reshape(own, devices, blocks, step).transpose(2, 0, 1, 3)
    far = jnp.concatenate([in_rows, out_rows.reshape(blocks, own, width)])
    far = lax.all_gather(far, AXES, axis=1, tiled=True)
    (far,) = fence(far.reshape(2, blocks * width, width))
    w_in = far[0]
    w_out = jnp.concatenate(
        [far[1, i * width : (i + 1) * width] for i in range(blocks)], axis=1
    )

    starts = jnp.sum(
        segment_ids[0][None, :] < jnp.arange(page_map.shape[1] + 1, dtype=jnp.int32)[:, None],
        axis=1,
    ).astype(jnp.int32)
    pages = page_map[0]
    most = LONGEST // QB + 1

    rows = block_in[0].astype(jnp.float32)
    a1 = (normalise(rows)[0] * norms[0] + norms[1]).astype(low)
    sq, sk, sv = [contract(a1, w_sqkv[i], (1,), (1,), low) for i in range(3)]
    so, s_stats = self_forward(starts, sq, sk, sv, most)
    x1 = row_major(rows + contract(so, w_so, (0,), (1,)))
    a2 = (normalise(x1)[0] * norms[2] + norms[3]).astype(low)
    cq = contract(a2, w_cq, (1,), (1,), low)
    ck = contract(images, w_ck, (2,), (1,), low)
    cv = contract(images, w_cv, (2,), (1,), low)
    co, c_stats = cross_forward(starts, pages, cq, ck, cv)
    x2 = row_major(x1 + contract(co, w_co, (0,), (1,)))
    a3 = (normalise(x2)[0] * norms[4] + norms[5]).astype(low)
    u = contract(a3, w_in, (1,), (1,))
    phi = 0.5 * (1.0 + lax.erf(u * ROOT_HALF))
    hidden = (u * phi).astype(low)
    slope = (phi + u * (ROOT_TAU * jnp.exp(-0.5 * u * u))).astype(low)

    eb = cotangent[0]
    e = eb.astype(jnp.float32)
    g_out = contract(eb, hidden, (0,), (0,), low)
    p_out = Partial(g_out, sizes)
    flying = p_out.send(CORE)
    eb, hidden, g_out = fence(eb, hidden, g_out)
    du = (contract(eb, w_out, (1,), (0,)) * slope.astype(jnp.float32)).astype(low)
    du, flying = fence(du, flying)
    p_out.take(flying)
    flying = p_out.send(ACROSS)
    g_in = contract(du, a3, (0,), (0,), low)
    du, g_in = fence(du, g_in)
    p_in = Partial(g_in, sizes, blocks)
    flying_in = p_in.send(CORE)
    d3 = contract(du, w_in, (1,), (0,))
    back, gg3, gs3 = norm_back(x2, norms[4], d3)
    e2 = e + back
    e2b = e2.astype(low)
    e2, e2b, flying, flying_in = fence(e2, e2b, flying, flying_in)
    p_out.take(flying)
    (g_mlp_out,) = scatter([p_out], sizes)
    p_in.take(flying_in)
    flying_in = p_in.send(ACROSS)
    d_co = contract(e2b, w_co, (1,), (0,), low)
    dcq, dck, dcv = cross_backward(starts, pages, cq, ck, cv, d_co, c_stats)
    dcq, dck, dcv, flying_in = fence(dcq, dck, dcv, flying_in)
    p_in.take(flying_in)
    (g_mlp_in,) = scatter([p_in], sizes)
    g_co = contract(e2b, co, (0,), (1,), low)
    g_cq = contract(dcq, a2, (1,), (0,), low)
    g_ck = contract(dck, images, (0, 1), (0, 1), low)
    g_cv = contract(dcv, images, (0, 1), (0, 1), low)
    dcq, g_cq, g_ck, g_cv, g_co = fence(dcq, g_cq, g_ck, g_cv, g_co)
    p_cross = [Partial(g, sizes) for g in (g_cq, g_ck, g_cv, g_co)]
    flying = [p.send(CORE) for p in p_cross]
    d2 = contract(dcq, w_cq, (0,), (0,))
    back, gg2, gs2 = norm_back(x1, norms[2], d2)
    e1 = e2 + back
    e1b = e1.astype(low)
    e1, e1b, *flying = fence(e1, e1b, *flying)
    for p, f in zip(p_cross, flying):
        p.take(f)
    flying = [p.send(ACROSS) for p in p_cross]
    g_so = contract(e1b, so, (0,), (1,), low)
    p_so = Partial(g_so, sizes)
    flying_so = p_so.send(CORE)
    d_so = contract(e1b, w_so, (1,), (0,), low)
    dsq, dsk, dsv = self_backward(starts, sq, sk, sv, d_so, s_stats, most)
    dsq, dsk, dsv, flying_so, *flying = fence(dsq, dsk, dsv, flying_so, *flying)
    for p, f in zip(p_cross, flying):
        p.take(f)
    g_cross = scatter(p_cross, sizes)
    orders = []
    keys = [ACROSS] + [("fsdp", 1 << i) for i in range(inner.bit_length() - 1)]
    for shift in range(3):
        orders.append(keys[shift:] + keys[:shift])
    p_so.take(flying_so)
    flying_so = p_so.send(keys[0])
    g_sq = contract(dsq, a1, (1,), (0,), low)
    g_sk = contract(dsk, a1, (0,), (0,), low)
    g_sv = contract(dsv, a1, (0,), (0,), low)
    dsq, dsk, dsv, g_sq, g_sk, g_sv, flying_so = fence(dsq, dsk, dsv, g_sq, g_sk, g_sv, flying_so)
    p_so.take(flying_so)
    p_self = [Partial(g, sizes) for g in (g_sq, g_sk, g_sv)]
    flying = [p.send(CORE) for p in p_self]
    flying_so = p_so.send(keys[1])
    d1 = (
        contract(dsq, w_sqkv[0], (0,), (0,))
        + contract(dsk, w_sqkv[1], (1,), (0,))
        + contract(dsv, w_sqkv[2], (1,), (0,))
    )

    def norm_one(d1):
        back, gg1, gs1 = norm_back(rows, norms[0], d1)
        return e1 + back, gg1, gs1

    def image_grads(dck, dcv):
        both = jnp.concatenate([dck, dcv], axis=2).transpose(1, 0, 2)
        tokens, count, _ = both.shape
        flat = contract(
            both.reshape(tokens * count, 2 * width), w_kv.reshape(2 * width, width), (1,), (0,)
        )
        return flat.reshape(tokens, count, width).transpose(1, 0, 2)

    def finish(hidden):
        return (x2 + contract(hidden, w_out, (1,), (1,))).astype(low)

    fillers = [(norm_one, (d1,)), (finish, (hidden,)), (image_grads, (dck, dcv))]
    results = []
    waits = (d1,)
    parts = p_self + [p_so]
    flights = flying + [flying_so]
    for stage in range(len(keys)):
        if stage < 3:
            job, needs = fillers[stage]
            fenced = fence(*(flights + list(waits) + list(needs)))
            needs = fenced[-len(needs) :]
        else:
            fenced = fence(*(flights + list(waits)))
        for p, f in zip(parts, fenced):
            p.take(f)
        parts = [p for p in parts if len(p.keys) > 1]
        flights = [p.send(o[stage]) for p, o in zip(p_self, orders)]
        if len(p_so.keys) > 1:
            flights.append(p_so.send(keys[stage + 2]))
        if stage < 3:
            done = job(*needs)
            waits = jax.tree.leaves(done)[:1]
            results.append(done)
    for p, f in zip(parts, flights):
        p.take(f)
    grad_in, gg1, gs1 = results[0]
    block_out, grad_images = results[1], results[2]
    g_self = [p.total(p.terms)[0] for p in p_self + [p_so]]
    norm_grads = butterfly_sum(jnp.stack([gg1, gs1, gg2, gs2, gg3, gs3]), axes)
    norm_grads = lax.dynamic_slice(norm_grads, (0, offset), (6, mine))
    g_mlp_out = g_mlp_out.reshape(own, blocks, devices, step).transpose(0, 2, 1, 3)
    g_mlp_out = g_mlp_out.reshape(own, -1)
    weight_grads = [g.T for g in g_self + g_cross + [g_mlp_in, g_mlp_out]]
    return (
        block_out[None], grad_in[None], grad_images, *[norm_grads[i] for i in range(6)],
        *weight_grads,
    )


def solution(mesh):
    sizes = (mesh.shape["dp"], mesh.shape["fsdp"])
    rows3 = P(AXES, None, None)
    rows2 = P(AXES, None)
    vector = P(AXES)
    columns = P(None, AXES)
    return jax.shard_map(
        functools.partial(layer, sizes),
        mesh=mesh,
        in_specs=(rows3, rows3, rows2, rows2) + (vector,) * 6 + (columns,) * 10 + (rows3,),
        out_specs=(rows3,) * 3 + (vector,) * 6 + (columns,) * 10,
        check_vma=False,
    )
```

```python
import functools
import jax
import jax.numpy as jnp
from jax import lax
from jax.experimental import pallas as pl
from jax.experimental.layout import Layout, with_layout_constraint
from jax.experimental.pallas import tpu as pltpu
from jax.sharding import PartitionSpec as P

LANES = 128
HALF = 64
QB = 128


def dot_nt(a, b):
    return lax.dot_general(a, b, (((1,), (1,)), ((), ())), preferred_element_type=jnp.float32)


def dot_nn(a, b):
    return lax.dot_general(a, b, (((1,), (0,)), ((), ())), preferred_element_type=jnp.float32)


def head_stack(block, scale=None):
    lane = lax.broadcasted_iota(jnp.int32, block.shape, 1)
    wide = block.astype(jnp.float32)
    if scale is not None:
        wide = wide * scale
    first = jnp.where(lane < HALF, wide, 0.0).astype(jnp.bfloat16)
    second = jnp.where(lane < HALF, 0.0, wide).astype(jnp.bfloat16)
    return jnp.concatenate([first, second], axis=0)


def twice(row):
    return jnp.concatenate([row, row], axis=1)


def diagonal(pair):
    return jnp.concatenate([pair[:HALF, :QB], pair[HALF:, QB:]], axis=0)


def attend(scores, values_turned):
    peaks = [jnp.max(s, axis=0, keepdims=True) for s in scores]
    raised = [jnp.exp(s - peak) for s, peak in zip(scores, peaks)]
    totals = [jnp.sum(r, axis=0, keepdims=True) for r in raised]
    low = [(r * (1.0 / total)).astype(jnp.bfloat16) for r, total in zip(raised, totals)]
    mixed = [diagonal(dot_nn(vt, p)).astype(jnp.bfloat16) for vt, p in zip(values_turned, low)]
    stats = []
    for peak, total in zip(peaks, totals):
        lse = peak + jnp.log(total)
        stats += [lse[:, :QB], lse[:, QB:]]
    return mixed, jnp.concatenate(stats, axis=0)


def pull_back(scores, values_in, pulled, stats, keys_turned):
    attention = [
        jnp.exp(s - jnp.concatenate([stats[2 * i : 2 * i + 1], stats[2 * i + 1 : 2 * i + 2]], axis=1))
        for i, s in enumerate(scores)
    ]
    low = [a.astype(jnp.bfloat16) for a in attention]
    pushed = [dot_nt(v, g) for v, g in zip(values_in, pulled)]
    inner = [jnp.sum(a * p, axis=0, keepdims=True) for a, p in zip(attention, pushed)]
    grads = [
        (a * (p - i)).astype(jnp.bfloat16) for a, p, i in zip(attention, pushed, inner)
    ]
    turned = [
        diagonal(dot_nn(kt, g) * 0.125).astype(jnp.bfloat16) for kt, g in zip(keys_turned, grads)
    ]
    return low, grads, turned


def query_places(block):
    return block * QB + lax.broadcasted_iota(jnp.int32, (1, QB), 1)


def cross_forward_kernel(pairs, starts, pages, q_ref, k_ref, v_ref, o_ref, l_ref, vt_ref):
    page_count = k_ref.shape[0]
    for page in range(page_count):
        image = pages[page]
        low, high = starts[page], starts[page + 1]
        for pair in range(pairs):
            lanes = slice(pair * LANES, (pair + 1) * LANES)
            vt_ref[pair] = flip(v_ref[image, :, lanes])

        def body(block, carry):
            rows = pl.ds(pl.multiple_of(block * QB, QB), QB)
            place = query_places(block)
            member = (place >= low) & (place < high)
            spans = [slice(pair * LANES, (pair + 1) * LANES) for pair in range(pairs)]
            scores = [
                dot_nt(k_ref[image, :, lanes], head_stack(q_ref[rows, lanes], 0.125))
                for lanes in spans
            ]
            mixed, stats = attend(scores, [vt_ref[pair] for pair in range(pairs)])
            for lanes, block_out in zip(spans, mixed):
                o_ref[lanes, rows] = jnp.where(member, block_out, o_ref[lanes, rows])
            l_ref[0, :, rows] = jnp.where(member, stats, l_ref[0, :, rows])
            return carry

        lax.fori_loop(low // QB, (high - 1) // QB + 1, body, 0)


def flip(block):
    return jnp.transpose(block)


def cross_backward_kernel(
    pairs, starts, pages, q_ref, k_ref, v_ref, g_ref, l_ref, dq_ref, dk_ref, dv_ref,
    kt_ref, dka_ref, dva_ref,
):
    page_count = k_ref.shape[0]
    for page in range(page_count):
        image = pages[page]
        low, high = starts[page], starts[page + 1]
        for pair in range(pairs):
            lanes = slice(pair * LANES, (pair + 1) * LANES)
            kt_ref[pair] = flip(k_ref[image, :, lanes])
            dka_ref[pair] = jnp.zeros(dka_ref.shape[1:], jnp.float32)
            dva_ref[pair] = jnp.zeros(dva_ref.shape[1:], jnp.float32)

        def body(block, carry):
            rows = pl.ds(pl.multiple_of(block * QB, QB), QB)
            place = query_places(block)
            member = (place >= low) & (place < high)
            spans = [slice(pair * LANES, (pair + 1) * LANES) for pair in range(pairs)]
            stacked = [head_stack(q_ref[rows, lanes], 0.125) for lanes in spans]
            pulled = [head_stack(g_ref[rows, lanes]) for lanes in spans]
            stats = jnp.where(member, l_ref[0, :, rows], 1e30)
            keys_in = [k_ref[image, :, lanes] for lanes in spans]
            values_in = [v_ref[image, :, lanes] for lanes in spans]
            soft, grads, turned = pull_back(
                [dot_nt(k, q) for k, q in zip(keys_in, stacked)], values_in, pulled, stats,
                [kt_ref[pair] for pair in range(pairs)],
            )
            for pair, lanes in enumerate(spans):
                dq_ref[lanes, rows] = jnp.where(member, turned[pair], dq_ref[lanes, rows])
            for pair in range(pairs):
                dva_ref[pair] += dot_nn(soft[pair], pulled[pair])
            for pair in range(pairs):
                dka_ref[pair] += dot_nn(grads[pair], stacked[pair])
            return carry

        lax.fori_loop(low // QB, (high - 1) // QB + 1, body, 0)
        for pair in range(pairs):
            lanes = slice(pair * LANES, (pair + 1) * LANES)
            dk_ref[image, :, lanes] = dka_ref[pair].astype(jnp.bfloat16)
            dv_ref[image, :, lanes] = dva_ref[pair].astype(jnp.bfloat16)


def self_window(starts, block):
    start = starts[0]
    for page in range(1, starts.shape[0] - 1):
        start = jnp.where(starts[page] <= block * QB, starts[page], start)
    first = start // QB
    return first, block + 1 - first


def self_allowed(starts, place, first, chunks):
    begin = jnp.zeros(place.shape, jnp.int32)
    for page in range(1, starts.shape[0] - 1):
        begin = jnp.where(place >= starts[page], starts[page], begin)
    begin, end = twice(begin), twice(place)
    key = first * QB + lax.broadcasted_iota(jnp.int32, (chunks * QB, 2 * QB), 0)
    return (key >= begin) & (key <= end)


def self_forward_kernel(pairs, most, starts, q_ref, k_ref, v_ref, o_ref, l_ref, vt_ref):
    for pair in range(pairs):
        lanes = slice(pair * LANES, (pair + 1) * LANES)
        vt_ref[pair] = flip(v_ref[:, lanes])

    def body(block, carry):
        rows = pl.ds(pl.multiple_of(block * QB, QB), QB)
        first, count = self_window(starts, block)
        for chunks in range(1, most + 1):

            @pl.when(count == chunks)
            def _():
                keys = pl.ds(pl.multiple_of(first * QB, QB), chunks * QB)
                allowed = self_allowed(starts, query_places(block), first, chunks)
                spans = [slice(pair * LANES, (pair + 1) * LANES) for pair in range(pairs)]
                scores = [
                    jnp.where(
                        allowed, dot_nt(k_ref[keys, lanes], head_stack(q_ref[rows, lanes], 0.125)), -1e30
                    )
                    for lanes in spans
                ]
                mixed, stats = attend(scores, [vt_ref[pair, :, keys] for pair in range(pairs)])
                for lanes, block_out in zip(spans, mixed):
                    o_ref[lanes, rows] = block_out
                l_ref[0, :, rows] = stats

        return carry

    lax.fori_loop(0, q_ref.shape[0] // QB, body, 0)


def self_backward_kernel(
    pairs, most, starts, q_ref, k_ref, v_ref, g_ref, l_ref, dq_ref, dk_ref, dv_ref,
    kt_ref, dka_ref, dva_ref,
):
    for pair in range(pairs):
        lanes = slice(pair * LANES, (pair + 1) * LANES)
        kt_ref[pair] = flip(k_ref[:, lanes])
    dka_ref[...] = jnp.zeros(dka_ref.shape, jnp.float32)
    dva_ref[...] = jnp.zeros(dva_ref.shape, jnp.float32)

    def body(block, carry):
        rows = pl.ds(pl.multiple_of(block * QB, QB), QB)
        first, count = self_window(starts, block)
        for chunks in range(1, most + 1):

            @pl.when(count == chunks)
            def _():
                keys = pl.ds(pl.multiple_of(first * QB, QB), chunks * QB)
                allowed = self_allowed(starts, query_places(block), first, chunks)
                spans = [slice(pair * LANES, (pair + 1) * LANES) for pair in range(pairs)]
                stacked = [head_stack(q_ref[rows, lanes], 0.125) for lanes in spans]
                pulled = [head_stack(g_ref[rows, lanes]) for lanes in spans]
                scores = [
                    jnp.where(allowed, dot_nt(k_ref[keys, lanes], q), -1e30)
                    for lanes, q in zip(spans, stacked)
                ]
                soft, grads, turned = pull_back(
                    scores, [v_ref[keys, lanes] for lanes in spans], pulled, l_ref[0, :, rows],
                    [kt_ref[pair, :, keys] for pair in range(pairs)],
                )
                for pair, lanes in enumerate(spans):
                    dq_ref[lanes, rows] = turned[pair]
                for pair in range(pairs):
                    dva_ref[pair, keys, :] += dot_nn(soft[pair], pulled[pair])
                for pair in range(pairs):
                    dka_ref[pair, keys, :] += dot_nn(grads[pair], stacked[pair])

        return carry

    lax.fori_loop(0, q_ref.shape[0] // QB, body, 0)
    for pair in range(pairs):
        lanes = slice(pair * LANES, (pair + 1) * LANES)
        dk_ref[:, lanes] = dka_ref[pair].astype(jnp.bfloat16)
        dv_ref[:, lanes] = dva_ref[pair].astype(jnp.bfloat16)


def cost(flops, bytes_accessed, exps):
    return pl.CostEstimate(flops=flops, bytes_accessed=bytes_accessed, transcendentals=exps)


def specs(pairs, prefetch):
    wide = pairs * LANES

    def at(index):
        return lambda step, *scalars: index(step)

    return {
        "rows": lambda length: pl.BlockSpec((length, wide), at(lambda i: (0, i))),
        "turned": lambda length: pl.BlockSpec((wide, length), at(lambda i: (i, 0))),
        "images": lambda count, tokens: pl.BlockSpec((count, tokens, wide), at(lambda i: (0, 0, i))),
        "stats": lambda length: pl.BlockSpec((1, 2 * pairs, length), at(lambda i: (i, 0, 0))),
    }


def cross_forward(starts, pages, queries, keys_all, values_all, pairs=4):
    length, width = queries.shape
    count, tokens, _ = keys_all.shape
    steps = width // (pairs * LANES)
    s = specs(pairs, 2)
    return pl.pallas_call(
        functools.partial(cross_forward_kernel, pairs),
        out_shape=(
            jax.ShapeDtypeStruct((width, length), jnp.bfloat16),
            jax.ShapeDtypeStruct((steps, 2 * pairs, length), jnp.float32),
        ),
        grid_spec=pltpu.PrefetchScalarGridSpec(
            num_scalar_prefetch=2,
            grid=(steps,),
            in_specs=[s["rows"](length), s["images"](count, tokens), s["images"](count, tokens)],
            out_specs=[s["turned"](length), s["stats"](length)],
            scratch_shapes=[pltpu.VMEM((pairs, LANES, tokens), jnp.bfloat16)],
        ),
        cost_estimate=cost(11 * 128 * tokens * width * 4 * 4, 20 * 2**20, 2**24),
        name="cross_forward",
    )(starts, pages, queries, keys_all, values_all)


def cross_backward(starts, pages, queries, keys_all, values_all, grads, stats, pairs=4):
    length, width = queries.shape
    count, tokens, _ = keys_all.shape
    steps = width // (pairs * LANES)
    s = specs(pairs, 2)
    image_spec = s["images"](count, tokens)
    return pl.pallas_call(
        functools.partial(cross_backward_kernel, pairs),
        out_shape=(
            jax.ShapeDtypeStruct((width, length), jnp.bfloat16),
            jax.ShapeDtypeStruct(keys_all.shape, jnp.bfloat16),
            jax.ShapeDtypeStruct(values_all.shape, jnp.bfloat16),
        ),
        grid_spec=pltpu.PrefetchScalarGridSpec(
            num_scalar_prefetch=2,
            grid=(steps,),
            in_specs=[s["rows"](length), image_spec, image_spec, s["rows"](length), s["stats"](length)],
            out_specs=[s["turned"](length), image_spec, image_spec],
            scratch_shapes=[
                pltpu.VMEM((pairs, LANES, tokens), jnp.bfloat16),
                pltpu.VMEM((pairs, tokens, LANES), jnp.float32),
                pltpu.VMEM((pairs, tokens, LANES), jnp.float32),
            ],
        ),
        cost_estimate=cost(11 * 128 * tokens * width * 10 * 4, 30 * 2**20, 2**24),
        name="cross_backward",
    )(starts, pages, queries, keys_all, values_all, grads, stats)


def self_forward(starts, queries, keys_all, values_all, most, pairs=4):
    length, width = queries.shape
    steps = width // (pairs * LANES)
    s = specs(pairs, 1)
    rows = s["rows"](length)
    return pl.pallas_call(
        functools.partial(self_forward_kernel, pairs, most),
        out_shape=(
            jax.ShapeDtypeStruct((width, length), jnp.bfloat16),
            jax.ShapeDtypeStruct((steps, 2 * pairs, length), jnp.float32),
        ),
        grid_spec=pltpu.PrefetchScalarGridSpec(
            num_scalar_prefetch=1,
            grid=(steps,),
            in_specs=[rows, rows, rows],
            out_specs=[s["turned"](length), s["stats"](length)],
            scratch_shapes=[pltpu.VMEM((pairs, LANES, length), jnp.bfloat16)],
        ),
        cost_estimate=cost(20 * 128 * 128 * width * 4 * 4, 10 * 2**20, 2**23),
        name="self_forward",
    )(starts, queries, keys_all, values_all)


def self_backward(starts, queries, keys_all, values_all, grads, stats, most, pairs=4):
    length, width = queries.shape
    steps = width // (pairs * LANES)
    s = specs(pairs, 1)
    rows = s["rows"](length)
    return pl.pallas_call(
        functools.partial(self_backward_kernel, pairs, most),
        out_shape=(
            jax.ShapeDtypeStruct((width, length), jnp.bfloat16),
            jax.ShapeDtypeStruct((length, width), jnp.bfloat16),
            jax.ShapeDtypeStruct((length, width), jnp.bfloat16),
        ),
        grid_spec=pltpu.PrefetchScalarGridSpec(
            num_scalar_prefetch=1,
            grid=(steps,),
            in_specs=[rows, rows, rows, rows, s["stats"](length)],
            out_specs=[s["turned"](length), rows, rows],
            scratch_shapes=[
                pltpu.VMEM((pairs, LANES, length), jnp.bfloat16),
                pltpu.VMEM((pairs, length, LANES), jnp.float32),
                pltpu.VMEM((pairs, length, LANES), jnp.float32),
            ],
        ),
        cost_estimate=cost(20 * 128 * 128 * width * 10 * 4, 16 * 2**20, 2**23),
        name="self_backward",
    )(starts, queries, keys_all, values_all, grads, stats)


EPSILON = 1e-05
ROOT_HALF = 0.7071067811865476
ROOT_TAU = 0.3989422804014327
AXES = ("dp", "fsdp")
LONGEST = 512


def contract(a, b, left, right, out=jnp.float32):
    return lax.dot_general(
        a, b, ((left, right), ((), ())), preferred_element_type=jnp.float32
    ).astype(out)


def row_major(values):
    return with_layout_constraint(values, Layout(major_to_minor=(0, 1)))


def normalise(values):
    average = jnp.mean(values, axis=-1, keepdims=True)
    centered = values - average
    variance = jnp.mean(centered * centered, axis=-1, keepdims=True)
    scale = lax.rsqrt(variance + EPSILON)
    return centered * scale, scale


def norm_back(values, gain, grads):
    hat, scale = normalise(values)
    pulled = grads * gain
    first = jnp.mean(pulled, axis=-1, keepdims=True)
    second = jnp.mean(pulled * hat, axis=-1, keepdims=True)
    back = scale * (pulled - first - hat * second)
    return back, jnp.sum(grads * hat, axis=0), jnp.sum(grads, axis=0)


def swap(value, axis, size, bit):
    return lax.ppermute(value, axis, [(i, i ^ bit) for i in range(size)])


def butterfly_sum(value, sizes):
    for axis, size in sizes:
        bit = 1
        while bit < size:
            value = value + swap(value, axis, size, bit)
            bit *= 2
    return value


def pick(value, index, axis):
    return lax.dynamic_index_in_dim(value, index, axis, keepdims=False)


def fence(*values):
    return lax.optimization_barrier(values)


class Partial:
    def __init__(self, value, sizes):
        dp_size, inner = sizes
        keys, places = [], {}
        for axis, size in (("dp", dp_size), ("fsdp", inner)):
            bit = size // 2
            while bit:
                keys.append((axis, bit))
                places[(axis, bit)] = (lax.axis_index(axis) // bit) % 2
                bit //= 2
        own = value.shape[0] // (dp_size * inner)
        self.sizes = {"dp": dp_size, "fsdp": inner}
        self.keys, self.places = keys, places
        self.terms = [value.reshape((2,) * len(keys) + (own, value.shape[1]))]

    def total(self, terms):
        wide = [term.astype(jnp.float32) for term in terms]
        return functools.reduce(jnp.add, wide)

    def send(self, key):
        axis = self.keys.index(key)
        self.keys.remove(key)
        out = self.total([pick(term, 1 - self.places[key], axis) for term in self.terms])
        self.terms = [pick(term, self.places[key], axis) for term in self.terms]
        return swap(out.astype(jnp.bfloat16), key[0], self.sizes[key[0]], key[1])

    def take(self, received):
        self.terms.append(received)

    def rest(self):
        return self.total(self.terms).astype(jnp.bfloat16)


class Spread:
    def __init__(self, value, sizes):
        dp_size, inner = sizes
        self.sizes = {"dp": dp_size, "fsdp": inner}
        self.ranks = {}
        for axis, size in (("dp", dp_size), ("fsdp", inner)):
            bit = size // 2
            while bit:
                self.ranks[(axis, bit)] = len(self.ranks)
                bit //= 2
        self.held, self.value = [], value

    def send(self, key):
        self.key = key
        return swap(self.value, key[0], self.sizes[key[0]], key[1])

    def take(self, received):
        axis, bit = self.key
        upper = (lax.axis_index(axis) // bit) % 2 == 1
        self.held.append(self.ranks[self.key])
        self.held.sort()
        place = self.held.index(self.ranks[self.key])
        pair = (self.value, received)
        both = jnp.where(upper, jnp.stack(pair[::-1], place), jnp.stack(pair, place))
        order = tuple(range(both.ndim))
        (self.value,) = fence(with_layout_constraint(both, Layout(major_to_minor=order)))

    def rows(self):
        return self.value.reshape(-1, self.value.shape[-1])


CORE = ("dp", 1)
ACROSS = ("dp", 2)


def scatter(parts, sizes):
    inner = sizes[1]
    rests = []
    for part in parts:
        rest = part.rest()
        own, columns = rest.shape[-2:]
        rests.append(rest.reshape(inner, own, columns))
    packed = rests[0] if len(rests) == 1 else jnp.concatenate(rests, axis=1)
    summed = lax.psum_scatter(
        packed.reshape(-1, columns), "fsdp", scatter_dimension=0, tiled=True
    ).astype(jnp.float32)
    return [summed[i * own : (i + 1) * own] for i in range(len(parts))]


def layer(
    sizes, block_in, images, segment_ids, page_map, ln1_gain, ln1_shift, ln2_gain, ln2_shift,
    ln3_gain, ln3_shift, self_query, self_key, self_value, self_out, cross_query, cross_key,
    cross_value, cross_out, mlp_in, mlp_out, cotangent,
):
    dp_size, inner = sizes
    axes = (("dp", dp_size), ("fsdp", inner))
    _, length, width = block_in.shape
    low = jnp.bfloat16

    def turned(master):
        return master.astype(low).T

    def gather(*masters):
        stacked = jnp.stack([turned(m) for m in masters])
        return lax.all_gather(stacked, AXES, axis=1, tiled=True)

    norms = jnp.stack([ln1_gain, ln1_shift, ln2_gain, ln2_shift, ln3_gain, ln3_shift])
    norms = norms.astype(low).astype(jnp.float32)
    mine = norms.shape[1]
    offset = (lax.axis_index("dp") * inner + lax.axis_index("fsdp")) * mine
    spread = lax.dynamic_update_slice(jnp.zeros((6, width), jnp.float32), norms, (0, offset))
    norms = butterfly_sum(spread, axes)
    near = gather(self_out, cross_query, cross_key, cross_value, cross_out)
    w_so, w_cq, w_ck, w_cv, w_co = [near[i] for i in range(5)]
    w_kv = near[2:4]
    w_in = lax.all_gather(row_major(turned(mlp_in)), AXES, axis=0, tiled=True)
    keys = [("fsdp", 1 << i) for i in reversed(range(inner.bit_length() - 1))] + [ACROSS]
    orders = [keys[:1] + keys[1 + i :] + keys[1 : 1 + i] for i in range(3)]
    whole = [Spread(turned(m), sizes) for m in (self_query, self_key, self_value)]
    spread_out = Spread(turned(mlp_out), sizes)
    for stage in range(len(keys) + 1):
        flights = [w.send(o[stage] if stage < len(keys) else CORE) for w, o in zip(whole, orders)]
        if stage + 1 < len(keys):
            flights.append(spread_out.send(keys[stage]))
        if stage + 1 == len(keys):
            flying_w = spread_out.send(ACROSS)
        flights = fence(*flights)
        for w, f in zip(whole + [spread_out], flights):
            w.take(f)
    w_sqkv = [w.rows() for w in whole]

    starts = jnp.sum(
        segment_ids[0][None, :] < jnp.arange(page_map.shape[1] + 1, dtype=jnp.int32)[:, None],
        axis=1,
    ).astype(jnp.int32)
    pages = page_map[0]
    most = LONGEST // QB + 1

    rows = block_in[0].astype(jnp.float32)
    a1 = (normalise(rows)[0] * norms[0] + norms[1]).astype(low)
    sq, sk, sv = [contract(a1, w_sqkv[i], (1,), (1,), low) for i in range(3)]
    so, s_stats = self_forward(starts, sq, sk, sv, most)
    x1 = row_major(rows + contract(so, w_so, (0,), (1,)))
    a2 = (normalise(x1)[0] * norms[2] + norms[3]).astype(low)
    cq = contract(a2, w_cq, (1,), (1,), low)
    ck = contract(images, w_ck, (2,), (1,), low)
    cv = contract(images, w_cv, (2,), (1,), low)
    cq, ck, cv, flying_w = fence(cq, ck, cv, flying_w)
    spread_out.take(flying_w)
    flying_w = spread_out.send(CORE)
    co, c_stats = cross_forward(starts, pages, cq, ck, cv)
    co, c_stats, flying_w = fence(co, c_stats, flying_w)
    spread_out.take(flying_w)
    w_out = spread_out.rows()
    x2 = row_major(x1 + contract(co, w_co, (0,), (1,)))
    a3 = (normalise(x2)[0] * norms[4] + norms[5]).astype(low)
    u = contract(a3, w_in, (1,), (1,))
    phi = 0.5 * (1.0 + lax.erf(u * ROOT_HALF))
    hidden = (u * phi).astype(low)
    slope = (phi + u * (ROOT_TAU * jnp.exp(-0.5 * u * u))).astype(low)

    eb = cotangent[0]
    e = eb.astype(jnp.float32)
    g_out = contract(eb, hidden, (0,), (0,), low)
    p_out = Partial(g_out, sizes)
    flying = p_out.send(CORE)
    eb, hidden, g_out = fence(eb, hidden, g_out)
    du = (contract(eb, w_out, (1,), (0,)) * slope.astype(jnp.float32)).astype(low)
    du, flying = fence(du, flying)
    p_out.take(flying)
    flying = p_out.send(ACROSS)
    g_in = contract(du, a3, (0,), (0,), low)
    du, g_in = fence(du, g_in)
    p_in = Partial(g_in, sizes)
    flying_in = p_in.send(CORE)
    d3 = contract(du, w_in, (1,), (0,))
    back, gg3, gs3 = norm_back(x2, norms[4], d3)
    e2 = e + back
    e2b = e2.astype(low)
    e2, e2b, flying_in = fence(e2, e2b, flying_in)
    p_in.take(flying_in)
    flying_in = p_in.send(ACROSS)
    d_co = contract(e2b, w_co, (1,), (0,), low)
    dcq, dck, dcv = cross_backward(starts, pages, cq, ck, cv, d_co, c_stats)
    dcq, dck, dcv, flying, flying_in = fence(dcq, dck, dcv, flying, flying_in)
    p_out.take(flying)
    (g_mlp_out,) = scatter([p_out], sizes)
    p_in.take(flying_in)
    (g_mlp_in,) = scatter([p_in], sizes)
    g_co = contract(e2b, co, (0,), (1,), low)
    g_cq = contract(dcq, a2, (1,), (0,), low)
    g_ck = contract(dck, images, (0, 1), (0, 1), low)
    g_cv = contract(dcv, images, (0, 1), (0, 1), low)
    dcq, g_cq, g_ck, g_cv, g_co = fence(dcq, g_cq, g_ck, g_cv, g_co)
    p_cross = [Partial(g, sizes) for g in (g_cq, g_ck, g_cv, g_co)]
    flying = [p.send(CORE) for p in p_cross]
    d2 = contract(dcq, w_cq, (0,), (0,))
    back, gg2, gs2 = norm_back(x1, norms[2], d2)
    e1 = e2 + back
    e1b = e1.astype(low)
    e1, e1b, *flying = fence(e1, e1b, *flying)
    for p, f in zip(p_cross, flying):
        p.take(f)
    flying = [p.send(ACROSS) for p in p_cross]
    g_so = contract(e1b, so, (0,), (1,), low)
    p_so = Partial(g_so, sizes)
    flying_so = p_so.send(CORE)
    d_so = contract(e1b, w_so, (1,), (0,), low)
    dsq, dsk, dsv = self_backward(starts, sq, sk, sv, d_so, s_stats, most)
    dsq, dsk, dsv, flying_so, *flying = fence(dsq, dsk, dsv, flying_so, *flying)
    for p, f in zip(p_cross, flying):
        p.take(f)
    g_cross = scatter(p_cross, sizes)
    orders = []
    keys = [ACROSS] + [("fsdp", 1 << i) for i in range(inner.bit_length() - 1)]
    for shift in range(3):
        orders.append(keys[shift:] + keys[:shift])
    p_so.take(flying_so)
    flying_so = p_so.send(keys[0])
    g_sq = contract(dsq, a1, (1,), (0,), low)
    g_sk = contract(dsk, a1, (0,), (0,), low)
    g_sv = contract(dsv, a1, (0,), (0,), low)
    dsq, dsk, dsv, g_sq, g_sk, g_sv, flying_so = fence(dsq, dsk, dsv, g_sq, g_sk, g_sv, flying_so)
    p_so.take(flying_so)
    p_self = [Partial(g, sizes) for g in (g_sq, g_sk, g_sv)]
    flying = [p.send(CORE) for p in p_self]
    flying_so = p_so.send(keys[1])
    d1 = (
        contract(dsq, w_sqkv[0], (0,), (0,))
        + contract(dsk, w_sqkv[1], (1,), (0,))
        + contract(dsv, w_sqkv[2], (1,), (0,))
    )

    def norm_one(d1):
        back, gg1, gs1 = norm_back(rows, norms[0], d1)
        return e1 + back, gg1, gs1

    def image_grads(dck, dcv):
        both = jnp.concatenate([dck, dcv], axis=2).transpose(1, 0, 2)
        tokens, count, _ = both.shape
        flat = contract(
            both.reshape(tokens * count, 2 * width), w_kv.reshape(2 * width, width), (1,), (0,)
        )
        return flat.reshape(tokens, count, width).transpose(1, 0, 2)

    def finish(hidden):
        return (x2 + contract(hidden, w_out, (1,), (1,))).astype(low)

    fillers = [(norm_one, (d1,)), (finish, (hidden,)), (image_grads, (dck, dcv))]
    results = []
    waits = (d1,)
    parts = p_self + [p_so]
    flights = flying + [flying_so]
    for stage in range(len(keys)):
        if stage < 3:
            job, needs = fillers[stage]
            fenced = fence(*(flights + list(waits) + list(needs)))
            needs = fenced[-len(needs) :]
        else:
            fenced = fence(*(flights + list(waits)))
        for p, f in zip(parts, fenced):
            p.take(f)
        parts = [p for p in parts if len(p.keys)]
        flights = [p.send(o[stage]) for p, o in zip(p_self, orders)]
        if len(p_so.keys):
            flights.append(p_so.send(p_so.keys[-1] if len(p_so.keys) == 1 else keys[stage + 2]))
        if stage < 3:
            done = job(*needs)
            waits = jax.tree.leaves(done)[:1]
            results.append(done)
    for p, f in zip(parts, flights):
        p.take(f)
    grad_in, gg1, gs1 = results[0]
    block_out, grad_images = results[1], results[2]
    g_self = [p.total(p.terms) for p in p_self + [p_so]]
    norm_grads = butterfly_sum(jnp.stack([gg1, gs1, gg2, gs2, gg3, gs3]), axes)
    norm_grads = lax.dynamic_slice(norm_grads, (0, offset), (6, mine))
    weight_grads = [g.T for g in g_self + g_cross + [g_mlp_in, g_mlp_out]]
    return (
        block_out[None], grad_in[None], grad_images, *[norm_grads[i] for i in range(6)],
        *weight_grads,
    )


def solution(mesh):
    sizes = (mesh.shape["dp"], mesh.shape["fsdp"])
    rows3 = P(AXES, None, None)
    rows2 = P(AXES, None)
    vector = P(AXES)
    columns = P(None, AXES)
    return jax.shard_map(
        functools.partial(layer, sizes),
        mesh=mesh,
        in_specs=(rows3, rows3, rows2, rows2) + (vector,) * 6 + (columns,) * 10 + (rows3,),
        out_specs=(rows3,) * 3 + (vector,) * 6 + (columns,) * 10,
        check_vma=False,
    )
```

```python
import functools
import jax
import jax.numpy as jnp
from jax import lax
from jax.experimental import pallas as pl
from jax.experimental.layout import Layout, with_layout_constraint
from jax.experimental.pallas import tpu as pltpu
from jax.sharding import PartitionSpec as P

LANES = 128
HALF = 64
QB = 128


def dot_nt(a, b):
    return lax.dot_general(a, b, (((1,), (1,)), ((), ())), preferred_element_type=jnp.float32)


def dot_nn(a, b):
    return lax.dot_general(a, b, (((1,), (0,)), ((), ())), preferred_element_type=jnp.float32)


def head_stack(block, scale=None):
    lane = lax.broadcasted_iota(jnp.int32, block.shape, 1)
    wide = block.astype(jnp.float32)
    if scale is not None:
        wide = wide * scale
    first = jnp.where(lane < HALF, wide, 0.0).astype(jnp.bfloat16)
    second = jnp.where(lane < HALF, 0.0, wide).astype(jnp.bfloat16)
    return jnp.concatenate([first, second], axis=0)


def twice(row):
    return jnp.concatenate([row, row], axis=1)


def diagonal(pair):
    return jnp.concatenate([pair[:HALF, :QB], pair[HALF:, QB:]], axis=0)


def attend(scores, values_turned):
    peaks = [jnp.max(s, axis=0, keepdims=True) for s in scores]
    raised = [jnp.exp(s - peak) for s, peak in zip(scores, peaks)]
    totals = [jnp.sum(r, axis=0, keepdims=True) for r in raised]
    low = [(r * (1.0 / total)).astype(jnp.bfloat16) for r, total in zip(raised, totals)]
    mixed = [diagonal(dot_nn(vt, p)).astype(jnp.bfloat16) for vt, p in zip(values_turned, low)]
    stats = []
    for peak, total in zip(peaks, totals):
        lse = peak + jnp.log(total)
        stats += [lse[:, :QB], lse[:, QB:]]
    return mixed, jnp.concatenate(stats, axis=0)


def pull_back(scores, values_in, pulled, stats, keys_turned):
    attention = [
        jnp.exp(s - jnp.concatenate([stats[2 * i : 2 * i + 1], stats[2 * i + 1 : 2 * i + 2]], axis=1))
        for i, s in enumerate(scores)
    ]
    low = [a.astype(jnp.bfloat16) for a in attention]
    pushed = [dot_nt(v, g) for v, g in zip(values_in, pulled)]
    inner = [jnp.sum(a * p, axis=0, keepdims=True) for a, p in zip(attention, pushed)]
    grads = [
        (a * (p - i)).astype(jnp.bfloat16) for a, p, i in zip(attention, pushed, inner)
    ]
    turned = [
        diagonal(dot_nn(kt, g) * 0.125).astype(jnp.bfloat16) for kt, g in zip(keys_turned, grads)
    ]
    return low, grads, turned


def query_places(block):
    return block * QB + lax.broadcasted_iota(jnp.int32, (1, QB), 1)


def cross_forward_kernel(pairs, starts, pages, q_ref, k_ref, v_ref, o_ref, l_ref, vt_ref):
    page_count = k_ref.shape[0]
    for page in range(page_count):
        image = pages[page]
        low, high = starts[page], starts[page + 1]
        for pair in range(pairs):
            lanes = slice(pair * LANES, (pair + 1) * LANES)
            vt_ref[pair] = flip(v_ref[image, :, lanes])

        def body(block, carry):
            rows = pl.ds(pl.multiple_of(block * QB, QB), QB)
            place = query_places(block)
            member = (place >= low) & (place < high)
            spans = [slice(pair * LANES, (pair + 1) * LANES) for pair in range(pairs)]
            scores = [
                dot_nt(k_ref[image, :, lanes], head_stack(q_ref[rows, lanes], 0.125))
                for lanes in spans
            ]
            mixed, stats = attend(scores, [vt_ref[pair] for pair in range(pairs)])
            for lanes, block_out in zip(spans, mixed):
                o_ref[lanes, rows] = jnp.where(member, block_out, o_ref[lanes, rows])
            l_ref[0, :, rows] = jnp.where(member, stats, l_ref[0, :, rows])
            return carry

        lax.fori_loop(low // QB, (high - 1) // QB + 1, body, 0)


def flip(block):
    return jnp.transpose(block)


def cross_backward_kernel(
    pairs, starts, pages, q_ref, k_ref, v_ref, g_ref, l_ref, dq_ref, dk_ref, dv_ref,
    kt_ref, dka_ref, dva_ref,
):
    page_count = k_ref.shape[0]
    for page in range(page_count):
        image = pages[page]
        low, high = starts[page], starts[page + 1]
        for pair in range(pairs):
            lanes = slice(pair * LANES, (pair + 1) * LANES)
            kt_ref[pair] = flip(k_ref[image, :, lanes])
            dka_ref[pair] = jnp.zeros(dka_ref.shape[1:], jnp.float32)
            dva_ref[pair] = jnp.zeros(dva_ref.shape[1:], jnp.float32)

        def body(block, carry):
            rows = pl.ds(pl.multiple_of(block * QB, QB), QB)
            place = query_places(block)
            member = (place >= low) & (place < high)
            spans = [slice(pair * LANES, (pair + 1) * LANES) for pair in range(pairs)]
            stacked = [head_stack(q_ref[rows, lanes], 0.125) for lanes in spans]
            pulled = [head_stack(g_ref[rows, lanes]) for lanes in spans]
            stats = jnp.where(member, l_ref[0, :, rows], 1e30)
            keys_in = [k_ref[image, :, lanes] for lanes in spans]
            values_in = [v_ref[image, :, lanes] for lanes in spans]
            soft, grads, turned = pull_back(
                [dot_nt(k, q) for k, q in zip(keys_in, stacked)], values_in, pulled, stats,
                [kt_ref[pair] for pair in range(pairs)],
            )
            for pair, lanes in enumerate(spans):
                dq_ref[lanes, rows] = jnp.where(member, turned[pair], dq_ref[lanes, rows])
            for pair in range(pairs):
                dva_ref[pair] += dot_nn(soft[pair], pulled[pair])
            for pair in range(pairs):
                dka_ref[pair] += dot_nn(grads[pair], stacked[pair])
            return carry

        lax.fori_loop(low // QB, (high - 1) // QB + 1, body, 0)
        for pair in range(pairs):
            lanes = slice(pair * LANES, (pair + 1) * LANES)
            dk_ref[image, :, lanes] = dka_ref[pair].astype(jnp.bfloat16)
            dv_ref[image, :, lanes] = dva_ref[pair].astype(jnp.bfloat16)


def self_window(starts, block):
    start = starts[0]
    for page in range(1, starts.shape[0] - 1):
        start = jnp.where(starts[page] <= block * QB, starts[page], start)
    first = start // QB
    return first, block + 1 - first


def self_allowed(starts, place, first, chunks):
    begin = jnp.zeros(place.shape, jnp.int32)
    for page in range(1, starts.shape[0] - 1):
        begin = jnp.where(place >= starts[page], starts[page], begin)
    begin, end = twice(begin), twice(place)
    key = first * QB + lax.broadcasted_iota(jnp.int32, (chunks * QB, 2 * QB), 0)
    return (key >= begin) & (key <= end)


def self_forward_kernel(pairs, most, starts, q_ref, k_ref, v_ref, o_ref, l_ref, vt_ref):
    for pair in range(pairs):
        lanes = slice(pair * LANES, (pair + 1) * LANES)
        vt_ref[pair] = flip(v_ref[:, lanes])

    def body(block, carry):
        rows = pl.ds(pl.multiple_of(block * QB, QB), QB)
        first, count = self_window(starts, block)
        for chunks in range(1, most + 1):

            @pl.when(count == chunks)
            def _():
                keys = pl.ds(pl.multiple_of(first * QB, QB), chunks * QB)
                allowed = self_allowed(starts, query_places(block), first, chunks)
                spans = [slice(pair * LANES, (pair + 1) * LANES) for pair in range(pairs)]
                scores = [
                    jnp.where(
                        allowed, dot_nt(k_ref[keys, lanes], head_stack(q_ref[rows, lanes], 0.125)), -1e30
                    )
                    for lanes in spans
                ]
                mixed, stats = attend(scores, [vt_ref[pair, :, keys] for pair in range(pairs)])
                for lanes, block_out in zip(spans, mixed):
                    o_ref[lanes, rows] = block_out
                l_ref[0, :, rows] = stats

        return carry

    lax.fori_loop(0, q_ref.shape[0] // QB, body, 0)


def self_backward_kernel(
    pairs, most, starts, q_ref, k_ref, v_ref, g_ref, l_ref, dq_ref, dk_ref, dv_ref,
    kt_ref, dka_ref, dva_ref,
):
    for pair in range(pairs):
        lanes = slice(pair * LANES, (pair + 1) * LANES)
        kt_ref[pair] = flip(k_ref[:, lanes])
    dka_ref[...] = jnp.zeros(dka_ref.shape, jnp.float32)
    dva_ref[...] = jnp.zeros(dva_ref.shape, jnp.float32)

    def body(block, carry):
        rows = pl.ds(pl.multiple_of(block * QB, QB), QB)
        first, count = self_window(starts, block)
        for chunks in range(1, most + 1):

            @pl.when(count == chunks)
            def _():
                keys = pl.ds(pl.multiple_of(first * QB, QB), chunks * QB)
                allowed = self_allowed(starts, query_places(block), first, chunks)
                spans = [slice(pair * LANES, (pair + 1) * LANES) for pair in range(pairs)]
                stacked = [head_stack(q_ref[rows, lanes], 0.125) for lanes in spans]
                pulled = [head_stack(g_ref[rows, lanes]) for lanes in spans]
                scores = [
                    jnp.where(allowed, dot_nt(k_ref[keys, lanes], q), -1e30)
                    for lanes, q in zip(spans, stacked)
                ]
                soft, grads, turned = pull_back(
                    scores, [v_ref[keys, lanes] for lanes in spans], pulled, l_ref[0, :, rows],
                    [kt_ref[pair, :, keys] for pair in range(pairs)],
                )
                for pair, lanes in enumerate(spans):
                    dq_ref[lanes, rows] = turned[pair]
                for pair in range(pairs):
                    dva_ref[pair, keys, :] += dot_nn(soft[pair], pulled[pair])
                for pair in range(pairs):
                    dka_ref[pair, keys, :] += dot_nn(grads[pair], stacked[pair])

        return carry

    lax.fori_loop(0, q_ref.shape[0] // QB, body, 0)
    for pair in range(pairs):
        lanes = slice(pair * LANES, (pair + 1) * LANES)
        dk_ref[:, lanes] = dka_ref[pair].astype(jnp.bfloat16)
        dv_ref[:, lanes] = dva_ref[pair].astype(jnp.bfloat16)


def cost(flops, bytes_accessed, exps):
    return pl.CostEstimate(flops=flops, bytes_accessed=bytes_accessed, transcendentals=exps)


def specs(pairs, prefetch):
    wide = pairs * LANES

    def at(index):
        return lambda step, *scalars: index(step)

    return {
        "rows": lambda length: pl.BlockSpec((length, wide), at(lambda i: (0, i))),
        "turned": lambda length: pl.BlockSpec((wide, length), at(lambda i: (i, 0))),
        "images": lambda count, tokens: pl.BlockSpec((count, tokens, wide), at(lambda i: (0, 0, i))),
        "stats": lambda length: pl.BlockSpec((1, 2 * pairs, length), at(lambda i: (i, 0, 0))),
    }


def cross_forward(starts, pages, queries, keys_all, values_all, pairs=4):
    length, width = queries.shape
    count, tokens, _ = keys_all.shape
    steps = width // (pairs * LANES)
    s = specs(pairs, 2)
    return pl.pallas_call(
        functools.partial(cross_forward_kernel, pairs),
        out_shape=(
            jax.ShapeDtypeStruct((width, length), jnp.bfloat16),
            jax.ShapeDtypeStruct((steps, 2 * pairs, length), jnp.float32),
        ),
        grid_spec=pltpu.PrefetchScalarGridSpec(
            num_scalar_prefetch=2,
            grid=(steps,),
            in_specs=[s["rows"](length), s["images"](count, tokens), s["images"](count, tokens)],
            out_specs=[s["turned"](length), s["stats"](length)],
            scratch_shapes=[pltpu.VMEM((pairs, LANES, tokens), jnp.bfloat16)],
        ),
        cost_estimate=cost(11 * 128 * tokens * width * 4 * 4, 20 * 2**20, 2**24),
        name="cross_forward",
    )(starts, pages, queries, keys_all, values_all)


def cross_backward(starts, pages, queries, keys_all, values_all, grads, stats, pairs=4):
    length, width = queries.shape
    count, tokens, _ = keys_all.shape
    steps = width // (pairs * LANES)
    s = specs(pairs, 2)
    image_spec = s["images"](count, tokens)
    return pl.pallas_call(
        functools.partial(cross_backward_kernel, pairs),
        out_shape=(
            jax.ShapeDtypeStruct((width, length), jnp.bfloat16),
            jax.ShapeDtypeStruct(keys_all.shape, jnp.bfloat16),
            jax.ShapeDtypeStruct(values_all.shape, jnp.bfloat16),
        ),
        grid_spec=pltpu.PrefetchScalarGridSpec(
            num_scalar_prefetch=2,
            grid=(steps,),
            in_specs=[s["rows"](length), image_spec, image_spec, s["rows"](length), s["stats"](length)],
            out_specs=[s["turned"](length), image_spec, image_spec],
            scratch_shapes=[
                pltpu.VMEM((pairs, LANES, tokens), jnp.bfloat16),
                pltpu.VMEM((pairs, tokens, LANES), jnp.float32),
                pltpu.VMEM((pairs, tokens, LANES), jnp.float32),
            ],
        ),
        cost_estimate=cost(11 * 128 * tokens * width * 10 * 4, 30 * 2**20, 2**24),
        name="cross_backward",
    )(starts, pages, queries, keys_all, values_all, grads, stats)


def self_forward(starts, queries, keys_all, values_all, most, pairs=4):
    length, width = queries.shape
    steps = width // (pairs * LANES)
    s = specs(pairs, 1)
    rows = s["rows"](length)
    return pl.pallas_call(
        functools.partial(self_forward_kernel, pairs, most),
        out_shape=(
            jax.ShapeDtypeStruct((width, length), jnp.bfloat16),
            jax.ShapeDtypeStruct((steps, 2 * pairs, length), jnp.float32),
        ),
        grid_spec=pltpu.PrefetchScalarGridSpec(
            num_scalar_prefetch=1,
            grid=(steps,),
            in_specs=[rows, rows, rows],
            out_specs=[s["turned"](length), s["stats"](length)],
            scratch_shapes=[pltpu.VMEM((pairs, LANES, length), jnp.bfloat16)],
        ),
        cost_estimate=cost(20 * 128 * 128 * width * 4 * 4, 10 * 2**20, 2**23),
        name="self_forward",
    )(starts, queries, keys_all, values_all)


def self_backward(starts, queries, keys_all, values_all, grads, stats, most, pairs=4):
    length, width = queries.shape
    steps = width // (pairs * LANES)
    s = specs(pairs, 1)
    rows = s["rows"](length)
    return pl.pallas_call(
        functools.partial(self_backward_kernel, pairs, most),
        out_shape=(
            jax.ShapeDtypeStruct((width, length), jnp.bfloat16),
            jax.ShapeDtypeStruct((length, width), jnp.bfloat16),
            jax.ShapeDtypeStruct((length, width), jnp.bfloat16),
        ),
        grid_spec=pltpu.PrefetchScalarGridSpec(
            num_scalar_prefetch=1,
            grid=(steps,),
            in_specs=[rows, rows, rows, rows, s["stats"](length)],
            out_specs=[s["turned"](length), rows, rows],
            scratch_shapes=[
                pltpu.VMEM((pairs, LANES, length), jnp.bfloat16),
                pltpu.VMEM((pairs, length, LANES), jnp.float32),
                pltpu.VMEM((pairs, length, LANES), jnp.float32),
            ],
        ),
        cost_estimate=cost(20 * 128 * 128 * width * 10 * 4, 16 * 2**20, 2**23),
        name="self_backward",
    )(starts, queries, keys_all, values_all, grads, stats)


EPSILON = 1e-05
ROOT_HALF = 0.7071067811865476
ROOT_TAU = 0.3989422804014327
AXES = ("dp", "fsdp")
LONGEST = 512


def contract(a, b, left, right, out=jnp.float32):
    return lax.dot_general(
        a, b, ((left, right), ((), ())), preferred_element_type=jnp.float32
    ).astype(out)


def row_major(values):
    return with_layout_constraint(values, Layout(major_to_minor=(0, 1)))


def normalise(values):
    average = jnp.mean(values, axis=-1, keepdims=True)
    centered = values - average
    variance = jnp.mean(centered * centered, axis=-1, keepdims=True)
    scale = lax.rsqrt(variance + EPSILON)
    return centered * scale, scale


def norm_back(values, gain, grads):
    hat, scale = normalise(values)
    pulled = grads * gain
    first = jnp.mean(pulled, axis=-1, keepdims=True)
    second = jnp.mean(pulled * hat, axis=-1, keepdims=True)
    back = scale * (pulled - first - hat * second)
    return back, jnp.sum(grads * hat, axis=0), jnp.sum(grads, axis=0)


def swap(value, axis, size, bit):
    return lax.ppermute(value, axis, [(i, i ^ bit) for i in range(size)])


def butterfly_sum(value, sizes):
    for axis, size in sizes:
        bit = 1
        while bit < size:
            value = value + swap(value, axis, size, bit)
            bit *= 2
    return value


def pick(value, index, axis):
    return lax.dynamic_index_in_dim(value, index, axis, keepdims=False)


def fence(*values):
    return lax.optimization_barrier(values)


class Partial:
    def __init__(self, value, sizes, blocks=1):
        dp_size, inner = sizes
        keys, places = ["block"], {}
        for axis, size in (("dp", dp_size), ("fsdp", inner)):
            bit = size // 2
            while bit:
                keys.append((axis, bit))
                places[(axis, bit)] = (lax.axis_index(axis) // bit) % 2
                bit //= 2
        own = value.shape[0] // (blocks * dp_size * inner)
        self.sizes = {"dp": dp_size, "fsdp": inner}
        self.keys, self.places = keys, places
        bits = (2,) * (len(keys) - 1)
        self.terms = [value.reshape((blocks,) + bits + (own, value.shape[1]))]

    def total(self, terms):
        wide = [term.astype(jnp.float32) for term in terms]
        return functools.reduce(jnp.add, wide)

    def send(self, key):
        return self.fly(self.cut(key), key)

    def fly(self, load, key):
        return swap(load, key[0], self.sizes[key[0]], key[1])

    def cut(self, key):
        axis = self.keys.index(key)
        self.keys.remove(key)
        out = self.total([pick(term, 1 - self.places[key], axis) for term in self.terms])
        self.terms = [pick(term, self.places[key], axis) for term in self.terms]
        return out.astype(jnp.bfloat16)

    def take(self, received):
        self.terms.append(received)

    def rest(self):
        return self.total(self.terms).astype(jnp.bfloat16)


CORE = ("dp", 1)
ACROSS = ("dp", 2)


def scatter(parts, sizes):
    inner = sizes[1]
    rests = []
    for part in parts:
        rest = part.rest()
        blocks, (own, columns) = rest.shape[0], rest.shape[-2:]
        rest = rest.reshape(blocks, inner, own, columns).transpose(1, 0, 2, 3)
        rests.append(rest.reshape(inner, blocks * own, columns))
    packed = rests[0] if len(rests) == 1 else jnp.concatenate(rests, axis=1)
    summed = lax.psum_scatter(
        packed.reshape(-1, columns), "fsdp", scatter_dimension=0, tiled=True
    ).astype(jnp.float32)
    own = summed.shape[0] // len(parts)
    return [summed[i * own : (i + 1) * own] for i in range(len(parts))]


def layer(
    sizes, block_in, images, segment_ids, page_map, ln1_gain, ln1_shift, ln2_gain, ln2_shift,
    ln3_gain, ln3_shift, self_query, self_key, self_value, self_out, cross_query, cross_key,
    cross_value, cross_out, mlp_in, mlp_out, cotangent,
):
    dp_size, inner = sizes
    axes = (("dp", dp_size), ("fsdp", inner))
    _, length, width = block_in.shape
    low = jnp.bfloat16

    def turned(master):
        return master.astype(low).T

    def gather(*masters):
        stacked = jnp.stack([turned(m) for m in masters])
        return lax.all_gather(stacked, AXES, axis=1, tiled=True)

    norms = jnp.stack([ln1_gain, ln1_shift, ln2_gain, ln2_shift, ln3_gain, ln3_shift])
    norms = norms.astype(low).astype(jnp.float32)
    mine = norms.shape[1]
    offset = (lax.axis_index("dp") * inner + lax.axis_index("fsdp")) * mine
    spread = lax.dynamic_update_slice(jnp.zeros((6, width), jnp.float32), norms, (0, offset))
    norms = butterfly_sum(spread, axes)
    near = gather(
        self_query, self_key, self_value, self_out, cross_query, cross_key, cross_value, cross_out
    )
    w_sqkv, w_kv = near[:3], near[5:7]
    w_so, w_cq, w_ck, w_cv, w_co = [near[i] for i in range(3, 8)]
    own, devices = mlp_out.shape[1], dp_size * inner
    blocks = mlp_out.shape[0] // width
    step = width // devices
    in_rows = turned(mlp_in).reshape(blocks, step, width)
    out_rows = turned(mlp_out).reshape(own, devices, blocks, step).transpose(2, 0, 1, 3)
    far = jnp.concatenate([in_rows, out_rows.reshape(blocks, own, width)])
    far = lax.all_gather(far, AXES, axis=1, tiled=True)
    (far,) = fence(far.reshape(2, blocks * width, width))
    w_in = far[0]
    w_out = jnp.concatenate(
        [far[1, i * width : (i + 1) * width] for i in range(blocks)], axis=1
    )

    starts = jnp.sum(
        segment_ids[0][None, :] < jnp.arange(page_map.shape[1] + 1, dtype=jnp.int32)[:, None],
        axis=1,
    ).astype(jnp.int32)
    pages = page_map[0]
    most = LONGEST // QB + 1

    rows = block_in[0].astype(jnp.float32)
    a1 = (normalise(rows)[0] * norms[0] + norms[1]).astype(low)
    sq, sk, sv = [contract(a1, w_sqkv[i], (1,), (1,), low) for i in range(3)]
    so, s_stats = self_forward(starts, sq, sk, sv, most)
    x1 = row_major(rows + contract(so, w_so, (0,), (1,)))
    a2 = (normalise(x1)[0] * norms[2] + norms[3]).astype(low)
    cq = contract(a2, w_cq, (1,), (1,), low)
    ck = contract(images, w_ck, (2,), (1,), low)
    cv = contract(images, w_cv, (2,), (1,), low)
    co, c_stats = cross_forward(starts, pages, cq, ck, cv)
    x2 = row_major(x1 + contract(co, w_co, (0,), (1,)))
    a3 = (normalise(x2)[0] * norms[4] + norms[5]).astype(low)
    u = contract(a3, w_in, (1,), (1,))
    phi = 0.5 * (1.0 + lax.erf(u * ROOT_HALF))
    hidden = (u * phi).astype(low)
    slope = (phi + u * (ROOT_TAU * jnp.exp(-0.5 * u * u))).astype(low)

    eb = cotangent[0]
    e = eb.astype(jnp.float32)
    g_out = contract(eb, hidden, (0,), (0,), low)
    p_out = Partial(g_out, sizes)
    flying = p_out.send(CORE)
    eb, hidden, g_out = fence(eb, hidden, g_out)
    du = (contract(eb, w_out, (1,), (0,)) * slope.astype(jnp.float32)).astype(low)
    du, flying = fence(du, flying)
    p_out.take(flying)
    flying = p_out.send(ACROSS)
    g_in = contract(du, a3, (0,), (0,), low)
    du, g_in = fence(du, g_in)
    p_in = Partial(g_in, sizes, blocks)
    flying_in = p_in.send(CORE)
    d3 = contract(du, w_in, (1,), (0,))
    back, gg3, gs3 = norm_back(x2, norms[4], d3)
    e2 = e + back
    e2b = e2.astype(low)
    e2, e2b, flying_in = fence(e2, e2b, flying_in)
    p_in.take(flying_in)
    flying_in = p_in.send(ACROSS)
    d_co = contract(e2b, w_co, (1,), (0,), low)
    dcq, dck, dcv = cross_backward(starts, pages, cq, ck, cv, d_co, c_stats)
    dcq, dck, dcv, flying, flying_in = fence(dcq, dck, dcv, flying, flying_in)
    p_out.take(flying)
    (g_mlp_out,) = scatter([p_out], sizes)
    p_in.take(flying_in)
    (g_mlp_in,) = scatter([p_in], sizes)
    g_co = contract(e2b, co, (0,), (1,), low)
    g_cq = contract(dcq, a2, (1,), (0,), low)
    g_ck = contract(dck, images, (0, 1), (0, 1), low)
    g_cv = contract(dcv, images, (0, 1), (0, 1), low)
    dcq, g_cq, g_ck, g_cv, g_co = fence(dcq, g_cq, g_ck, g_cv, g_co)
    p_cross = [Partial(g, sizes) for g in (g_cq, g_ck, g_cv, g_co)]
    flying = [p.send(CORE) for p in p_cross]
    d2 = contract(dcq, w_cq, (0,), (0,))
    back, gg2, gs2 = norm_back(x1, norms[2], d2)
    e1 = e2 + back
    e1b = e1.astype(low)
    e1, e1b, *flying = fence(e1, e1b, *flying)
    for p, f in zip(p_cross, flying):
        p.take(f)
    flying = [p.send(ACROSS) for p in p_cross]
    g_so = contract(e1b, so, (0,), (1,), low)
    d_so = contract(e1b, w_so, (1,), (0,), low)
    dsq, dsk, dsv = self_backward(starts, sq, sk, sv, d_so, s_stats, most)
    dsq, dsk, dsv, g_so, *flying = fence(dsq, dsk, dsv, g_so, *flying)
    for p, f in zip(p_cross, flying):
        p.take(f)
    g_cross = scatter(p_cross, sizes)
    g_sq = contract(dsq, a1, (1,), (0,), low)
    g_sk = contract(dsk, a1, (0,), (0,), low)
    g_sv = contract(dsv, a1, (0,), (0,), low)
    pairs = (jnp.concatenate([g_sq, g_sk]), jnp.concatenate([g_sv, g_so]))
    dsq, dsk, dsv, *pairs = fence(dsq, dsk, dsv, *pairs)
    groups = [Partial(pair, sizes, 2) for pair in pairs]
    keys = [("fsdp", 1 << i) for i in range(inner.bit_length() - 1)]
    orders = [[ACROSS] + keys, keys[:-1] + [ACROSS] + keys[-1:]]
    flights = [g.send(CORE) for g in groups]
    d1 = (
        contract(dsq, w_sqkv[0], (0,), (0,))
        + contract(dsk, w_sqkv[1], (1,), (0,))
        + contract(dsv, w_sqkv[2], (1,), (0,))
    )

    def norm_one(d1):
        back, gg1, gs1 = norm_back(rows, norms[0], d1)
        return e1 + back, gg1, gs1

    def image_grads(dck, dcv):
        both = jnp.concatenate([dck, dcv], axis=2).transpose(1, 0, 2)
        tokens, count, _ = both.shape
        flat = contract(
            both.reshape(tokens * count, 2 * width), w_kv.reshape(2 * width, width), (1,), (0,)
        )
        return flat.reshape(tokens, count, width)

    def finish(hidden):
        return (x2 + contract(hidden, w_out, (1,), (1,))).astype(low)

    grad_in, gg1, gs1 = norm_one(d1)
    grad_in, hidden, dck, dcv, *flights = fence(grad_in, hidden, dck, dcv, *flights)
    for stage in range(len(keys) + 1):
        for g, f in zip(groups, flights):
            g.take(f)
        loads = [g.cut(o[stage]) for g, o in zip(groups, orders)]
        if stage == 0:
            hidden, *loads = fence(hidden, *loads)
        if stage == 1:
            dck, dcv, *loads = fence(dck, dcv, *loads)
        flights = [g.fly(load, o[stage]) for g, load, o in zip(groups, loads, orders)]
        if stage == 0:
            block_out, *flights = fence(finish(hidden), *flights)
        if stage == 1:
            grad_images, *flights = fence(image_grads(dck, dcv), *flights)
            grad_images = grad_images.transpose(1, 0, 2)
    for g, f in zip(groups, flights):
        g.take(f)
    g_self = [g.total(g.terms)[i] for g in groups for i in range(2)]
    norm_grads = butterfly_sum(jnp.stack([gg1, gs1, gg2, gs2, gg3, gs3]), axes)
    norm_grads = lax.dynamic_slice(norm_grads, (0, offset), (6, mine))
    g_mlp_out = g_mlp_out.reshape(own, blocks, devices, step).transpose(0, 2, 1, 3)
    g_mlp_out = g_mlp_out.reshape(own, -1)
    weight_grads = [g.T for g in g_self + g_cross + [g_mlp_in, g_mlp_out]]
    return (
        block_out[None], grad_in[None], grad_images, *[norm_grads[i] for i in range(6)],
        *weight_grads,
    )


def solution(mesh):
    sizes = (mesh.shape["dp"], mesh.shape["fsdp"])
    rows3 = P(AXES, None, None)
    rows2 = P(AXES, None)
    vector = P(AXES)
    columns = P(None, AXES)
    return jax.shard_map(
        functools.partial(layer, sizes),
        mesh=mesh,
        in_specs=(rows3, rows3, rows2, rows2) + (vector,) * 6 + (columns,) * 10 + (rows3,),
        out_specs=(rows3,) * 3 + (vector,) * 6 + (columns,) * 10,
        check_vma=False,
    )
```

```python
import functools
import jax
import jax.numpy as jnp
from jax import lax
from jax.experimental import pallas as pl
from jax.experimental.layout import Layout, with_layout_constraint
from jax.experimental.pallas import tpu as pltpu
from jax.sharding import PartitionSpec as P

LANES = 128
HALF = 64
QB = 128


def dot_nt(a, b):
    return lax.dot_general(a, b, (((1,), (1,)), ((), ())), preferred_element_type=jnp.float32)


def dot_nn(a, b):
    return lax.dot_general(a, b, (((1,), (0,)), ((), ())), preferred_element_type=jnp.float32)


def head_stack(block, scale=None):
    lane = lax.broadcasted_iota(jnp.int32, block.shape, 1)
    wide = block.astype(jnp.float32)
    if scale is not None:
        wide = wide * scale
    first = jnp.where(lane < HALF, wide, 0.0).astype(jnp.bfloat16)
    second = jnp.where(lane < HALF, 0.0, wide).astype(jnp.bfloat16)
    return jnp.concatenate([first, second], axis=0)


def twice(row):
    return jnp.concatenate([row, row], axis=1)


def diagonal(pair):
    return jnp.concatenate([pair[:HALF, :QB], pair[HALF:, QB:]], axis=0)


def attend(scores, values_turned):
    peaks = [jnp.max(s, axis=0, keepdims=True) for s in scores]
    raised = [jnp.exp(s - peak) for s, peak in zip(scores, peaks)]
    totals = [jnp.sum(r, axis=0, keepdims=True) for r in raised]
    low = [(r * (1.0 / total)).astype(jnp.bfloat16) for r, total in zip(raised, totals)]
    mixed = [diagonal(dot_nn(vt, p)).astype(jnp.bfloat16) for vt, p in zip(values_turned, low)]
    stats = []
    for peak, total in zip(peaks, totals):
        lse = peak + jnp.log(total)
        stats += [lse[:, :QB], lse[:, QB:]]
    return mixed, jnp.concatenate(stats, axis=0)


def pull_back(scores, values_in, pulled, stats, keys_turned):
    attention = [
        jnp.exp(s - jnp.concatenate([stats[2 * i : 2 * i + 1], stats[2 * i + 1 : 2 * i + 2]], axis=1))
        for i, s in enumerate(scores)
    ]
    low = [a.astype(jnp.bfloat16) for a in attention]
    pushed = [dot_nt(v, g) for v, g in zip(values_in, pulled)]
    inner = [jnp.sum(a * p, axis=0, keepdims=True) for a, p in zip(attention, pushed)]
    grads = [
        (a * (p - i)).astype(jnp.bfloat16) for a, p, i in zip(attention, pushed, inner)
    ]
    turned = [
        diagonal(dot_nn(kt, g) * 0.125).astype(jnp.bfloat16) for kt, g in zip(keys_turned, grads)
    ]
    return low, grads, turned


def query_places(block):
    return block * QB + lax.broadcasted_iota(jnp.int32, (1, QB), 1)


def cross_forward_kernel(pairs, starts, pages, q_ref, k_ref, v_ref, o_ref, l_ref, vt_ref):
    page_count = k_ref.shape[0]
    for page in range(page_count):
        image = pages[page]
        low, high = starts[page], starts[page + 1]
        for pair in range(pairs):
            lanes = slice(pair * LANES, (pair + 1) * LANES)
            vt_ref[pair] = flip(v_ref[image, :, lanes])

        def body(block, carry):
            rows = pl.ds(pl.multiple_of(block * QB, QB), QB)
            place = query_places(block)
            member = (place >= low) & (place < high)
            spans = [slice(pair * LANES, (pair + 1) * LANES) for pair in range(pairs)]
            scores = [
                dot_nt(k_ref[image, :, lanes], head_stack(q_ref[rows, lanes], 0.125))
                for lanes in spans
            ]
            mixed, stats = attend(scores, [vt_ref[pair] for pair in range(pairs)])
            for lanes, block_out in zip(spans, mixed):
                o_ref[lanes, rows] = jnp.where(member, block_out, o_ref[lanes, rows])
            l_ref[0, :, rows] = jnp.where(member, stats, l_ref[0, :, rows])
            return carry

        lax.fori_loop(low // QB, (high - 1) // QB + 1, body, 0)


def flip(block):
    return jnp.transpose(block)


def cross_backward_kernel(
    pairs, starts, pages, q_ref, k_ref, v_ref, g_ref, l_ref, dq_ref, dk_ref, dv_ref,
    kt_ref, dka_ref, dva_ref,
):
    page_count = k_ref.shape[0]
    for page in range(page_count):
        image = pages[page]
        low, high = starts[page], starts[page + 1]
        for pair in range(pairs):
            lanes = slice(pair * LANES, (pair + 1) * LANES)
            kt_ref[pair] = flip(k_ref[image, :, lanes])
            dka_ref[pair] = jnp.zeros(dka_ref.shape[1:], jnp.float32)
            dva_ref[pair] = jnp.zeros(dva_ref.shape[1:], jnp.float32)

        def body(block, carry):
            rows = pl.ds(pl.multiple_of(block * QB, QB), QB)
            place = query_places(block)
            member = (place >= low) & (place < high)
            spans = [slice(pair * LANES, (pair + 1) * LANES) for pair in range(pairs)]
            stacked = [head_stack(q_ref[rows, lanes], 0.125) for lanes in spans]
            pulled = [head_stack(g_ref[rows, lanes]) for lanes in spans]
            stats = jnp.where(member, l_ref[0, :, rows], 1e30)
            keys_in = [k_ref[image, :, lanes] for lanes in spans]
            values_in = [v_ref[image, :, lanes] for lanes in spans]
            soft, grads, turned = pull_back(
                [dot_nt(k, q) for k, q in zip(keys_in, stacked)], values_in, pulled, stats,
                [kt_ref[pair] for pair in range(pairs)],
            )
            for pair, lanes in enumerate(spans):
                dq_ref[lanes, rows] = jnp.where(member, turned[pair], dq_ref[lanes, rows])
            for pair in range(pairs):
                dva_ref[pair] += dot_nn(soft[pair], pulled[pair])
            for pair in range(pairs):
                dka_ref[pair] += dot_nn(grads[pair], stacked[pair])
            return carry

        lax.fori_loop(low // QB, (high - 1) // QB + 1, body, 0)
        for pair in range(pairs):
            lanes = slice(pair * LANES, (pair + 1) * LANES)
            dk_ref[image, :, lanes] = dka_ref[pair].astype(jnp.bfloat16)
            dv_ref[image, :, lanes] = dva_ref[pair].astype(jnp.bfloat16)


def self_window(starts, block):
    start = starts[0]
    for page in range(1, starts.shape[0] - 1):
        start = jnp.where(starts[page] <= block * QB, starts[page], start)
    first = start // QB
    return first, block + 1 - first


def self_allowed(starts, place, first, chunks):
    begin = jnp.zeros(place.shape, jnp.int32)
    for page in range(1, starts.shape[0] - 1):
        begin = jnp.where(place >= starts[page], starts[page], begin)
    begin, end = twice(begin), twice(place)
    key = first * QB + lax.broadcasted_iota(jnp.int32, (chunks * QB, 2 * QB), 0)
    return (key >= begin) & (key <= end)


def self_forward_kernel(pairs, most, starts, q_ref, k_ref, v_ref, o_ref, l_ref, vt_ref):
    for pair in range(pairs):
        lanes = slice(pair * LANES, (pair + 1) * LANES)
        vt_ref[pair] = flip(v_ref[:, lanes])

    def body(block, carry):
        rows = pl.ds(pl.multiple_of(block * QB, QB), QB)
        first, count = self_window(starts, block)
        for chunks in range(1, most + 1):

            @pl.when(count == chunks)
            def _():
                keys = pl.ds(pl.multiple_of(first * QB, QB), chunks * QB)
                allowed = self_allowed(starts, query_places(block), first, chunks)
                spans = [slice(pair * LANES, (pair + 1) * LANES) for pair in range(pairs)]
                scores = [
                    jnp.where(
                        allowed, dot_nt(k_ref[keys, lanes], head_stack(q_ref[rows, lanes], 0.125)), -1e30
                    )
                    for lanes in spans
                ]
                mixed, stats = attend(scores, [vt_ref[pair, :, keys] for pair in range(pairs)])
                for lanes, block_out in zip(spans, mixed):
                    o_ref[lanes, rows] = block_out
                l_ref[0, :, rows] = stats

        return carry

    lax.fori_loop(0, q_ref.shape[0] // QB, body, 0)


def self_backward_kernel(
    pairs, most, starts, q_ref, k_ref, v_ref, g_ref, l_ref, dq_ref, dk_ref, dv_ref,
    kt_ref, dka_ref, dva_ref,
):
    for pair in range(pairs):
        lanes = slice(pair * LANES, (pair + 1) * LANES)
        kt_ref[pair] = flip(k_ref[:, lanes])
    dka_ref[...] = jnp.zeros(dka_ref.shape, jnp.float32)
    dva_ref[...] = jnp.zeros(dva_ref.shape, jnp.float32)

    def body(block, carry):
        rows = pl.ds(pl.multiple_of(block * QB, QB), QB)
        first, count = self_window(starts, block)
        for chunks in range(1, most + 1):

            @pl.when(count == chunks)
            def _():
                keys = pl.ds(pl.multiple_of(first * QB, QB), chunks * QB)
                allowed = self_allowed(starts, query_places(block), first, chunks)
                spans = [slice(pair * LANES, (pair + 1) * LANES) for pair in range(pairs)]
                stacked = [head_stack(q_ref[rows, lanes], 0.125) for lanes in spans]
                pulled = [head_stack(g_ref[rows, lanes]) for lanes in spans]
                scores = [
                    jnp.where(allowed, dot_nt(k_ref[keys, lanes], q), -1e30)
                    for lanes, q in zip(spans, stacked)
                ]
                soft, grads, turned = pull_back(
                    scores, [v_ref[keys, lanes] for lanes in spans], pulled, l_ref[0, :, rows],
                    [kt_ref[pair, :, keys] for pair in range(pairs)],
                )
                for pair, lanes in enumerate(spans):
                    dq_ref[lanes, rows] = turned[pair]
                for pair in range(pairs):
                    dva_ref[pair, keys, :] += dot_nn(soft[pair], pulled[pair])
                for pair in range(pairs):
                    dka_ref[pair, keys, :] += dot_nn(grads[pair], stacked[pair])

        return carry

    lax.fori_loop(0, q_ref.shape[0] // QB, body, 0)
    for pair in range(pairs):
        lanes = slice(pair * LANES, (pair + 1) * LANES)
        dk_ref[:, lanes] = dka_ref[pair].astype(jnp.bfloat16)
        dv_ref[:, lanes] = dva_ref[pair].astype(jnp.bfloat16)


def cost(flops, bytes_accessed, exps):
    return pl.CostEstimate(flops=flops, bytes_accessed=bytes_accessed, transcendentals=exps)


def specs(pairs, prefetch):
    wide = pairs * LANES

    def at(index):
        return lambda step, *scalars: index(step)

    return {
        "rows": lambda length: pl.BlockSpec((length, wide), at(lambda i: (0, i))),
        "turned": lambda length: pl.BlockSpec((wide, length), at(lambda i: (i, 0))),
        "images": lambda count, tokens: pl.BlockSpec((count, tokens, wide), at(lambda i: (0, 0, i))),
        "stats": lambda length: pl.BlockSpec((1, 2 * pairs, length), at(lambda i: (i, 0, 0))),
    }


def cross_forward(starts, pages, queries, keys_all, values_all, pairs=4):
    length, width = queries.shape
    count, tokens, _ = keys_all.shape
    steps = width // (pairs * LANES)
    s = specs(pairs, 2)
    return pl.pallas_call(
        functools.partial(cross_forward_kernel, pairs),
        out_shape=(
            jax.ShapeDtypeStruct((width, length), jnp.bfloat16),
            jax.ShapeDtypeStruct((steps, 2 * pairs, length), jnp.float32),
        ),
        grid_spec=pltpu.PrefetchScalarGridSpec(
            num_scalar_prefetch=2,
            grid=(steps,),
            in_specs=[s["rows"](length), s["images"](count, tokens), s["images"](count, tokens)],
            out_specs=[s["turned"](length), s["stats"](length)],
            scratch_shapes=[pltpu.VMEM((pairs, LANES, tokens), jnp.bfloat16)],
        ),
        cost_estimate=cost(11 * 128 * tokens * width * 4 * 4, 20 * 2**20, 2**24),
        name="cross_forward",
    )(starts, pages, queries, keys_all, values_all)


def cross_backward(starts, pages, queries, keys_all, values_all, grads, stats, pairs=4):
    length, width = queries.shape
    count, tokens, _ = keys_all.shape
    steps = width // (pairs * LANES)
    s = specs(pairs, 2)
    image_spec = s["images"](count, tokens)
    return pl.pallas_call(
        functools.partial(cross_backward_kernel, pairs),
        out_shape=(
            jax.ShapeDtypeStruct((width, length), jnp.bfloat16),
            jax.ShapeDtypeStruct(keys_all.shape, jnp.bfloat16),
            jax.ShapeDtypeStruct(values_all.shape, jnp.bfloat16),
        ),
        grid_spec=pltpu.PrefetchScalarGridSpec(
            num_scalar_prefetch=2,
            grid=(steps,),
            in_specs=[s["rows"](length), image_spec, image_spec, s["rows"](length), s["stats"](length)],
            out_specs=[s["turned"](length), image_spec, image_spec],
            scratch_shapes=[
                pltpu.VMEM((pairs, LANES, tokens), jnp.bfloat16),
                pltpu.VMEM((pairs, tokens, LANES), jnp.float32),
                pltpu.VMEM((pairs, tokens, LANES), jnp.float32),
            ],
        ),
        cost_estimate=cost(11 * 128 * tokens * width * 10 * 4, 30 * 2**20, 2**24),
        name="cross_backward",
    )(starts, pages, queries, keys_all, values_all, grads, stats)


def self_forward(starts, queries, keys_all, values_all, most, pairs=4):
    length, width = queries.shape
    steps = width // (pairs * LANES)
    s = specs(pairs, 1)
    rows = s["rows"](length)
    return pl.pallas_call(
        functools.partial(self_forward_kernel, pairs, most),
        out_shape=(
            jax.ShapeDtypeStruct((width, length), jnp.bfloat16),
            jax.ShapeDtypeStruct((steps, 2 * pairs, length), jnp.float32),
        ),
        grid_spec=pltpu.PrefetchScalarGridSpec(
            num_scalar_prefetch=1,
            grid=(steps,),
            in_specs=[rows, rows, rows],
            out_specs=[s["turned"](length), s["stats"](length)],
            scratch_shapes=[pltpu.VMEM((pairs, LANES, length), jnp.bfloat16)],
        ),
        cost_estimate=cost(20 * 128 * 128 * width * 4 * 4, 10 * 2**20, 2**23),
        name="self_forward",
    )(starts, queries, keys_all, values_all)


def self_backward(starts, queries, keys_all, values_all, grads, stats, most, pairs=4):
    length, width = queries.shape
    steps = width // (pairs * LANES)
    s = specs(pairs, 1)
    rows = s["rows"](length)
    return pl.pallas_call(
        functools.partial(self_backward_kernel, pairs, most),
        out_shape=(
            jax.ShapeDtypeStruct((width, length), jnp.bfloat16),
            jax.ShapeDtypeStruct((length, width), jnp.bfloat16),
            jax.ShapeDtypeStruct((length, width), jnp.bfloat16),
        ),
        grid_spec=pltpu.PrefetchScalarGridSpec(
            num_scalar_prefetch=1,
            grid=(steps,),
            in_specs=[rows, rows, rows, rows, s["stats"](length)],
            out_specs=[s["turned"](length), rows, rows],
            scratch_shapes=[
                pltpu.VMEM((pairs, LANES, length), jnp.bfloat16),
                pltpu.VMEM((pairs, length, LANES), jnp.float32),
                pltpu.VMEM((pairs, length, LANES), jnp.float32),
            ],
        ),
        cost_estimate=cost(20 * 128 * 128 * width * 10 * 4, 16 * 2**20, 2**23),
        name="self_backward",
    )(starts, queries, keys_all, values_all, grads, stats)


EPSILON = 1e-05
ROOT_HALF = 0.7071067811865476
ROOT_TAU = 0.3989422804014327
AXES = ("dp", "fsdp")
LONGEST = 512


def contract(a, b, left, right, out=jnp.float32):
    return lax.dot_general(
        a, b, ((left, right), ((), ())), preferred_element_type=jnp.float32
    ).astype(out)


def row_major(values):
    return with_layout_constraint(values, Layout(major_to_minor=(0, 1)))


def normalise(values):
    average = jnp.mean(values, axis=-1, keepdims=True)
    centered = values - average
    variance = jnp.mean(centered * centered, axis=-1, keepdims=True)
    scale = lax.rsqrt(variance + EPSILON)
    return centered * scale, scale


def norm_back(values, gain, grads):
    hat, scale = normalise(values)
    pulled = grads * gain
    first = jnp.mean(pulled, axis=-1, keepdims=True)
    second = jnp.mean(pulled * hat, axis=-1, keepdims=True)
    back = scale * (pulled - first - hat * second)
    return back, jnp.sum(grads * hat, axis=0), jnp.sum(grads, axis=0)


def swap(value, axis, size, bit):
    return lax.ppermute(value, axis, [(i, i ^ bit) for i in range(size)])


def butterfly_sum(value, sizes):
    for axis, size in sizes:
        bit = 1
        while bit < size:
            value = value + swap(value, axis, size, bit)
            bit *= 2
    return value


def pick(value, index, axis):
    return lax.dynamic_index_in_dim(value, index, axis, keepdims=False)


def fence(*values):
    return lax.optimization_barrier(values)


class Partial:
    def __init__(self, value, sizes, blocks=1):
        dp_size, inner = sizes
        keys, places = ["block"], {}
        for axis, size in (("dp", dp_size), ("fsdp", inner)):
            bit = size // 2
            while bit:
                keys.append((axis, bit))
                places[(axis, bit)] = (lax.axis_index(axis) // bit) % 2
                bit //= 2
        own = value.shape[0] // (blocks * dp_size * inner)
        self.sizes = {"dp": dp_size, "fsdp": inner}
        self.keys, self.places = keys, places
        bits = (2,) * (len(keys) - 1)
        self.terms = [value.reshape((blocks,) + bits + (own, value.shape[1]))]

    def total(self, terms):
        wide = [term.astype(jnp.float32) for term in terms]
        return functools.reduce(jnp.add, wide)

    def send(self, key):
        return self.fly(self.cut(key), key)

    def fly(self, load, key):
        return swap(load, key[0], self.sizes[key[0]], key[1])

    def cut(self, key):
        axis = self.keys.index(key)
        self.keys.remove(key)
        out = self.total([pick(term, 1 - self.places[key], axis) for term in self.terms])
        self.terms = [pick(term, self.places[key], axis) for term in self.terms]
        return out.astype(jnp.bfloat16)

    def take(self, received):
        self.terms.append(received)

    def rest(self):
        return self.total(self.terms).astype(jnp.bfloat16)


CORE = ("dp", 1)
ACROSS = ("dp", 2)


def scatter(parts, sizes):
    inner = sizes[1]
    rests = []
    for part in parts:
        rest = part.rest()
        blocks, (own, columns) = rest.shape[0], rest.shape[-2:]
        rest = rest.reshape(blocks, inner, own, columns).transpose(1, 0, 2, 3)
        rests.append(rest.reshape(inner, blocks * own, columns))
    packed = rests[0] if len(rests) == 1 else jnp.concatenate(rests, axis=1)
    summed = lax.psum_scatter(
        packed.reshape(-1, columns), "fsdp", scatter_dimension=0, tiled=True
    ).astype(jnp.float32)
    own = summed.shape[0] // len(parts)
    return [summed[i * own : (i + 1) * own] for i in range(len(parts))]


def side_by_side_kernel(own, blocks, rows_ref, out_ref):
    width = rows_ref.shape[1]
    for device in range(out_ref.shape[0] // own):
        for block in range(blocks):
            first = (device * blocks + block) * own
            out_ref[device * own : (device + 1) * own, block * width : (block + 1) * width] = (
                rows_ref[first : first + own, :]
            )


def side_by_side(far, own, blocks, devices=4):
    _, rows, width = far.shape
    step = devices * own
    return pl.pallas_call(
        functools.partial(side_by_side_kernel, own, blocks),
        out_shape=jax.ShapeDtypeStruct((rows // blocks, blocks * width), far.dtype),
        grid=(rows // (blocks * step),),
        in_specs=[pl.BlockSpec((None, blocks * step, width), lambda i: (1, i, 0))],
        out_specs=pl.BlockSpec((step, blocks * width), lambda i: (i, 0)),
        cost_estimate=cost(0, 4 * rows * width, 0),
        name="side_by_side",
    )(far)


def layer(
    sizes, block_in, images, segment_ids, page_map, ln1_gain, ln1_shift, ln2_gain, ln2_shift,
    ln3_gain, ln3_shift, self_query, self_key, self_value, self_out, cross_query, cross_key,
    cross_value, cross_out, mlp_in, mlp_out, cotangent,
):
    dp_size, inner = sizes
    axes = (("dp", dp_size), ("fsdp", inner))
    _, length, width = block_in.shape
    low = jnp.bfloat16

    def turned(master):
        return master.astype(low).T

    def gather(*masters):
        stacked = jnp.stack([turned(m) for m in masters])
        return lax.all_gather(stacked, AXES, axis=1, tiled=True)

    norms = jnp.stack([ln1_gain, ln1_shift, ln2_gain, ln2_shift, ln3_gain, ln3_shift])
    norms = norms.astype(low).astype(jnp.float32)
    mine = norms.shape[1]
    offset = (lax.axis_index("dp") * inner + lax.axis_index("fsdp")) * mine
    spread = lax.dynamic_update_slice(jnp.zeros((6, width), jnp.float32), norms, (0, offset))
    norms = butterfly_sum(spread, axes)
    near = gather(
        self_query, self_key, self_value, self_out, cross_query, cross_key, cross_value, cross_out
    )
    w_sqkv, w_kv = near[:3], near[5:7]
    w_so, w_cq, w_ck, w_cv, w_co = [near[i] for i in range(3, 8)]
    own = mlp_out.shape[1]
    blocks = mlp_out.shape[0] // width
    out_rows = turned(mlp_out).reshape(own, blocks, width).transpose(1, 0, 2)
    far = jnp.stack([turned(mlp_in), out_rows.reshape(blocks * own, width)])
    far = lax.all_gather(far, AXES, axis=1, tiled=True)
    w_in = far[0]
    w_out = side_by_side(far, own, blocks)

    starts = jnp.sum(
        segment_ids[0][None, :] < jnp.arange(page_map.shape[1] + 1, dtype=jnp.int32)[:, None],
        axis=1,
    ).astype(jnp.int32)
    pages = page_map[0]
    most = LONGEST // QB + 1

    rows = block_in[0].astype(jnp.float32)
    a1 = (normalise(rows)[0] * norms[0] + norms[1]).astype(low)
    sq, sk, sv = [contract(a1, w_sqkv[i], (1,), (1,), low) for i in range(3)]
    so, s_stats = self_forward(starts, sq, sk, sv, most)
    x1 = row_major(rows + contract(so, w_so, (0,), (1,)))
    a2 = (normalise(x1)[0] * norms[2] + norms[3]).astype(low)
    cq = contract(a2, w_cq, (1,), (1,), low)
    ck = contract(images, w_ck, (2,), (1,), low)
    cv = contract(images, w_cv, (2,), (1,), low)
    co, c_stats = cross_forward(starts, pages, cq, ck, cv)
    x2 = row_major(x1 + contract(co, w_co, (0,), (1,)))
    a3 = (normalise(x2)[0] * norms[4] + norms[5]).astype(low)
    u = contract(a3, w_in, (1,), (1,))
    phi = 0.5 * (1.0 + lax.erf(u * ROOT_HALF))
    hidden = (u * phi).astype(low)
    slope = (phi + u * (ROOT_TAU * jnp.exp(-0.5 * u * u))).astype(low)

    eb = cotangent[0]
    e = eb.astype(jnp.float32)
    g_out = contract(eb, hidden, (0,), (0,), low)
    p_out = Partial(g_out, sizes)
    flying = p_out.send(CORE)
    eb, hidden, g_out = fence(eb, hidden, g_out)
    du = (contract(eb, w_out, (1,), (0,)) * slope.astype(jnp.float32)).astype(low)
    du, flying = fence(du, flying)
    p_out.take(flying)
    flying = p_out.send(ACROSS)
    g_in = contract(du, a3, (0,), (0,), low)
    du, g_in = fence(du, g_in)
    p_in = Partial(g_in, sizes)
    flying_in = p_in.send(CORE)
    d3 = contract(du, w_in, (1,), (0,))
    back, gg3, gs3 = norm_back(x2, norms[4], d3)
    e2 = e + back
    e2b = e2.astype(low)
    e2, e2b, flying_in = fence(e2, e2b, flying_in)
    p_in.take(flying_in)
    flying_in = p_in.send(ACROSS)
    d_co = contract(e2b, w_co, (1,), (0,), low)
    dcq, dck, dcv = cross_backward(starts, pages, cq, ck, cv, d_co, c_stats)
    dcq, dck, dcv, flying, flying_in = fence(dcq, dck, dcv, flying, flying_in)
    p_out.take(flying)
    (g_mlp_out,) = scatter([p_out], sizes)
    p_in.take(flying_in)
    (g_mlp_in,) = scatter([p_in], sizes)
    g_co = contract(e2b, co, (0,), (1,), low)
    g_cq = contract(dcq, a2, (1,), (0,), low)
    g_ck = contract(dck, images, (0, 1), (0, 1), low)
    g_cv = contract(dcv, images, (0, 1), (0, 1), low)
    dcq, g_cq, g_ck, g_cv, g_co = fence(dcq, g_cq, g_ck, g_cv, g_co)
    p_cross = [Partial(g, sizes) for g in (g_cq, g_ck, g_cv, g_co)]
    flying = [p.send(CORE) for p in p_cross]
    d2 = contract(dcq, w_cq, (0,), (0,))
    back, gg2, gs2 = norm_back(x1, norms[2], d2)
    e1 = e2 + back
    e1b = e1.astype(low)
    e1, e1b, *flying = fence(e1, e1b, *flying)
    for p, f in zip(p_cross, flying):
        p.take(f)
    flying = [p.send(ACROSS) for p in p_cross]
    g_so = contract(e1b, so, (0,), (1,), low)
    d_so = contract(e1b, w_so, (1,), (0,), low)
    dsq, dsk, dsv = self_backward(starts, sq, sk, sv, d_so, s_stats, most)
    dsq, dsk, dsv, g_so, *flying = fence(dsq, dsk, dsv, g_so, *flying)
    for p, f in zip(p_cross, flying):
        p.take(f)
    g_cross = scatter(p_cross, sizes)
    g_sq = contract(dsq, a1, (1,), (0,), low)
    g_sk = contract(dsk, a1, (0,), (0,), low)
    g_sv = contract(dsv, a1, (0,), (0,), low)
    pairs = (jnp.concatenate([g_sq, g_sk]), jnp.concatenate([g_sv, g_so]))
    dsq, dsk, dsv, *pairs = fence(dsq, dsk, dsv, *pairs)
    groups = [Partial(pair, sizes, 2) for pair in pairs]
    keys = [("fsdp", 1 << i) for i in range(inner.bit_length() - 1)]
    orders = [[ACROSS] + keys, keys[:-1] + [ACROSS] + keys[-1:]]
    flights = [g.send(CORE) for g in groups]
    d1 = (
        contract(dsq, w_sqkv[0], (0,), (0,))
        + contract(dsk, w_sqkv[1], (1,), (0,))
        + contract(dsv, w_sqkv[2], (1,), (0,))
    )

    def norm_one(d1):
        back, gg1, gs1 = norm_back(rows, norms[0], d1)
        return e1 + back, gg1, gs1

    def image_grads(dck, dcv):
        both = jnp.concatenate([dck, dcv], axis=2).transpose(1, 0, 2)
        tokens, count, _ = both.shape
        flat = contract(
            both.reshape(tokens * count, 2 * width), w_kv.reshape(2 * width, width), (1,), (0,)
        )
        return flat.reshape(tokens, count, width)

    def finish(hidden):
        return (x2 + contract(hidden, w_out, (1,), (1,))).astype(low)

    grad_in, gg1, gs1 = norm_one(d1)
    grad_in, hidden, dck, dcv, *flights = fence(grad_in, hidden, dck, dcv, *flights)
    for stage in range(len(keys) + 1):
        for g, f in zip(groups, flights):
            g.take(f)
        loads = [g.cut(o[stage]) for g, o in zip(groups, orders)]
        if stage == 0:
            dck, dcv, *loads = fence(dck, dcv, *loads)
        if stage == 1:
            hidden, *loads = fence(hidden, *loads)
        flights = [g.fly(load, o[stage]) for g, load, o in zip(groups, loads, orders)]
        if stage == 0:
            grad_images = image_grads(dck, dcv).transpose(1, 0, 2)
            grad_images, *flights = fence(grad_images, *flights)
        if stage == 1:
            block_out, *flights = fence(finish(hidden), *flights)
    for g, f in zip(groups, flights):
        g.take(f)
    g_self = [g.total(g.terms)[i] for g in groups for i in range(2)]
    norm_grads = butterfly_sum(jnp.stack([gg1, gs1, gg2, gs2, gg3, gs3]), axes)
    norm_grads = lax.dynamic_slice(norm_grads, (0, offset), (6, mine))
    weight_grads = [g.T for g in g_self + g_cross + [g_mlp_in, g_mlp_out]]
    return (
        block_out[None], grad_in[None], grad_images, *[norm_grads[i] for i in range(6)],
        *weight_grads,
    )


def solution(mesh):
    sizes = (mesh.shape["dp"], mesh.shape["fsdp"])
    rows3 = P(AXES, None, None)
    rows2 = P(AXES, None)
    vector = P(AXES)
    columns = P(None, AXES)
    return jax.shard_map(
        functools.partial(layer, sizes),
        mesh=mesh,
        in_specs=(rows3, rows3, rows2, rows2) + (vector,) * 6 + (columns,) * 10 + (rows3,),
        out_specs=(rows3,) * 3 + (vector,) * 6 + (columns,) * 10,
        check_vma=False,
    )
```

```python
import functools
import jax
import jax.numpy as jnp
from jax import lax
from jax.experimental import pallas as pl
from jax.experimental.layout import Layout, with_layout_constraint
from jax.experimental.pallas import tpu as pltpu
from jax.sharding import PartitionSpec as P

LANES = 128
HALF = 64
QB = 128


def dot_nt(a, b):
    return lax.dot_general(a, b, (((1,), (1,)), ((), ())), preferred_element_type=jnp.float32)


def dot_nn(a, b):
    return lax.dot_general(a, b, (((1,), (0,)), ((), ())), preferred_element_type=jnp.float32)


def head_stack(block, scale=None):
    lane = lax.broadcasted_iota(jnp.int32, block.shape, 1)
    wide = block.astype(jnp.float32)
    if scale is not None:
        wide = wide * scale
    first = jnp.where(lane < HALF, wide, 0.0).astype(jnp.bfloat16)
    second = jnp.where(lane < HALF, 0.0, wide).astype(jnp.bfloat16)
    return jnp.concatenate([first, second], axis=0)


def twice(row):
    return jnp.concatenate([row, row], axis=1)


def diagonal(pair):
    return jnp.concatenate([pair[:HALF, :QB], pair[HALF:, QB:]], axis=0)


def attend(scores, values_turned):
    peaks = [jnp.max(s, axis=0, keepdims=True) for s in scores]
    raised = [jnp.exp(s - peak) for s, peak in zip(scores, peaks)]
    totals = [jnp.sum(r, axis=0, keepdims=True) for r in raised]
    low = [(r * (1.0 / total)).astype(jnp.bfloat16) for r, total in zip(raised, totals)]
    mixed = [diagonal(dot_nn(vt, p)).astype(jnp.bfloat16) for vt, p in zip(values_turned, low)]
    stats = []
    for peak, total in zip(peaks, totals):
        lse = peak + jnp.log(total)
        stats += [lse[:, :QB], lse[:, QB:]]
    return mixed, jnp.concatenate(stats, axis=0)


def pull_back(scores, values_in, pulled, stats, keys_turned):
    attention = [
        jnp.exp(s - jnp.concatenate([stats[2 * i : 2 * i + 1], stats[2 * i + 1 : 2 * i + 2]], axis=1))
        for i, s in enumerate(scores)
    ]
    low = [a.astype(jnp.bfloat16) for a in attention]
    pushed = [dot_nt(v, g) for v, g in zip(values_in, pulled)]
    inner = [jnp.sum(a * p, axis=0, keepdims=True) for a, p in zip(attention, pushed)]
    grads = [
        (a * (p - i)).astype(jnp.bfloat16) for a, p, i in zip(attention, pushed, inner)
    ]
    turned = [
        diagonal(dot_nn(kt, g) * 0.125).astype(jnp.bfloat16) for kt, g in zip(keys_turned, grads)
    ]
    return low, grads, turned


def query_places(block):
    return block * QB + lax.broadcasted_iota(jnp.int32, (1, QB), 1)


def cross_forward_kernel(pairs, starts, pages, q_ref, k_ref, v_ref, o_ref, l_ref, vt_ref):
    page_count = k_ref.shape[0]
    for page in range(page_count):
        image = pages[page]
        low, high = starts[page], starts[page + 1]
        for pair in range(pairs):
            lanes = slice(pair * LANES, (pair + 1) * LANES)
            vt_ref[pair] = flip(v_ref[image, :, lanes])

        def body(block, carry):
            rows = pl.ds(pl.multiple_of(block * QB, QB), QB)
            place = query_places(block)
            member = (place >= low) & (place < high)
            spans = [slice(pair * LANES, (pair + 1) * LANES) for pair in range(pairs)]
            scores = [
                dot_nt(k_ref[image, :, lanes], head_stack(q_ref[rows, lanes], 0.125))
                for lanes in spans
            ]
            mixed, stats = attend(scores, [vt_ref[pair] for pair in range(pairs)])
            for lanes, block_out in zip(spans, mixed):
                o_ref[lanes, rows] = jnp.where(member, block_out, o_ref[lanes, rows])
            l_ref[0, :, rows] = jnp.where(member, stats, l_ref[0, :, rows])
            return carry

        lax.fori_loop(low // QB, (high - 1) // QB + 1, body, 0)


def flip(block):
    return jnp.transpose(block)


def cross_backward_kernel(
    pairs, starts, pages, q_ref, k_ref, v_ref, g_ref, l_ref, dq_ref, dk_ref, dv_ref,
    kt_ref, dka_ref, dva_ref,
):
    page_count = k_ref.shape[0]
    for page in range(page_count):
        image = pages[page]
        low, high = starts[page], starts[page + 1]
        for pair in range(pairs):
            lanes = slice(pair * LANES, (pair + 1) * LANES)
            kt_ref[pair] = flip(k_ref[image, :, lanes])
            dka_ref[pair] = jnp.zeros(dka_ref.shape[1:], jnp.float32)
            dva_ref[pair] = jnp.zeros(dva_ref.shape[1:], jnp.float32)

        def body(block, carry):
            rows = pl.ds(pl.multiple_of(block * QB, QB), QB)
            place = query_places(block)
            member = (place >= low) & (place < high)
            spans = [slice(pair * LANES, (pair + 1) * LANES) for pair in range(pairs)]
            stacked = [head_stack(q_ref[rows, lanes], 0.125) for lanes in spans]
            pulled = [head_stack(g_ref[rows, lanes]) for lanes in spans]
            stats = jnp.where(member, l_ref[0, :, rows], 1e30)
            keys_in = [k_ref[image, :, lanes] for lanes in spans]
            values_in = [v_ref[image, :, lanes] for lanes in spans]
            soft, grads, turned = pull_back(
                [dot_nt(k, q) for k, q in zip(keys_in, stacked)], values_in, pulled, stats,
                [kt_ref[pair] for pair in range(pairs)],
            )
            for pair, lanes in enumerate(spans):
                dq_ref[lanes, rows] = jnp.where(member, turned[pair], dq_ref[lanes, rows])
            for pair in range(pairs):
                dva_ref[pair] += dot_nn(soft[pair], pulled[pair])
            for pair in range(pairs):
                dka_ref[pair] += dot_nn(grads[pair], stacked[pair])
            return carry

        lax.fori_loop(low // QB, (high - 1) // QB + 1, body, 0)
        for pair in range(pairs):
            lanes = slice(pair * LANES, (pair + 1) * LANES)
            dk_ref[image, :, lanes] = dka_ref[pair].astype(jnp.bfloat16)
            dv_ref[image, :, lanes] = dva_ref[pair].astype(jnp.bfloat16)


def self_window(starts, block):
    start = starts[0]
    for page in range(1, starts.shape[0] - 1):
        start = jnp.where(starts[page] <= block * QB, starts[page], start)
    first = start // QB
    return first, block + 1 - first


def self_allowed(starts, place, first, chunks):
    begin = jnp.zeros(place.shape, jnp.int32)
    for page in range(1, starts.shape[0] - 1):
        begin = jnp.where(place >= starts[page], starts[page], begin)
    begin, end = twice(begin), twice(place)
    key = first * QB + lax.broadcasted_iota(jnp.int32, (chunks * QB, 2 * QB), 0)
    return (key >= begin) & (key <= end)


def self_forward_kernel(pairs, most, starts, q_ref, k_ref, v_ref, o_ref, l_ref, vt_ref):
    for pair in range(pairs):
        lanes = slice(pair * LANES, (pair + 1) * LANES)
        vt_ref[pair] = flip(v_ref[:, lanes])

    def body(block, carry):
        rows = pl.ds(pl.multiple_of(block * QB, QB), QB)
        first, count = self_window(starts, block)
        for chunks in range(1, most + 1):

            @pl.when(count == chunks)
            def _():
                keys = pl.ds(pl.multiple_of(first * QB, QB), chunks * QB)
                allowed = self_allowed(starts, query_places(block), first, chunks)
                spans = [slice(pair * LANES, (pair + 1) * LANES) for pair in range(pairs)]
                scores = [
                    jnp.where(
                        allowed, dot_nt(k_ref[keys, lanes], head_stack(q_ref[rows, lanes], 0.125)), -1e30
                    )
                    for lanes in spans
                ]
                mixed, stats = attend(scores, [vt_ref[pair, :, keys] for pair in range(pairs)])
                for lanes, block_out in zip(spans, mixed):
                    o_ref[lanes, rows] = block_out
                l_ref[0, :, rows] = stats

        return carry

    lax.fori_loop(0, q_ref.shape[0] // QB, body, 0)


def self_backward_kernel(
    pairs, most, starts, q_ref, k_ref, v_ref, g_ref, l_ref, dq_ref, dk_ref, dv_ref,
    kt_ref, dka_ref, dva_ref,
):
    for pair in range(pairs):
        lanes = slice(pair * LANES, (pair + 1) * LANES)
        kt_ref[pair] = flip(k_ref[:, lanes])
    dka_ref[...] = jnp.zeros(dka_ref.shape, jnp.float32)
    dva_ref[...] = jnp.zeros(dva_ref.shape, jnp.float32)

    def body(block, carry):
        rows = pl.ds(pl.multiple_of(block * QB, QB), QB)
        first, count = self_window(starts, block)
        for chunks in range(1, most + 1):

            @pl.when(count == chunks)
            def _():
                keys = pl.ds(pl.multiple_of(first * QB, QB), chunks * QB)
                allowed = self_allowed(starts, query_places(block), first, chunks)
                spans = [slice(pair * LANES, (pair + 1) * LANES) for pair in range(pairs)]
                stacked = [head_stack(q_ref[rows, lanes], 0.125) for lanes in spans]
                pulled = [head_stack(g_ref[rows, lanes]) for lanes in spans]
                scores = [
                    jnp.where(allowed, dot_nt(k_ref[keys, lanes], q), -1e30)
                    for lanes, q in zip(spans, stacked)
                ]
                soft, grads, turned = pull_back(
                    scores, [v_ref[keys, lanes] for lanes in spans], pulled, l_ref[0, :, rows],
                    [kt_ref[pair, :, keys] for pair in range(pairs)],
                )
                for pair, lanes in enumerate(spans):
                    dq_ref[lanes, rows] = turned[pair]
                for pair in range(pairs):
                    dva_ref[pair, keys, :] += dot_nn(soft[pair], pulled[pair])
                for pair in range(pairs):
                    dka_ref[pair, keys, :] += dot_nn(grads[pair], stacked[pair])

        return carry

    lax.fori_loop(0, q_ref.shape[0] // QB, body, 0)
    for pair in range(pairs):
        lanes = slice(pair * LANES, (pair + 1) * LANES)
        dk_ref[:, lanes] = dka_ref[pair].astype(jnp.bfloat16)
        dv_ref[:, lanes] = dva_ref[pair].astype(jnp.bfloat16)


def cost(flops, bytes_accessed, exps):
    return pl.CostEstimate(flops=flops, bytes_accessed=bytes_accessed, transcendentals=exps)


def specs(pairs, prefetch):
    wide = pairs * LANES

    def at(index):
        return lambda step, *scalars: index(step)

    return {
        "rows": lambda length: pl.BlockSpec((length, wide), at(lambda i: (0, i))),
        "turned": lambda length: pl.BlockSpec((wide, length), at(lambda i: (i, 0))),
        "images": lambda count, tokens: pl.BlockSpec((count, tokens, wide), at(lambda i: (0, 0, i))),
        "stats": lambda length: pl.BlockSpec((1, 2 * pairs, length), at(lambda i: (i, 0, 0))),
    }


def cross_forward(starts, pages, queries, keys_all, values_all, pairs=4):
    length, width = queries.shape
    count, tokens, _ = keys_all.shape
    steps = width // (pairs * LANES)
    s = specs(pairs, 2)
    return pl.pallas_call(
        functools.partial(cross_forward_kernel, pairs),
        out_shape=(
            jax.ShapeDtypeStruct((width, length), jnp.bfloat16),
            jax.ShapeDtypeStruct((steps, 2 * pairs, length), jnp.float32),
        ),
        grid_spec=pltpu.PrefetchScalarGridSpec(
            num_scalar_prefetch=2,
            grid=(steps,),
            in_specs=[s["rows"](length), s["images"](count, tokens), s["images"](count, tokens)],
            out_specs=[s["turned"](length), s["stats"](length)],
            scratch_shapes=[pltpu.VMEM((pairs, LANES, tokens), jnp.bfloat16)],
        ),
        cost_estimate=cost(11 * 128 * tokens * width * 4 * 4, 20 * 2**20, 2**24),
        name="cross_forward",
    )(starts, pages, queries, keys_all, values_all)


def cross_backward(starts, pages, queries, keys_all, values_all, grads, stats, pairs=4):
    length, width = queries.shape
    count, tokens, _ = keys_all.shape
    steps = width // (pairs * LANES)
    s = specs(pairs, 2)
    image_spec = s["images"](count, tokens)
    return pl.pallas_call(
        functools.partial(cross_backward_kernel, pairs),
        out_shape=(
            jax.ShapeDtypeStruct((width, length), jnp.bfloat16),
            jax.ShapeDtypeStruct(keys_all.shape, jnp.bfloat16),
            jax.ShapeDtypeStruct(values_all.shape, jnp.bfloat16),
        ),
        grid_spec=pltpu.PrefetchScalarGridSpec(
            num_scalar_prefetch=2,
            grid=(steps,),
            in_specs=[s["rows"](length), image_spec, image_spec, s["rows"](length), s["stats"](length)],
            out_specs=[s["turned"](length), image_spec, image_spec],
            scratch_shapes=[
                pltpu.VMEM((pairs, LANES, tokens), jnp.bfloat16),
                pltpu.VMEM((pairs, tokens, LANES), jnp.float32),
                pltpu.VMEM((pairs, tokens, LANES), jnp.float32),
            ],
        ),
        cost_estimate=cost(11 * 128 * tokens * width * 10 * 4, 30 * 2**20, 2**24),
        name="cross_backward",
    )(starts, pages, queries, keys_all, values_all, grads, stats)


def self_forward(starts, queries, keys_all, values_all, most, pairs=4):
    length, width = queries.shape
    steps = width // (pairs * LANES)
    s = specs(pairs, 1)
    rows = s["rows"](length)
    return pl.pallas_call(
        functools.partial(self_forward_kernel, pairs, most),
        out_shape=(
            jax.ShapeDtypeStruct((width, length), jnp.bfloat16),
            jax.ShapeDtypeStruct((steps, 2 * pairs, length), jnp.float32),
        ),
        grid_spec=pltpu.PrefetchScalarGridSpec(
            num_scalar_prefetch=1,
            grid=(steps,),
            in_specs=[rows, rows, rows],
            out_specs=[s["turned"](length), s["stats"](length)],
            scratch_shapes=[pltpu.VMEM((pairs, LANES, length), jnp.bfloat16)],
        ),
        cost_estimate=cost(20 * 128 * 128 * width * 4 * 4, 10 * 2**20, 2**23),
        name="self_forward",
    )(starts, queries, keys_all, values_all)


def self_backward(starts, queries, keys_all, values_all, grads, stats, most, pairs=4):
    length, width = queries.shape
    steps = width // (pairs * LANES)
    s = specs(pairs, 1)
    rows = s["rows"](length)
    return pl.pallas_call(
        functools.partial(self_backward_kernel, pairs, most),
        out_shape=(
            jax.ShapeDtypeStruct((width, length), jnp.bfloat16),
            jax.ShapeDtypeStruct((length, width), jnp.bfloat16),
            jax.ShapeDtypeStruct((length, width), jnp.bfloat16),
        ),
        grid_spec=pltpu.PrefetchScalarGridSpec(
            num_scalar_prefetch=1,
            grid=(steps,),
            in_specs=[rows, rows, rows, rows, s["stats"](length)],
            out_specs=[s["turned"](length), rows, rows],
            scratch_shapes=[
                pltpu.VMEM((pairs, LANES, length), jnp.bfloat16),
                pltpu.VMEM((pairs, length, LANES), jnp.float32),
                pltpu.VMEM((pairs, length, LANES), jnp.float32),
            ],
        ),
        cost_estimate=cost(20 * 128 * 128 * width * 10 * 4, 16 * 2**20, 2**23),
        name="self_backward",
    )(starts, queries, keys_all, values_all, grads, stats)


EPSILON = 1e-05
ROOT_HALF = 0.7071067811865476
ROOT_TAU = 0.3989422804014327
AXES = ("dp", "fsdp")
LONGEST = 512


def contract(a, b, left, right, out=jnp.float32):
    return lax.dot_general(
        a, b, ((left, right), ((), ())), preferred_element_type=jnp.float32
    ).astype(out)


def row_major(values):
    return with_layout_constraint(values, Layout(major_to_minor=(0, 1)))


def normalise(values):
    average = jnp.mean(values, axis=-1, keepdims=True)
    centered = values - average
    variance = jnp.mean(centered * centered, axis=-1, keepdims=True)
    scale = lax.rsqrt(variance + EPSILON)
    return centered * scale, scale


def norm_back(values, gain, grads):
    hat, scale = normalise(values)
    pulled = grads * gain
    first = jnp.mean(pulled, axis=-1, keepdims=True)
    second = jnp.mean(pulled * hat, axis=-1, keepdims=True)
    back = scale * (pulled - first - hat * second)
    return back, jnp.sum(grads * hat, axis=0), jnp.sum(grads, axis=0)


def swap(value, axis, size, bit):
    return lax.ppermute(value, axis, [(i, i ^ bit) for i in range(size)])


def butterfly_sum(value, sizes):
    for axis, size in sizes:
        bit = 1
        while bit < size:
            value = value + swap(value, axis, size, bit)
            bit *= 2
    return value


def pick(value, index, axis):
    return lax.dynamic_index_in_dim(value, index, axis, keepdims=False)


def fence(*values):
    return lax.optimization_barrier(values)


class Partial:
    def __init__(self, value, sizes, blocks=1):
        dp_size, inner = sizes
        keys, places = ["block"], {}
        for axis, size in (("dp", dp_size), ("fsdp", inner)):
            bit = size // 2
            while bit:
                keys.append((axis, bit))
                places[(axis, bit)] = (lax.axis_index(axis) // bit) % 2
                bit //= 2
        own = value.shape[0] // (blocks * dp_size * inner)
        self.sizes = {"dp": dp_size, "fsdp": inner}
        self.keys, self.places = keys, places
        bits = (2,) * (len(keys) - 1)
        self.terms = [value.reshape((blocks,) + bits + (own, value.shape[1]))]

    def total(self, terms):
        wide = [term.astype(jnp.float32) for term in terms]
        return functools.reduce(jnp.add, wide)

    def send(self, key):
        return self.fly(self.cut(key), key)

    def fly(self, load, key):
        return swap(load, key[0], self.sizes[key[0]], key[1])

    def cut(self, key):
        axis = self.keys.index(key)
        self.keys.remove(key)
        out = self.total([pick(term, 1 - self.places[key], axis) for term in self.terms])
        self.terms = [pick(term, self.places[key], axis) for term in self.terms]
        return out.astype(jnp.bfloat16)

    def take(self, received):
        self.terms.append(received)

    def rest(self):
        return self.total(self.terms).astype(jnp.bfloat16)


CORE = ("dp", 1)
ACROSS = ("dp", 2)


def scatter(parts, sizes):
    inner = sizes[1]
    rests = []
    for part in parts:
        rest = part.rest()
        blocks, (own, columns) = rest.shape[0], rest.shape[-2:]
        rest = rest.reshape(blocks, inner, own, columns).transpose(1, 0, 2, 3)
        rests.append(rest.reshape(inner, blocks * own, columns))
    packed = rests[0] if len(rests) == 1 else jnp.concatenate(rests, axis=1)
    summed = lax.psum_scatter(
        packed.reshape(-1, columns), "fsdp", scatter_dimension=0, tiled=True
    ).astype(jnp.float32)
    own = summed.shape[0] // len(parts)
    return [summed[i * own : (i + 1) * own] for i in range(len(parts))]


def side_by_side_kernel(own, blocks, rows_ref, out_ref):
    width = rows_ref.shape[1]
    for device in range(out_ref.shape[0] // own):
        for block in range(blocks):
            first = (device * blocks + block) * own
            out_ref[device * own : (device + 1) * own, block * width : (block + 1) * width] = (
                rows_ref[first : first + own, :]
            )


def side_by_side(far, own, blocks, devices=4):
    _, rows, width = far.shape
    step = devices * own
    return pl.pallas_call(
        functools.partial(side_by_side_kernel, own, blocks),
        out_shape=jax.ShapeDtypeStruct((rows // blocks, blocks * width), far.dtype),
        grid=(rows // (blocks * step),),
        in_specs=[pl.BlockSpec((None, blocks * step, width), lambda i: (1, i, 0))],
        out_specs=pl.BlockSpec((step, blocks * width), lambda i: (i, 0)),
        cost_estimate=cost(0, 4 * rows * width, 0),
        name="side_by_side",
    )(far)


def lower_stack_kernel(*refs):
    for i, master in enumerate(refs[:-1]):
        refs[-1][i] = master[...].astype(refs[-1].dtype)


def lower_stack(masters):
    rows, width = masters[0].shape
    count = len(masters)
    return pl.pallas_call(
        lower_stack_kernel,
        out_shape=jax.ShapeDtypeStruct((count, rows, width), jnp.bfloat16),
        cost_estimate=cost(0, 6 * count * rows * width, 0),
        name="lower_stack",
    )(*masters)


def layer(
    sizes, block_in, images, segment_ids, page_map, ln1_gain, ln1_shift, ln2_gain, ln2_shift,
    ln3_gain, ln3_shift, self_query, self_key, self_value, self_out, cross_query, cross_key,
    cross_value, cross_out, mlp_in, mlp_out, cotangent,
):
    dp_size, inner = sizes
    axes = (("dp", dp_size), ("fsdp", inner))
    _, length, width = block_in.shape
    low = jnp.bfloat16

    def turned(master):
        return master.astype(low).T

    def gather(*masters):
        return lax.all_gather(lower_stack([m.T for m in masters]), AXES, axis=1, tiled=True)

    norms = jnp.stack([ln1_gain, ln1_shift, ln2_gain, ln2_shift, ln3_gain, ln3_shift])
    norms = norms.astype(low).astype(jnp.float32)
    mine = norms.shape[1]
    offset = (lax.axis_index("dp") * inner + lax.axis_index("fsdp")) * mine
    spread = lax.dynamic_update_slice(jnp.zeros((6, width), jnp.float32), norms, (0, offset))
    norms = butterfly_sum(spread, axes)
    near = gather(
        self_query, self_key, self_value, self_out, cross_query, cross_key, cross_value, cross_out
    )
    w_sqkv, w_kv = near[:3], near[5:7]
    w_so, w_cq, w_ck, w_cv, w_co = [near[i] for i in range(3, 8)]
    own = mlp_out.shape[1]
    blocks = mlp_out.shape[0] // width
    out_rows = turned(mlp_out).reshape(own, blocks, width).transpose(1, 0, 2)
    far = jnp.stack([turned(mlp_in), out_rows.reshape(blocks * own, width)])
    far = lax.all_gather(far, AXES, axis=1, tiled=True)
    w_in = far[0]
    w_out = side_by_side(far, own, blocks)

    starts = jnp.sum(
        segment_ids[0][None, :] < jnp.arange(page_map.shape[1] + 1, dtype=jnp.int32)[:, None],
        axis=1,
    ).astype(jnp.int32)
    pages = page_map[0]
    most = LONGEST // QB + 1

    rows = block_in[0].astype(jnp.float32)
    a1 = (normalise(rows)[0] * norms[0] + norms[1]).astype(low)
    sq, sk, sv = [contract(a1, w_sqkv[i], (1,), (1,), low) for i in range(3)]
    so, s_stats = self_forward(starts, sq, sk, sv, most)
    x1 = row_major(rows + contract(so, w_so, (0,), (1,)))
    a2 = (normalise(x1)[0] * norms[2] + norms[3]).astype(low)
    cq = contract(a2, w_cq, (1,), (1,), low)
    ck = contract(images, w_ck, (2,), (1,), low)
    cv = contract(images, w_cv, (2,), (1,), low)
    co, c_stats = cross_forward(starts, pages, cq, ck, cv)
    x2 = row_major(x1 + contract(co, w_co, (0,), (1,)))
    a3 = (normalise(x2)[0] * norms[4] + norms[5]).astype(low)
    u = contract(a3, w_in, (1,), (1,))
    phi = 0.5 * (1.0 + lax.erf(u * ROOT_HALF))
    hidden = (u * phi).astype(low)
    slope = (phi + u * (ROOT_TAU * jnp.exp(-0.5 * u * u))).astype(low)

    eb = cotangent[0]
    e = eb.astype(jnp.float32)
    g_out = contract(eb, hidden, (0,), (0,), low)
    p_out = Partial(g_out, sizes)
    flying = p_out.send(CORE)
    eb, hidden, g_out = fence(eb, hidden, g_out)
    du = (contract(eb, w_out, (1,), (0,)) * slope.astype(jnp.float32)).astype(low)
    du, flying = fence(du, flying)
    p_out.take(flying)
    flying = p_out.send(ACROSS)
    g_in = contract(du, a3, (0,), (0,), low)
    du, g_in = fence(du, g_in)
    p_in = Partial(g_in, sizes)
    flying_in = p_in.send(CORE)
    d3 = contract(du, w_in, (1,), (0,))
    back, gg3, gs3 = norm_back(x2, norms[4], d3)
    e2 = e + back
    e2b = e2.astype(low)
    e2, e2b, flying_in = fence(e2, e2b, flying_in)
    p_in.take(flying_in)
    flying_in = p_in.send(ACROSS)
    d_co = contract(e2b, w_co, (1,), (0,), low)
    dcq, dck, dcv = cross_backward(starts, pages, cq, ck, cv, d_co, c_stats)
    dcq, dck, dcv, flying, flying_in = fence(dcq, dck, dcv, flying, flying_in)
    p_out.take(flying)
    (g_mlp_out,) = scatter([p_out], sizes)
    p_in.take(flying_in)
    (g_mlp_in,) = scatter([p_in], sizes)
    g_co = contract(e2b, co, (0,), (1,), low)
    g_cq = contract(dcq, a2, (1,), (0,), low)
    g_ck = contract(dck, images, (0, 1), (0, 1), low)
    g_cv = contract(dcv, images, (0, 1), (0, 1), low)
    dcq, g_cq, g_ck, g_cv, g_co = fence(dcq, g_cq, g_ck, g_cv, g_co)
    p_cross = [Partial(g, sizes) for g in (g_cq, g_ck, g_cv, g_co)]
    flying = [p.send(CORE) for p in p_cross]
    d2 = contract(dcq, w_cq, (0,), (0,))
    back, gg2, gs2 = norm_back(x1, norms[2], d2)
    e1 = e2 + back
    e1b = e1.astype(low)
    e1, e1b, *flying = fence(e1, e1b, *flying)
    for p, f in zip(p_cross, flying):
        p.take(f)
    flying = [p.send(ACROSS) for p in p_cross]
    g_so = contract(e1b, so, (0,), (1,), low)
    d_so = contract(e1b, w_so, (1,), (0,), low)
    dsq, dsk, dsv = self_backward(starts, sq, sk, sv, d_so, s_stats, most)
    dsq, dsk, dsv, g_so, *flying = fence(dsq, dsk, dsv, g_so, *flying)
    for p, f in zip(p_cross, flying):
        p.take(f)
    g_cross = scatter(p_cross, sizes)
    g_sq = contract(dsq, a1, (1,), (0,), low)
    g_sk = contract(dsk, a1, (0,), (0,), low)
    g_sv = contract(dsv, a1, (0,), (0,), low)
    pairs = (jnp.concatenate([g_sq, g_sk]), jnp.concatenate([g_sv, g_so]))
    dsq, dsk, dsv, *pairs = fence(dsq, dsk, dsv, *pairs)
    groups = [Partial(pair, sizes, 2) for pair in pairs]
    keys = [("fsdp", 1 << i) for i in range(inner.bit_length() - 1)]
    orders = [[ACROSS] + keys, keys[:-1] + [ACROSS] + keys[-1:]]
    flights = [g.send(CORE) for g in groups]
    d1 = (
        contract(dsq, w_sqkv[0], (0,), (0,))
        + contract(dsk, w_sqkv[1], (1,), (0,))
        + contract(dsv, w_sqkv[2], (1,), (0,))
    )

    def norm_one(d1):
        back, gg1, gs1 = norm_back(rows, norms[0], d1)
        return e1 + back, gg1, gs1

    def image_grads(dck, dcv):
        both = jnp.concatenate([dck, dcv], axis=2).transpose(1, 0, 2)
        tokens, count, _ = both.shape
        flat = contract(
            both.reshape(tokens * count, 2 * width), w_kv.reshape(2 * width, width), (1,), (0,)
        )
        return flat.reshape(tokens, count, width)

    def finish(hidden):
        return (x2 + contract(hidden, w_out, (1,), (1,))).astype(low)

    grad_in, gg1, gs1 = norm_one(d1)
    grad_in, hidden, dck, dcv, *flights = fence(grad_in, hidden, dck, dcv, *flights)
    for stage in range(len(keys) + 1):
        for g, f in zip(groups, flights):
            g.take(f)
        loads = [g.cut(o[stage]) for g, o in zip(groups, orders)]
        if stage == 0:
            dck, dcv, *loads = fence(dck, dcv, *loads)
        if stage == 1:
            hidden, *loads = fence(hidden, *loads)
        flights = [g.fly(load, o[stage]) for g, load, o in zip(groups, loads, orders)]
        if stage == 0:
            grad_images = image_grads(dck, dcv).transpose(1, 0, 2)
            grad_images, *flights = fence(grad_images, *flights)
        if stage == 1:
            block_out, *flights = fence(finish(hidden), *flights)
    for g, f in zip(groups, flights):
        g.take(f)
    g_self = [g.total(g.terms)[i] for g in groups for i in range(2)]
    norm_grads = butterfly_sum(jnp.stack([gg1, gs1, gg2, gs2, gg3, gs3]), axes)
    norm_grads = lax.dynamic_slice(norm_grads, (0, offset), (6, mine))
    weight_grads = [g.T for g in g_self + g_cross + [g_mlp_in, g_mlp_out]]
    return (
        block_out[None], grad_in[None], grad_images, *[norm_grads[i] for i in range(6)],
        *weight_grads,
    )


def solution(mesh):
    sizes = (mesh.shape["dp"], mesh.shape["fsdp"])
    rows3 = P(AXES, None, None)
    rows2 = P(AXES, None)
    vector = P(AXES)
    columns = P(None, AXES)
    return jax.shard_map(
        functools.partial(layer, sizes),
        mesh=mesh,
        in_specs=(rows3, rows3, rows2, rows2) + (vector,) * 6 + (columns,) * 10 + (rows3,),
        out_specs=(rows3,) * 3 + (vector,) * 6 + (columns,) * 10,
        check_vma=False,
    )
```

```python
import functools
import jax
import jax.numpy as jnp
from jax import lax
from jax.experimental import pallas as pl
from jax.experimental.layout import Layout, with_layout_constraint
from jax.experimental.pallas import tpu as pltpu
from jax.sharding import PartitionSpec as P

LANES = 128
HALF = 64
QB = 128


def dot_nt(a, b):
    return lax.dot_general(a, b, (((1,), (1,)), ((), ())), preferred_element_type=jnp.float32)


def dot_nn(a, b):
    return lax.dot_general(a, b, (((1,), (0,)), ((), ())), preferred_element_type=jnp.float32)


def head_stack(block, scale=None):
    lane = lax.broadcasted_iota(jnp.int32, block.shape, 1)
    wide = block.astype(jnp.float32)
    if scale is not None:
        wide = wide * scale
    first = jnp.where(lane < HALF, wide, 0.0).astype(jnp.bfloat16)
    second = jnp.where(lane < HALF, 0.0, wide).astype(jnp.bfloat16)
    return jnp.concatenate([first, second], axis=0)


def twice(row):
    return jnp.concatenate([row, row], axis=1)


def diagonal(pair):
    return jnp.concatenate([pair[:HALF, :QB], pair[HALF:, QB:]], axis=0)


def attend(scores, values_turned):
    peaks = [jnp.max(s, axis=0, keepdims=True) for s in scores]
    raised = [jnp.exp(s - peak) for s, peak in zip(scores, peaks)]
    totals = [jnp.sum(r, axis=0, keepdims=True) for r in raised]
    low = [(r * (1.0 / total)).astype(jnp.bfloat16) for r, total in zip(raised, totals)]
    mixed = [diagonal(dot_nn(vt, p)).astype(jnp.bfloat16) for vt, p in zip(values_turned, low)]
    stats = []
    for peak, total in zip(peaks, totals):
        lse = peak + jnp.log(total)
        stats += [lse[:, :QB], lse[:, QB:]]
    return mixed, jnp.concatenate(stats, axis=0)


def pull_back(scores, values_in, pulled, stats, keys_turned):
    attention = [
        jnp.exp(s - jnp.concatenate([stats[2 * i : 2 * i + 1], stats[2 * i + 1 : 2 * i + 2]], axis=1))
        for i, s in enumerate(scores)
    ]
    low = [a.astype(jnp.bfloat16) for a in attention]
    pushed = [dot_nt(v, g) for v, g in zip(values_in, pulled)]
    inner = [jnp.sum(a * p, axis=0, keepdims=True) for a, p in zip(attention, pushed)]
    grads = [
        (a * (p - i)).astype(jnp.bfloat16) for a, p, i in zip(attention, pushed, inner)
    ]
    turned = [
        diagonal(dot_nn(kt, g) * 0.125).astype(jnp.bfloat16) for kt, g in zip(keys_turned, grads)
    ]
    return low, grads, turned


def query_places(block):
    return block * QB + lax.broadcasted_iota(jnp.int32, (1, QB), 1)


def cross_forward_kernel(pairs, starts, pages, q_ref, k_ref, v_ref, o_ref, l_ref, vt_ref):
    page_count = k_ref.shape[0]
    for page in range(page_count):
        image = pages[page]
        low, high = starts[page], starts[page + 1]
        for pair in range(pairs):
            lanes = slice(pair * LANES, (pair + 1) * LANES)
            vt_ref[pair] = flip(v_ref[image, :, lanes])

        def body(block, carry):
            rows = pl.ds(pl.multiple_of(block * QB, QB), QB)
            place = query_places(block)
            member = (place >= low) & (place < high)
            spans = [slice(pair * LANES, (pair + 1) * LANES) for pair in range(pairs)]
            scores = [
                dot_nt(k_ref[image, :, lanes], head_stack(q_ref[rows, lanes], 0.125))
                for lanes in spans
            ]
            mixed, stats = attend(scores, [vt_ref[pair] for pair in range(pairs)])
            for lanes, block_out in zip(spans, mixed):
                o_ref[lanes, rows] = jnp.where(member, block_out, o_ref[lanes, rows])
            l_ref[0, :, rows] = jnp.where(member, stats, l_ref[0, :, rows])
            return carry

        lax.fori_loop(low // QB, (high - 1) // QB + 1, body, 0)


def flip(block):
    return jnp.transpose(block)


def cross_backward_kernel(
    pairs, starts, pages, q_ref, k_ref, v_ref, g_ref, l_ref, dq_ref, dk_ref, dv_ref,
    kt_ref, dka_ref, dva_ref,
):
    page_count = k_ref.shape[0]
    for page in range(page_count):
        image = pages[page]
        low, high = starts[page], starts[page + 1]
        for pair in range(pairs):
            lanes = slice(pair * LANES, (pair + 1) * LANES)
            kt_ref[pair] = flip(k_ref[image, :, lanes])
            dka_ref[pair] = jnp.zeros(dka_ref.shape[1:], jnp.float32)
            dva_ref[pair] = jnp.zeros(dva_ref.shape[1:], jnp.float32)

        def body(block, carry):
            rows = pl.ds(pl.multiple_of(block * QB, QB), QB)
            place = query_places(block)
            member = (place >= low) & (place < high)
            spans = [slice(pair * LANES, (pair + 1) * LANES) for pair in range(pairs)]
            stacked = [head_stack(q_ref[rows, lanes], 0.125) for lanes in spans]
            pulled = [head_stack(g_ref[rows, lanes]) for lanes in spans]
            stats = jnp.where(member, l_ref[0, :, rows], 1e30)
            keys_in = [k_ref[image, :, lanes] for lanes in spans]
            values_in = [v_ref[image, :, lanes] for lanes in spans]
            soft, grads, turned = pull_back(
                [dot_nt(k, q) for k, q in zip(keys_in, stacked)], values_in, pulled, stats,
                [kt_ref[pair] for pair in range(pairs)],
            )
            for pair, lanes in enumerate(spans):
                dq_ref[lanes, rows] = jnp.where(member, turned[pair], dq_ref[lanes, rows])
            for pair in range(pairs):
                dva_ref[pair] += dot_nn(soft[pair], pulled[pair])
            for pair in range(pairs):
                dka_ref[pair] += dot_nn(grads[pair], stacked[pair])
            return carry

        lax.fori_loop(low // QB, (high - 1) // QB + 1, body, 0)
        for pair in range(pairs):
            lanes = slice(pair * LANES, (pair + 1) * LANES)
            dk_ref[image, :, lanes] = dka_ref[pair].astype(jnp.bfloat16)
            dv_ref[image, :, lanes] = dva_ref[pair].astype(jnp.bfloat16)


def self_window(starts, block):
    start = starts[0]
    for page in range(1, starts.shape[0] - 1):
        start = jnp.where(starts[page] <= block * QB, starts[page], start)
    first = start // QB
    return first, block + 1 - first


def self_allowed(starts, place, first, chunks):
    begin = jnp.zeros(place.shape, jnp.int32)
    for page in range(1, starts.shape[0] - 1):
        begin = jnp.where(place >= starts[page], starts[page], begin)
    begin, end = twice(begin), twice(place)
    key = first * QB + lax.broadcasted_iota(jnp.int32, (chunks * QB, 2 * QB), 0)
    return (key >= begin) & (key <= end)


def self_forward_kernel(pairs, most, starts, q_ref, k_ref, v_ref, o_ref, l_ref, vt_ref):
    for pair in range(pairs):
        lanes = slice(pair * LANES, (pair + 1) * LANES)
        vt_ref[pair] = flip(v_ref[:, lanes])

    def body(block, carry):
        rows = pl.ds(pl.multiple_of(block * QB, QB), QB)
        first, count = self_window(starts, block)
        for chunks in range(1, most + 1):

            @pl.when(count == chunks)
            def _():
                keys = pl.ds(pl.multiple_of(first * QB, QB), chunks * QB)
                allowed = self_allowed(starts, query_places(block), first, chunks)
                spans = [slice(pair * LANES, (pair + 1) * LANES) for pair in range(pairs)]
                scores = [
                    jnp.where(
                        allowed, dot_nt(k_ref[keys, lanes], head_stack(q_ref[rows, lanes], 0.125)), -1e30
                    )
                    for lanes in spans
                ]
                mixed, stats = attend(scores, [vt_ref[pair, :, keys] for pair in range(pairs)])
                for lanes, block_out in zip(spans, mixed):
                    o_ref[lanes, rows] = block_out
                l_ref[0, :, rows] = stats

        return carry

    lax.fori_loop(0, q_ref.shape[0] // QB, body, 0)


def self_backward_kernel(
    pairs, most, starts, q_ref, k_ref, v_ref, g_ref, l_ref, dq_ref, dk_ref, dv_ref,
    kt_ref, dka_ref, dva_ref,
):
    for pair in range(pairs):
        lanes = slice(pair * LANES, (pair + 1) * LANES)
        kt_ref[pair] = flip(k_ref[:, lanes])
    dka_ref[...] = jnp.zeros(dka_ref.shape, jnp.float32)
    dva_ref[...] = jnp.zeros(dva_ref.shape, jnp.float32)

    def body(block, carry):
        rows = pl.ds(pl.multiple_of(block * QB, QB), QB)
        first, count = self_window(starts, block)
        for chunks in range(1, most + 1):

            @pl.when(count == chunks)
            def _():
                keys = pl.ds(pl.multiple_of(first * QB, QB), chunks * QB)
                allowed = self_allowed(starts, query_places(block), first, chunks)
                spans = [slice(pair * LANES, (pair + 1) * LANES) for pair in range(pairs)]
                stacked = [head_stack(q_ref[rows, lanes], 0.125) for lanes in spans]
                pulled = [head_stack(g_ref[rows, lanes]) for lanes in spans]
                scores = [
                    jnp.where(allowed, dot_nt(k_ref[keys, lanes], q), -1e30)
                    for lanes, q in zip(spans, stacked)
                ]
                soft, grads, turned = pull_back(
                    scores, [v_ref[keys, lanes] for lanes in spans], pulled, l_ref[0, :, rows],
                    [kt_ref[pair, :, keys] for pair in range(pairs)],
                )
                for pair, lanes in enumerate(spans):
                    dq_ref[lanes, rows] = turned[pair]
                for pair in range(pairs):
                    dva_ref[pair, keys, :] += dot_nn(soft[pair], pulled[pair])
                for pair in range(pairs):
                    dka_ref[pair, keys, :] += dot_nn(grads[pair], stacked[pair])

        return carry

    lax.fori_loop(0, q_ref.shape[0] // QB, body, 0)
    for pair in range(pairs):
        lanes = slice(pair * LANES, (pair + 1) * LANES)
        dk_ref[:, lanes] = dka_ref[pair].astype(jnp.bfloat16)
        dv_ref[:, lanes] = dva_ref[pair].astype(jnp.bfloat16)


def cost(flops, bytes_accessed, exps):
    return pl.CostEstimate(flops=flops, bytes_accessed=bytes_accessed, transcendentals=exps)


def specs(pairs, prefetch):
    wide = pairs * LANES

    def at(index):
        return lambda step, *scalars: index(step)

    return {
        "rows": lambda length: pl.BlockSpec((length, wide), at(lambda i: (0, i))),
        "turned": lambda length: pl.BlockSpec((wide, length), at(lambda i: (i, 0))),
        "images": lambda count, tokens: pl.BlockSpec((count, tokens, wide), at(lambda i: (0, 0, i))),
        "stats": lambda length: pl.BlockSpec((1, 2 * pairs, length), at(lambda i: (i, 0, 0))),
    }


def cross_forward(starts, pages, queries, keys_all, values_all, pairs=4):
    length, width = queries.shape
    count, tokens, _ = keys_all.shape
    steps = width // (pairs * LANES)
    s = specs(pairs, 2)
    return pl.pallas_call(
        functools.partial(cross_forward_kernel, pairs),
        out_shape=(
            jax.ShapeDtypeStruct((width, length), jnp.bfloat16),
            jax.ShapeDtypeStruct((steps, 2 * pairs, length), jnp.float32),
        ),
        grid_spec=pltpu.PrefetchScalarGridSpec(
            num_scalar_prefetch=2,
            grid=(steps,),
            in_specs=[s["rows"](length), s["images"](count, tokens), s["images"](count, tokens)],
            out_specs=[s["turned"](length), s["stats"](length)],
            scratch_shapes=[pltpu.VMEM((pairs, LANES, tokens), jnp.bfloat16)],
        ),
        cost_estimate=cost(11 * 128 * tokens * width * 4 * 4, 20 * 2**20, 2**24),
        name="cross_forward",
    )(starts, pages, queries, keys_all, values_all)


def cross_backward(starts, pages, queries, keys_all, values_all, grads, stats, pairs=4):
    length, width = queries.shape
    count, tokens, _ = keys_all.shape
    steps = width // (pairs * LANES)
    s = specs(pairs, 2)
    image_spec = s["images"](count, tokens)
    return pl.pallas_call(
        functools.partial(cross_backward_kernel, pairs),
        out_shape=(
            jax.ShapeDtypeStruct((width, length), jnp.bfloat16),
            jax.ShapeDtypeStruct(keys_all.shape, jnp.bfloat16),
            jax.ShapeDtypeStruct(values_all.shape, jnp.bfloat16),
        ),
        grid_spec=pltpu.PrefetchScalarGridSpec(
            num_scalar_prefetch=2,
            grid=(steps,),
            in_specs=[s["rows"](length), image_spec, image_spec, s["rows"](length), s["stats"](length)],
            out_specs=[s["turned"](length), image_spec, image_spec],
            scratch_shapes=[
                pltpu.VMEM((pairs, LANES, tokens), jnp.bfloat16),
                pltpu.VMEM((pairs, tokens, LANES), jnp.float32),
                pltpu.VMEM((pairs, tokens, LANES), jnp.float32),
            ],
        ),
        cost_estimate=cost(11 * 128 * tokens * width * 10 * 4, 30 * 2**20, 2**24),
        name="cross_backward",
    )(starts, pages, queries, keys_all, values_all, grads, stats)


def self_forward(starts, queries, keys_all, values_all, most, pairs=4):
    length, width = queries.shape
    steps = width // (pairs * LANES)
    s = specs(pairs, 1)
    rows = s["rows"](length)
    return pl.pallas_call(
        functools.partial(self_forward_kernel, pairs, most),
        out_shape=(
            jax.ShapeDtypeStruct((width, length), jnp.bfloat16),
            jax.ShapeDtypeStruct((steps, 2 * pairs, length), jnp.float32),
        ),
        grid_spec=pltpu.PrefetchScalarGridSpec(
            num_scalar_prefetch=1,
            grid=(steps,),
            in_specs=[rows, rows, rows],
            out_specs=[s["turned"](length), s["stats"](length)],
            scratch_shapes=[pltpu.VMEM((pairs, LANES, length), jnp.bfloat16)],
        ),
        cost_estimate=cost(20 * 128 * 128 * width * 4 * 4, 10 * 2**20, 2**23),
        name="self_forward",
    )(starts, queries, keys_all, values_all)


def self_backward(starts, queries, keys_all, values_all, grads, stats, most, pairs=4):
    length, width = queries.shape
    steps = width // (pairs * LANES)
    s = specs(pairs, 1)
    rows = s["rows"](length)
    return pl.pallas_call(
        functools.partial(self_backward_kernel, pairs, most),
        out_shape=(
            jax.ShapeDtypeStruct((width, length), jnp.bfloat16),
            jax.ShapeDtypeStruct((length, width), jnp.bfloat16),
            jax.ShapeDtypeStruct((length, width), jnp.bfloat16),
        ),
        grid_spec=pltpu.PrefetchScalarGridSpec(
            num_scalar_prefetch=1,
            grid=(steps,),
            in_specs=[rows, rows, rows, rows, s["stats"](length)],
            out_specs=[s["turned"](length), rows, rows],
            scratch_shapes=[
                pltpu.VMEM((pairs, LANES, length), jnp.bfloat16),
                pltpu.VMEM((pairs, length, LANES), jnp.float32),
                pltpu.VMEM((pairs, length, LANES), jnp.float32),
            ],
        ),
        cost_estimate=cost(20 * 128 * 128 * width * 10 * 4, 16 * 2**20, 2**23),
        name="self_backward",
    )(starts, queries, keys_all, values_all, grads, stats)


EPSILON = 1e-05
ROOT_HALF = 0.7071067811865476
ROOT_TAU = 0.3989422804014327
AXES = ("dp", "fsdp")
LONGEST = 512


def contract(a, b, left, right, out=jnp.float32):
    return lax.dot_general(
        a, b, ((left, right), ((), ())), preferred_element_type=jnp.float32
    ).astype(out)


def row_major(values):
    return with_layout_constraint(values, Layout(major_to_minor=(0, 1)))


def normalise(values):
    average = jnp.mean(values, axis=-1, keepdims=True)
    centered = values - average
    variance = jnp.mean(centered * centered, axis=-1, keepdims=True)
    scale = lax.rsqrt(variance + EPSILON)
    return centered * scale, scale


def norm_back(values, gain, grads):
    hat, scale = normalise(values)
    pulled = grads * gain
    first = jnp.mean(pulled, axis=-1, keepdims=True)
    second = jnp.mean(pulled * hat, axis=-1, keepdims=True)
    back = scale * (pulled - first - hat * second)
    return back, jnp.sum(grads * hat, axis=0), jnp.sum(grads, axis=0)


def swap(value, axis, size, bit):
    return lax.ppermute(value, axis, [(i, i ^ bit) for i in range(size)])


def butterfly_sum(value, sizes):
    for axis, size in sizes:
        bit = 1
        while bit < size:
            value = value + swap(value, axis, size, bit)
            bit *= 2
    return value


def pick(value, index, axis):
    return lax.dynamic_index_in_dim(value, index, axis, keepdims=False)


def fence(*values):
    return lax.optimization_barrier(values)


class Partial:
    def __init__(self, value, sizes, blocks=1):
        dp_size, inner = sizes
        keys, places = ["block"], {}
        for axis, size in (("dp", dp_size), ("fsdp", inner)):
            bit = size // 2
            while bit:
                keys.append((axis, bit))
                places[(axis, bit)] = (lax.axis_index(axis) // bit) % 2
                bit //= 2
        own = value.shape[0] // (blocks * dp_size * inner)
        self.sizes = {"dp": dp_size, "fsdp": inner}
        self.keys, self.places = keys, places
        bits = (2,) * (len(keys) - 1)
        self.terms = [value.reshape((blocks,) + bits + (own, value.shape[1]))]

    def total(self, terms):
        wide = [term.astype(jnp.float32) for term in terms]
        return functools.reduce(jnp.add, wide)

    def send(self, key):
        return self.fly(self.cut(key), key)

    def fly(self, load, key):
        return swap(load, key[0], self.sizes[key[0]], key[1])

    def cut(self, key):
        axis = self.keys.index(key)
        self.keys.remove(key)
        out = self.total([pick(term, 1 - self.places[key], axis) for term in self.terms])
        self.terms = [pick(term, self.places[key], axis) for term in self.terms]
        return out.astype(jnp.bfloat16)

    def take(self, received):
        self.terms.append(received)

    def rest(self):
        return self.total(self.terms).astype(jnp.bfloat16)


CORE = ("dp", 1)
ACROSS = ("dp", 2)


def scatter(parts, sizes):
    inner = sizes[1]
    rests = []
    for part in parts:
        rest = part.rest()
        blocks, (own, columns) = rest.shape[0], rest.shape[-2:]
        rest = rest.reshape(blocks, inner, own, columns).transpose(1, 0, 2, 3)
        rests.append(rest.reshape(inner, blocks * own, columns))
    packed = rests[0] if len(rests) == 1 else jnp.concatenate(rests, axis=1)
    summed = lax.psum_scatter(
        packed.reshape(-1, columns), "fsdp", scatter_dimension=0, tiled=True
    ).astype(jnp.float32)
    own = summed.shape[0] // len(parts)
    return [summed[i * own : (i + 1) * own] for i in range(len(parts))]


def side_by_side_kernel(own, blocks, rows_ref, out_ref):
    width = rows_ref.shape[1]
    for device in range(out_ref.shape[0] // own):
        for block in range(blocks):
            first = (device * blocks + block) * own
            out_ref[device * own : (device + 1) * own, block * width : (block + 1) * width] = (
                rows_ref[first : first + own, :]
            )


def side_by_side(far, own, blocks, devices=4):
    _, rows, width = far.shape
    step = devices * own
    return pl.pallas_call(
        functools.partial(side_by_side_kernel, own, blocks),
        out_shape=jax.ShapeDtypeStruct((rows // blocks, blocks * width), far.dtype),
        grid=(rows // (blocks * step),),
        in_specs=[pl.BlockSpec((None, blocks * step, width), lambda i: (1, i, 0))],
        out_specs=pl.BlockSpec((step, blocks * width), lambda i: (i, 0)),
        cost_estimate=cost(0, 4 * rows * width, 0),
        name="side_by_side",
    )(far)


def lower_stack_kernel(*refs):
    for i, master in enumerate(refs[:-1]):
        refs[-1][i] = master[...].astype(refs[-1].dtype)


def lower_stack(masters):
    rows, width = masters[0].shape
    count = len(masters)
    return pl.pallas_call(
        lower_stack_kernel,
        out_shape=jax.ShapeDtypeStruct((count, rows, width), jnp.bfloat16),
        cost_estimate=cost(0, 6 * count * rows * width, 0),
        name="lower_stack",
    )(*masters)


def layer(
    sizes, block_in, images, segment_ids, page_map, ln1_gain, ln1_shift, ln2_gain, ln2_shift,
    ln3_gain, ln3_shift, self_query, self_key, self_value, self_out, cross_query, cross_key,
    cross_value, cross_out, mlp_in, mlp_out, cotangent,
):
    dp_size, inner = sizes
    axes = (("dp", dp_size), ("fsdp", inner))
    _, length, width = block_in.shape
    low = jnp.bfloat16

    def turned(master):
        return master.astype(low).T

    def gather(*masters):
        return lax.all_gather(lower_stack([m.T for m in masters]), AXES, axis=1, tiled=True)

    norms = jnp.stack([ln1_gain, ln1_shift, ln2_gain, ln2_shift, ln3_gain, ln3_shift])
    norms = norms.astype(low).astype(jnp.float32)
    mine = norms.shape[1]
    offset = (lax.axis_index("dp") * inner + lax.axis_index("fsdp")) * mine
    spread = lax.dynamic_update_slice(jnp.zeros((6, width), jnp.float32), norms, (0, offset))
    norms = butterfly_sum(spread, axes)
    near = gather(
        self_query, self_key, self_value, self_out, cross_query, cross_key, cross_value, cross_out
    )
    w_sqkv, w_kv = near[:3], near[5:7]
    w_so, w_cq, w_ck, w_cv, w_co = [near[i] for i in range(3, 8)]
    own = mlp_out.shape[1]
    blocks = mlp_out.shape[0] // width
    out_rows = turned(mlp_out).reshape(own, blocks, width).transpose(1, 0, 2)
    far = jnp.stack([turned(mlp_in), out_rows.reshape(blocks * own, width)])
    far = lax.all_gather(far, AXES, axis=1, tiled=True)
    w_in = far[0]
    w_out = side_by_side(far, own, blocks)

    starts = jnp.sum(
        segment_ids[0][None, :] < jnp.arange(page_map.shape[1] + 1, dtype=jnp.int32)[:, None],
        axis=1,
    ).astype(jnp.int32)
    pages = page_map[0]
    most = LONGEST // QB + 1

    rows = block_in[0].astype(jnp.float32)
    a1 = (normalise(rows)[0] * norms[0] + norms[1]).astype(low)
    sq, sk, sv = [contract(a1, w_sqkv[i], (1,), (1,), low) for i in range(3)]
    so, s_stats = self_forward(starts, sq, sk, sv, most)
    x1 = row_major(rows + contract(so, w_so, (0,), (1,)))
    a2 = (normalise(x1)[0] * norms[2] + norms[3]).astype(low)
    cq = contract(a2, w_cq, (1,), (1,), low)
    ck = contract(images, w_ck, (2,), (1,), low)
    cv = contract(images, w_cv, (2,), (1,), low)
    co, c_stats = cross_forward(starts, pages, cq, ck, cv)
    x2 = row_major(x1 + contract(co, w_co, (0,), (1,)))
    a3 = (normalise(x2)[0] * norms[4] + norms[5]).astype(low)
    u = contract(a3, w_in, (1,), (1,))
    phi = 0.5 * (1.0 + lax.erf(u * ROOT_HALF))
    hidden = (u * phi).astype(low)
    slope = (phi + u * (ROOT_TAU * jnp.exp(-0.5 * u * u))).astype(low)

    eb = cotangent[0]
    e = eb.astype(jnp.float32)
    g_out = contract(eb, hidden, (0,), (0,), low)
    p_out = Partial(g_out, sizes)
    flying = p_out.send(CORE)
    eb, hidden, g_out = fence(eb, hidden, g_out)
    du = (contract(eb, w_out, (1,), (0,)) * slope.astype(jnp.float32)).astype(low)
    du, flying = fence(du, flying)
    p_out.take(flying)
    flying = p_out.send(ACROSS)
    g_in = contract(du, a3, (0,), (0,), low)
    du, g_in = fence(du, g_in)
    p_in = Partial(g_in, sizes)
    flying_in = p_in.send(CORE)
    d3 = contract(du, w_in, (1,), (0,))
    back, gg3, gs3 = norm_back(x2, norms[4], d3)
    e2 = e + back
    e2b = e2.astype(low)
    e2, e2b, flying_in = fence(e2, e2b, flying_in)
    p_in.take(flying_in)
    flying_in = p_in.send(ACROSS)
    d_co = contract(e2b, w_co, (1,), (0,), low)
    dcq, dck, dcv = cross_backward(starts, pages, cq, ck, cv, d_co, c_stats)
    dcq, dck, dcv, flying, flying_in = fence(dcq, dck, dcv, flying, flying_in)
    p_out.take(flying)
    (g_mlp_out,) = scatter([p_out], sizes)
    p_in.take(flying_in)
    (g_mlp_in,) = scatter([p_in], sizes)
    g_co = contract(e2b, co, (0,), (1,), low)
    g_cq = contract(dcq, a2, (1,), (0,), low)
    g_ck = contract(dck, images, (0, 1), (0, 1), low)
    g_cv = contract(dcv, images, (0, 1), (0, 1), low)
    dcq, g_cq, g_ck, g_cv, g_co = fence(dcq, g_cq, g_ck, g_cv, g_co)
    p_cross = [Partial(g, sizes) for g in (g_cq, g_ck, g_cv, g_co)]
    flying = [p.send(CORE) for p in p_cross]
    d2 = contract(dcq, w_cq, (0,), (0,))
    back, gg2, gs2 = norm_back(x1, norms[2], d2)
    e1 = e2 + back
    e1b = e1.astype(low)
    e1, e1b, *flying = fence(e1, e1b, *flying)
    for p, f in zip(p_cross, flying):
        p.take(f)
    flying = [p.send(ACROSS) for p in p_cross]
    g_so = contract(e1b, so, (0,), (1,), low)
    d_so = contract(e1b, w_so, (1,), (0,), low)
    dsq, dsk, dsv = self_backward(starts, sq, sk, sv, d_so, s_stats, most)
    dsq, dsk, dsv, g_so, *flying = fence(dsq, dsk, dsv, g_so, *flying)
    for p, f in zip(p_cross, flying):
        p.take(f)
    g_cross = scatter(p_cross, sizes)
    g_sq = contract(dsq, a1, (1,), (0,), low)
    g_sk = contract(dsk, a1, (0,), (0,), low)
    g_sv = contract(dsv, a1, (0,), (0,), low)
    pairs = (jnp.concatenate([g_sq, g_sk]), jnp.concatenate([g_sv, g_so]))
    dsq, dsk, dsv, *pairs = fence(dsq, dsk, dsv, *pairs)
    groups = [Partial(pair, sizes, 2) for pair in pairs]
    keys = [("fsdp", 1 << i) for i in range(inner.bit_length() - 1)]
    orders = [[ACROSS] + keys, keys[:-1] + [ACROSS] + keys[-1:]]
    flights = [g.send(CORE) for g in groups]
    d1 = (
        contract(dsq, w_sqkv[0], (0,), (0,))
        + contract(dsk, w_sqkv[1], (1,), (0,))
        + contract(dsv, w_sqkv[2], (1,), (0,))
    )

    def norm_one(d1):
        back, gg1, gs1 = norm_back(rows, norms[0], d1)
        return e1 + back, gg1, gs1

    def image_grads(dck, dcv):
        both = jnp.concatenate([dck, dcv], axis=2).transpose(1, 0, 2)
        tokens, count, _ = both.shape
        flat = contract(
            both.reshape(tokens * count, 2 * width), w_kv.reshape(2 * width, width), (1,), (0,)
        )
        return flat.reshape(tokens, count, width)

    def finish(hidden):
        return (x2 + contract(hidden, w_out, (1,), (1,))).astype(low)

    grad_in, gg1, gs1 = norm_one(d1)
    norm_grads = jnp.stack([gg1, gs1, gg2, gs2, gg3, gs3])
    grad_in, norm_grads, hidden, dck, dcv, *flights = fence(
        grad_in, norm_grads, hidden, dck, dcv, *flights
    )
    for stage in range(len(keys) + 1):
        for g, f in zip(groups, flights):
            g.take(f)
        loads = [g.cut(o[stage]) for g, o in zip(groups, orders)]
        if stage == 0:
            dck, dcv, *loads = fence(dck, dcv, *loads)
        if stage == 1:
            hidden, *loads = fence(hidden, *loads)
        flights = [g.fly(load, o[stage]) for g, load, o in zip(groups, loads, orders)]
        if stage == 0:
            grad_images = image_grads(dck, dcv).transpose(1, 0, 2)
            other = swap(norm_grads, "dp", dp_size, 1)
            grad_images, other, *flights = fence(grad_images, other, *flights)
            norm_grads = norm_grads + other
        if stage == 1:
            other = swap(norm_grads, "dp", dp_size, 2)
            block_out, other, *flights = fence(finish(hidden), other, *flights)
            norm_grads = norm_grads + other
    for g, f in zip(groups, flights):
        g.take(f)
    g_self = [g.total(g.terms)[i] for g in groups for i in range(2)]
    norm_grads = butterfly_sum(norm_grads, axes[1:])
    norm_grads = lax.dynamic_slice(norm_grads, (0, offset), (6, mine))
    weight_grads = [g.T for g in g_self + g_cross + [g_mlp_in, g_mlp_out]]
    return (
        block_out[None], grad_in[None], grad_images, *[norm_grads[i] for i in range(6)],
        *weight_grads,
    )


def solution(mesh):
    sizes = (mesh.shape["dp"], mesh.shape["fsdp"])
    rows3 = P(AXES, None, None)
    rows2 = P(AXES, None)
    vector = P(AXES)
    columns = P(None, AXES)
    return jax.shard_map(
        functools.partial(layer, sizes),
        mesh=mesh,
        in_specs=(rows3, rows3, rows2, rows2) + (vector,) * 6 + (columns,) * 10 + (rows3,),
        out_specs=(rows3,) * 3 + (vector,) * 6 + (columns,) * 10,
        check_vma=False,
    )
```
